256 devices in a mesh: member: 64 (over z, y, x_lo), dp: 4 (over x_hi, core).
Axes of the slice: x: 4 (x_hi: 2, x_lo: 2; x = x_hi * 2 + x_lo), y: 4, z: 8, core: 2. Of those that a mesh axis runs over, the one named last changes fastest.
Arguments:
- tokens: bfloat16 [64, 16, 196, 768], P('member', 'dp'), may hold values from -6 to 6
- labels: int32 [64, 16], P('member', 'dp'), may hold values from 0 to 499
- source: int32 [64], replicated, may hold values from 0 to 63, as said below
- learn_rate: float32 [64], P('member'), may hold values from 0.02 to 0.2
- weight_decay: float32 [64], P('member'), may hold values from 0.1 to 1
- classifier: bfloat16 [768, 500], replicated, may hold values from -8 to 8
- up_param: float32 [64, 768, 1536], P('member', 'dp'), may hold values from -6 to 6
- up_first: bfloat16 [64, 768, 1536], P('member', 'dp'), may hold values from -0.005859375 to 0.005859375
- up_second: float32 [64, 768, 1536], P('member', 'dp'), may hold values from 1e-07 to 1e-05
- down_param: float32 [64, 1536, 768], P('member', 'dp'), may hold values from -6 to 6
- down_first: bfloat16 [64, 1536, 768], P('member', 'dp'), may hold values from -0.005859375 to 0.005859375
- down_second: float32 [64, 1536, 768], P('member', 'dp'), may hold values from 1e-07 to 1e-05
Outputs:
- up_weight: float32 [64, 768, 1536], P('member', 'dp')
- up_moment: bfloat16 [64, 768, 1536], P('member', 'dp')
- up_variance: float32 [64, 768, 1536], P('member', 'dp')
- down_weight: float32 [64, 1536, 768], P('member', 'dp')
- down_moment: bfloat16 [64, 1536, 768], P('member', 'dp')
- down_variance: float32 [64, 1536, 768], P('member', 'dp')
The draws below stay inside these ranges and needn't reach their ends.
Inputs may be any that keep to these rules, and one draw needn't show every extreme that they name: source[i] = i except for the 16 members of the lowest quartile of a ranking; each of those names a member of the highest quartile, which keeps its own index; a winner may be named by several losers.
All inputs are finite; a program needn't handle non-finite values.
Results may differ from the reference program's by a relative error of at most 0.009.
Values may be sent and summed in bfloat16 or wider, within the bound.
A program may use at most 128 MiB of HBM per device.

```python
import math
import jax
import jax.numpy as jnp
from jax import lax

D = 768
FF = 1536
CLASSES = 500
PATCHES = 196
IMG_DEV = 4
STEP = 1000
MEMBERS = 64
BATCH = 16
N_DP = 4


def draw_source(key, part):
    ranking = jax.random.permutation(jax.random.fold_in(key, 11), MEMBERS).astype(jnp.int32)
    quarter = MEMBERS // 4
    winners = ranking[:quarter]
    losers = ranking[MEMBERS - quarter:]
    picks = jax.random.randint(jax.random.fold_in(key, 12), (quarter,), 0, quarter)
    mapping = jnp.arange(MEMBERS, dtype=jnp.int32)
    return mapping.at[losers].set(winners[picks]).astype(jnp.int32)


def set_ends(result, rng, smallest, top_value):
    longest = result.shape.index(max(result.shape))
    spots = []
    for shift in (0, 1):
        where = [jax.random.randint(jax.random.fold_in(rng, axis), (), 0, length) for axis, length in enumerate(result.shape)]
        where[longest] = (where[longest] + shift) % result.shape[longest]
        spots.append(tuple(where))
    return result.at[spots[0]].set(smallest).at[spots[1]].set(top_value)


def block_levels(stream_key, dims, shards, least, high):
    loudness, own = 1.0, jax.random.fold_in(stream_key, 6)
    for position, parts in shards:
        heights = jnp.exp(jax.random.uniform(jax.random.fold_in(own, position), (parts,), jnp.float32, least / len(shards), high / len(shards)))
        loudness = loudness * jnp.repeat(heights, dims[position] // parts).reshape([-1 if axis == position else 1 for axis in range(len(dims))])
    return loudness


def noise(rng, shape, deviation, bound, pieces=(), held_as=jnp.bfloat16):
    result = deviation * jax.random.normal(rng, shape, jnp.float32)
    if pieces:
        result = result * block_levels(rng, shape, pieces, -0.22, 0.18)
    return jnp.clip(result, -bound, bound).astype(held_as)


def setup_inputs(seed: int = 0) -> dict:
    arg_keys = jax.random.split(jax.random.key(seed), 13)
    tokens = noise(arg_keys[0], (MEMBERS, BATCH, PATCHES, D), 1.0, 6.0, ((0, 64), (1, 4)))
    labels = set_ends(jax.random.randint(arg_keys[1], (MEMBERS, BATCH), 0, CLASSES), jax.random.fold_in(arg_keys[1], 1), 0, CLASSES - 1).astype(jnp.int32)
    source = draw_source(jax.random.fold_in(arg_keys[12], 71), 0)
    learn_rate = jnp.clip(jnp.exp(math.log(0.2) - 2.3025851 * jax.random.uniform(arg_keys[3], (MEMBERS,), jnp.float32) ** block_levels(arg_keys[3], (MEMBERS,), ((0, 64),), -0.2, 0.2)), 0.02, 0.2)
    weight_decay = jnp.clip(jnp.exp(math.log(1.0) - 2.3025851 * jax.random.uniform(arg_keys[4], (MEMBERS,), jnp.float32) ** block_levels(arg_keys[4], (MEMBERS,), ((0, 64),), -0.2, 0.2)), 0.1, 1.0)
    classifier = noise(arg_keys[5], (D, CLASSES), 1.5, 8.0)
    up_param = noise(arg_keys[6], (MEMBERS, D, FF), 1.0, 6.0, ((0, 64), (1, 4)), jnp.float32)
    up_first = noise(arg_keys[7], (MEMBERS, D, FF), 0.001, 0.005859375, ((0, 64), (1, 4)))
    up_second = jnp.clip(jnp.exp(math.log(9.999999747378752e-06) - 4.6051701 * jax.random.uniform(arg_keys[8], (MEMBERS, D, FF), jnp.float32) ** block_levels(arg_keys[8], (MEMBERS, D, FF), ((0, 64), (1, 4)), -0.2, 0.2)), 1.0000000116860974e-07, 9.999999747378752e-06)
    down_param = noise(arg_keys[9], (MEMBERS, FF, D), 1.0, 6.0, ((0, 64), (1, 4)), jnp.float32)
    down_first = noise(arg_keys[10], (MEMBERS, FF, D), 0.001, 0.005859375, ((0, 64), (1, 4)))
    down_second = jnp.clip(jnp.exp(math.log(9.999999747378752e-06) - 4.6051701 * jax.random.uniform(arg_keys[11], (MEMBERS, FF, D), jnp.float32) ** block_levels(arg_keys[11], (MEMBERS, FF, D), ((0, 64), (1, 4)), -0.2, 0.2)), 1.0000000116860974e-07, 9.999999747378752e-06)
    return dict(tokens=tokens, labels=labels, source=source, learn_rate=learn_rate, weight_decay=weight_decay, classifier=classifier, up_param=up_param, up_first=up_first, up_second=up_second, down_param=down_param, down_first=down_first, down_second=down_second)


def local_gradients(tokens, labels, up_weight, down_weight, classifier, batch_total):
    images, patches, features = tokens.shape
    hidden_units = up_weight.shape[1]
    token_rows = tokens.reshape(images * patches, features).astype(jnp.float32)
    center = token_rows - lax.optimization_barrier(jnp.mean(token_rows, axis=1, keepdims=True))
    normed = (center * lax.rsqrt(lax.optimization_barrier(jnp.mean(center * center, axis=1, keepdims=True)) + 1e-06)).astype(jnp.bfloat16)
    preact = jnp.dot(normed, up_weight, preferred_element_type=jnp.float32) * features ** (-0.5)
    activated = (0.5 * preact * (1.0 + lax.erf(preact * 0.7071067811865476))).astype(jnp.bfloat16)
    residual = token_rows + jnp.dot(activated, down_weight, preferred_element_type=jnp.float32) * hidden_units ** (-0.5)
    out_center = residual - lax.optimization_barrier(jnp.mean(residual, axis=1, keepdims=True))
    inverse = lax.rsqrt(lax.optimization_barrier(jnp.mean(out_center * out_center, axis=1, keepdims=True)) + 1e-06)
    out_normed = out_center * inverse
    pooled = lax.optimization_barrier(jnp.mean(out_normed.reshape(images, patches, features), axis=1)).astype(jnp.bfloat16)
    logits = jnp.dot(pooled, classifier, preferred_element_type=jnp.float32)
    powered = jnp.exp(logits)
    softmax_out = powered / lax.optimization_barrier(jnp.sum(powered, axis=1, keepdims=True))
    onehot = (labels[:, None] == jnp.arange(classifier.shape[1], dtype=jnp.int32)[None, :]).astype(jnp.float32)
    logit_delta = ((softmax_out - onehot) / batch_total).astype(jnp.bfloat16)
    pool_delta = lax.dot_general(logit_delta, classifier, (((1,), (1,)), ((), ())), preferred_element_type=jnp.float32) / patches
    token_delta = jnp.broadcast_to(pool_delta[:, None, :], (images, patches, features)).reshape(images * patches, features)
    residual_delta = inverse * (token_delta - lax.optimization_barrier(jnp.mean(token_delta, axis=1, keepdims=True)) - out_normed * lax.optimization_barrier(jnp.mean(token_delta * out_normed, axis=1, keepdims=True)))
    residual_delta = residual_delta.astype(jnp.bfloat16)
    down_scale = hidden_units ** (-0.5)
    down_gradient = lax.dot_general(activated, residual_delta, (((0,), (0,)), ((), ())), preferred_element_type=jnp.float32) * down_scale
    hidden_delta = lax.dot_general(residual_delta, down_weight, (((1,), (1,)), ((), ())), preferred_element_type=jnp.float32) * down_scale
    derivative = 0.5 * (1.0 + lax.erf(preact * 0.7071067811865476)) + preact * jnp.exp(-0.5 * preact * preact) * 0.3989422804014327
    preact_delta = (hidden_delta * derivative).astype(jnp.bfloat16)
    up_gradient = lax.dot_general(normed, preact_delta, (((0,), (0,)), ((), ())), preferred_element_type=jnp.float32) * features ** (-0.5)
    return (up_gradient, down_gradient)

def adamw_step(param, first, second, gradient, rate_value, decay_value):
    moment = 0.9 * first.astype(jnp.float32) + 0.1 * gradient
    variance = 0.999 * second + 0.001 * gradient * gradient
    update = moment / (1.0 - 0.9 ** STEP) / (jnp.sqrt(variance / (1.0 - 0.999 ** STEP)) + 1e-08) + decay_value * param
    return (param - rate_value * update, moment.astype(jnp.bfloat16), variance)

def reference(tokens, labels, source, learn_rate, weight_decay, classifier, up_param, up_first, up_second, down_param, down_first, down_second):

    def member_update(index):
        winner = source[index]

        def chosen(array):
            return lax.dynamic_index_in_dim(array, winner, 0, keepdims=False)
        up_now, up_mom, up_var = (chosen(up_param), chosen(up_first), chosen(up_second))
        down_now, down_mom, down_var = (chosen(down_param), chosen(down_first), chosen(down_second))
        up_bf = up_now.astype(jnp.bfloat16)
        down_bf = down_now.astype(jnp.bfloat16)
        member_tokens = lax.dynamic_index_in_dim(tokens, index, 0, keepdims=False)
        member_labels = lax.dynamic_index_in_dim(labels, index, 0, keepdims=False)
        up_total = jnp.zeros((D, FF), jnp.float32)
        down_total = jnp.zeros((FF, D), jnp.float32)
        for group in range(N_DP):
            first_grad, second_grad = local_gradients(member_tokens[group * IMG_DEV:(group + 1) * IMG_DEV], member_labels[group * IMG_DEV:(group + 1) * IMG_DEV], up_bf, down_bf, classifier, BATCH)
            up_total = up_total + lax.optimization_barrier(first_grad.astype(jnp.bfloat16)).astype(jnp.float32)
            down_total = down_total + lax.optimization_barrier(second_grad.astype(jnp.bfloat16)).astype(jnp.float32)
        rate_value = learn_rate[index]
        decay_value = weight_decay[index]
        up_new = adamw_step(up_now, up_mom, up_var, up_total, rate_value, decay_value)
        down_new = adamw_step(down_now, down_mom, down_var, down_total, rate_value, decay_value)
        return up_new + down_new
    results = lax.map(member_update, jnp.arange(MEMBERS, dtype=jnp.int32))
    return (results[0], results[1], results[2], results[3], results[4], results[5])
```

```python
import jax
import jax.numpy as jnp
from jax import lax
from jax.sharding import PartitionSpec as P

STEP = 1000


def local_gradients(tokens, labels, up_weight, down_weight, classifier, batch_total):
    images, patches, features = tokens.shape
    hidden_units = up_weight.shape[1]
    token_rows = tokens.reshape(images * patches, features).astype(jnp.float32)
    center = token_rows - jnp.mean(token_rows, axis=1, keepdims=True)
    normed = (center * lax.rsqrt(jnp.mean(center * center, axis=1, keepdims=True) + 1e-06)).astype(
        jnp.bfloat16
    )
    preact = jnp.dot(normed, up_weight, preferred_element_type=jnp.float32) * features ** (-0.5)
    activated = (0.5 * preact * (1.0 + lax.erf(preact * 0.7071067811865476))).astype(jnp.bfloat16)
    residual = token_rows + jnp.dot(
        activated, down_weight, preferred_element_type=jnp.float32
    ) * hidden_units ** (-0.5)
    out_center = residual - jnp.mean(residual, axis=1, keepdims=True)
    inverse = lax.rsqrt(jnp.mean(out_center * out_center, axis=1, keepdims=True) + 1e-06)
    out_normed = out_center * inverse
    pooled = jnp.mean(out_normed.reshape(images, patches, features), axis=1).astype(jnp.bfloat16)
    logits = jnp.dot(pooled, classifier, preferred_element_type=jnp.float32)
    powered = jnp.exp(logits)
    softmax_out = powered / jnp.sum(powered, axis=1, keepdims=True)
    onehot = (labels[:, None] == jnp.arange(classifier.shape[1], dtype=jnp.int32)[None, :]).astype(
        jnp.float32
    )
    logit_delta = ((softmax_out - onehot) / batch_total).astype(jnp.bfloat16)
    pool_delta = (
        lax.dot_general(
            logit_delta, classifier, (((1,), (1,)), ((), ())), preferred_element_type=jnp.float32
        )
        / patches
    )
    token_delta = jnp.broadcast_to(pool_delta[:, None, :], (images, patches, features)).reshape(
        images * patches, features
    )
    residual_delta = inverse * (
        token_delta
        - jnp.mean(token_delta, axis=1, keepdims=True)
        - out_normed * jnp.mean(token_delta * out_normed, axis=1, keepdims=True)
    )
    residual_delta = residual_delta.astype(jnp.bfloat16)
    down_scale = hidden_units ** (-0.5)
    down_gradient = (
        lax.dot_general(
            activated, residual_delta, (((0,), (0,)), ((), ())), preferred_element_type=jnp.float32
        )
        * down_scale
    )
    hidden_delta = (
        lax.dot_general(
            residual_delta,
            down_weight,
            (((1,), (1,)), ((), ())),
            preferred_element_type=jnp.float32,
        )
        * down_scale
    )
    derivative = (
        0.5 * (1.0 + lax.erf(preact * 0.7071067811865476))
        + preact * jnp.exp(-0.5 * preact * preact) * 0.3989422804014327
    )
    preact_delta = (hidden_delta * derivative).astype(jnp.bfloat16)
    up_gradient = lax.dot_general(
        normed, preact_delta, (((0,), (0,)), ((), ())), preferred_element_type=jnp.float32
    ) * features ** (-0.5)
    return (up_gradient, down_gradient)


def adamw_step(param, first, second, gradient, rate_value, decay_value):
    moment = 0.9 * first.astype(jnp.float32) + 0.1 * gradient
    variance = 0.999 * second + 0.001 * gradient * gradient
    update = (
        moment / (1.0 - 0.9**STEP) / (jnp.sqrt(variance / (1.0 - 0.999**STEP)) + 1e-08)
        + decay_value * param
    )
    return (param - rate_value * update, moment.astype(jnp.bfloat16), variance)


def exploit(parts, source, members):
    sizes = [part.size for part in parts]
    packed = jnp.concatenate(
        [part.astype(jnp.bfloat16).reshape(members, -1) for part in parts], axis=1
    )
    chunks = lax.all_to_all(packed, "member", split_axis=0, concat_axis=0, tiled=True)
    picked = jnp.take(chunks, source, axis=0)
    back = lax.all_to_all(picked, "member", split_axis=0, concat_axis=0, tiled=True)
    out = []
    start = 0
    for part, size in zip(parts, sizes):
        width = size // members
        out.append(back[:, start:start + width].reshape(part.shape))
        start += width
    return out


def per_device(
    tokens,
    labels,
    source,
    learn_rate,
    weight_decay,
    classifier,
    up_param,
    up_first,
    up_second,
    down_param,
    down_first,
    down_second,
):
    members = lax.axis_size("member")
    shards = lax.axis_size("dp")
    me = lax.axis_index("member")
    own = source[me] == me

    up_bf, down_bf = exploit((up_param[0], down_param[0]), source, members)
    up_mom, down_mom, up_var_bf, down_var_bf = exploit(
        (up_first[0], down_first[0], up_second[0], down_second[0]), source, members
    )

    up_full = lax.all_gather(up_bf, "dp", axis=0, tiled=True)
    down_full = lax.all_gather(down_bf, "dp", axis=0, tiled=True)
    batch_total = tokens.shape[1] * shards
    up_gradient, down_gradient = local_gradients(
        tokens[0], labels[0], up_full, down_full, classifier, batch_total
    )
    up_share = lax.psum_scatter(
        up_gradient.astype(jnp.bfloat16), "dp", scatter_dimension=0, tiled=True
    ).astype(jnp.float32)
    down_share = lax.psum_scatter(
        down_gradient.astype(jnp.bfloat16), "dp", scatter_dimension=0, tiled=True
    ).astype(jnp.float32)

    up_now = jnp.where(own, up_param[0], up_bf.astype(jnp.float32))
    down_now = jnp.where(own, down_param[0], down_bf.astype(jnp.float32))
    up_var = jnp.where(own, up_second[0], up_var_bf.astype(jnp.float32))
    down_var = jnp.where(own, down_second[0], down_var_bf.astype(jnp.float32))

    rate_value = learn_rate[0]
    decay_value = weight_decay[0]
    up_new = adamw_step(up_now, up_mom, up_var, up_share, rate_value, decay_value)
    down_new = adamw_step(down_now, down_mom, down_var, down_share, rate_value, decay_value)
    return tuple(value[None] for value in up_new + down_new)


def solution(mesh):
    placed = (
        P("member", "dp", None, None),
        P("member", "dp"),
        P(),
        P("member"),
        P("member"),
        P(),
        P("member", "dp", None),
        P("member", "dp", None),
        P("member", "dp", None),
        P("member", "dp", None),
        P("member", "dp", None),
        P("member", "dp", None),
    )
    return jax.shard_map(
        per_device,
        mesh=mesh,
        in_specs=placed,
        out_specs=(P("member", "dp", None),) * 6,
        check_vma=False,
    )
```

```python
import functools

import jax
import jax.numpy as jnp
from jax import lax
from jax.experimental import pallas as pl
from jax.experimental.pallas import tpu as pltpu
from jax.sharding import PartitionSpec as P

MESH_ID = pl.DeviceIdType.MESH

STEP = 1000


def local_gradients(tokens, labels, up_weight, down_weight, classifier, batch_total):
    images, patches, features = tokens.shape
    hidden_units = up_weight.shape[1]
    token_rows = tokens.reshape(images * patches, features).astype(jnp.float32)
    center = token_rows - jnp.mean(token_rows, axis=1, keepdims=True)
    normed = (center * lax.rsqrt(jnp.mean(center * center, axis=1, keepdims=True) + 1e-06)).astype(
        jnp.bfloat16
    )
    preact = jnp.dot(normed, up_weight, preferred_element_type=jnp.float32) * features ** (-0.5)
    activated = (0.5 * preact * (1.0 + lax.erf(preact * 0.7071067811865476))).astype(jnp.bfloat16)
    residual = token_rows + jnp.dot(
        activated, down_weight, preferred_element_type=jnp.float32
    ) * hidden_units ** (-0.5)
    out_center = residual - jnp.mean(residual, axis=1, keepdims=True)
    inverse = lax.rsqrt(jnp.mean(out_center * out_center, axis=1, keepdims=True) + 1e-06)
    out_normed = out_center * inverse
    pooled = jnp.mean(out_normed.reshape(images, patches, features), axis=1).astype(jnp.bfloat16)
    logits = jnp.dot(pooled, classifier, preferred_element_type=jnp.float32)
    powered = jnp.exp(logits)
    softmax_out = powered / jnp.sum(powered, axis=1, keepdims=True)
    onehot = (labels[:, None] == jnp.arange(classifier.shape[1], dtype=jnp.int32)[None, :]).astype(
        jnp.float32
    )
    logit_delta = ((softmax_out - onehot) / batch_total).astype(jnp.bfloat16)
    pool_delta = (
        lax.dot_general(
            logit_delta, classifier, (((1,), (1,)), ((), ())), preferred_element_type=jnp.float32
        )
        / patches
    )
    token_delta = jnp.broadcast_to(pool_delta[:, None, :], (images, patches, features)).reshape(
        images * patches, features
    )
    residual_delta = inverse * (
        token_delta
        - jnp.mean(token_delta, axis=1, keepdims=True)
        - out_normed * jnp.mean(token_delta * out_normed, axis=1, keepdims=True)
    )
    residual_delta = residual_delta.astype(jnp.bfloat16)
    down_scale = hidden_units ** (-0.5)
    down_gradient = (
        lax.dot_general(
            activated, residual_delta, (((0,), (0,)), ((), ())), preferred_element_type=jnp.float32
        )
        * down_scale
    )
    hidden_delta = (
        lax.dot_general(
            residual_delta,
            down_weight,
            (((1,), (1,)), ((), ())),
            preferred_element_type=jnp.float32,
        )
        * down_scale
    )
    derivative = (
        0.5 * (1.0 + lax.erf(preact * 0.7071067811865476))
        + preact * jnp.exp(-0.5 * preact * preact) * 0.3989422804014327
    )
    preact_delta = (hidden_delta * derivative).astype(jnp.bfloat16)
    up_gradient = lax.dot_general(
        normed, preact_delta, (((0,), (0,)), ((), ())), preferred_element_type=jnp.float32
    ) * features ** (-0.5)
    return (up_gradient, down_gradient)


def adamw_step(param, first, second, gradient, rate_value, decay_value):
    moment = 0.9 * first.astype(jnp.float32) + 0.1 * gradient
    variance = 0.999 * second + 0.001 * gradient * gradient
    update = (
        moment / (1.0 - 0.9**STEP) / (jnp.sqrt(variance / (1.0 - 0.999**STEP)) + 1e-08)
        + decay_value * param
    )
    return (param - rate_value * update, moment.astype(jnp.bfloat16), variance)


def enter(n, me):
    barrier = pltpu.get_barrier_semaphore()

    def greet(k, carry):
        pl.semaphore_signal(
            barrier, inc=1, device_id={"member": lax.rem(me + k, n)}, device_id_type=MESH_ID
        )
        return carry

    lax.fori_loop(1, n, greet, 0)
    pl.semaphore_wait(barrier, n - 1)


def transpose(n, me, src, dst, send_sem, recv_sem):
    def copy(k):
        target = lax.rem(me + k, n)
        return pltpu.make_async_remote_copy(
            src_ref=src.at[target],
            dst_ref=dst.at[me],
            send_sem=send_sem.at[k],
            recv_sem=recv_sem.at[k],
            device_id={"member": target},
            device_id_type=MESH_ID,
        )

    def start(k, carry):
        copy(k).start()
        return carry

    def finish(k, carry):
        copy(k).wait()
        return carry

    lax.fori_loop(1, n, start, 0)
    dst[me] = src[me]
    lax.fori_loop(1, n, finish, 0)


def pick_rows(n, source_ref, held, picked):
    def pick(i, carry):
        picked[i] = held[source_ref[i]]
        return carry

    lax.fori_loop(0, n, pick, 0)


def exploit_kernel(n, source_ref, send_ref, out_ref, held, picked, send1, recv1, send2, recv2):
    me = lax.axis_index("member")
    enter(n, me)
    transpose(n, me, send_ref, held, send1, recv1)
    pick_rows(n, source_ref, held, picked)
    transpose(n, me, picked, out_ref, send2, recv2)


def gather_kernel(n, source_ref, send_ref, out_ref, held, send1, recv1):
    me = lax.axis_index("member")
    enter(n, me)
    transpose(n, me, send_ref, held, send1, recv1)
    pick_rows(n, source_ref, held, out_ref)


def scatter_kernel(n, send_ref, out_ref, send1, recv1):
    me = lax.axis_index("member")
    enter(n, me)
    transpose(n, me, send_ref, out_ref, send1, recv1)


def member_call(body, packed, operands, scratch, kernel_id):
    n, rows, lanes = packed.shape
    moved = packed.size * packed.dtype.itemsize
    smem = [pl.BlockSpec(memory_space=pltpu.SMEM)] * (len(operands) - 1)
    return pl.pallas_call(
        functools.partial(body, n),
        out_shape=jax.ShapeDtypeStruct(packed.shape, packed.dtype),
        in_specs=smem + [pl.BlockSpec(memory_space=pltpu.VMEM)],
        out_specs=pl.BlockSpec(memory_space=pltpu.VMEM),
        scratch_shapes=scratch,
        compiler_params=pltpu.CompilerParams(
            collective_id=kernel_id, has_side_effects=True, vmem_limit_bytes=48 * 1024 * 1024
        ),
        cost_estimate=pl.CostEstimate(flops=0, transcendentals=0, bytes_accessed=moved * 20),
    )(*operands)


def exploit_transfer(packed, source, kernel_id):
    n, rows, lanes = packed.shape
    block = pltpu.VMEM((n, rows, lanes), packed.dtype)
    sems = [pltpu.SemaphoreType.DMA((n,))] * 4
    return member_call(exploit_kernel, packed, (source, packed), [block, block] + sems, kernel_id)


def exploit_gather(packed, source, kernel_id):
    n, rows, lanes = packed.shape
    block = pltpu.VMEM((n, rows, lanes), packed.dtype)
    sems = [pltpu.SemaphoreType.DMA((n,))] * 2
    return member_call(gather_kernel, packed, (source, packed), [block] + sems, kernel_id)


def exploit_scatter(packed, kernel_id):
    n = packed.shape[0]
    sems = [pltpu.SemaphoreType.DMA((n,))] * 2
    return member_call(scatter_kernel, packed, (packed,), sems, kernel_id)


def lane_major(part, lanes):
    rows, cols = part.shape
    return part.reshape(rows, cols // lanes, lanes).transpose(1, 0, 2).reshape(-1, lanes)


def from_lane_major(flat, shape, lanes):
    rows, cols = shape
    return flat.reshape(cols // lanes, rows, lanes).transpose(1, 0, 2).reshape(rows, cols)


def exploit_rows(parts, source, members, kernel_id):
    lanes = 128
    rows = [part.size // (members * lanes) for part in parts]
    pad = -sum(rows) % 16
    pieces = [part.astype(jnp.bfloat16).reshape(members, -1, lanes) for part in parts]
    if pad:
        pieces.append(jnp.zeros((members, pad, lanes), jnp.bfloat16))
    back = exploit_transfer(jnp.concatenate(pieces, axis=1), source, kernel_id)
    out = []
    start = 0
    for part, count in zip(parts, rows):
        out.append(back[:, start:start + count].reshape(part.shape))
        start += count
    return out


def pack_tiles(parts, members):
    lanes = 128
    flat = jnp.concatenate([lane_major(part.astype(jnp.bfloat16), lanes) for part in parts])
    return flat.reshape(members, -1, flat.shape[-1])


def unpack_tiles(back, parts):
    lanes = back.shape[-1]
    back = back.reshape(-1, lanes)
    out = []
    start = 0
    for part in parts:
        count = part.size // lanes
        out.append(from_lane_major(back[start:start + count], part.shape, lanes))
        start += count
    return out


def per_device(
    tokens,
    labels,
    source,
    learn_rate,
    weight_decay,
    classifier,
    up_param,
    up_first,
    up_second,
    down_param,
    down_first,
    down_second,
):
    members = lax.axis_size("member")
    shards = lax.axis_size("dp")
    me = lax.axis_index("member")
    own = source[me] == me

    up_bf, down_bf = exploit_rows((up_param[0], down_param[0]), source, members, 0)
    up_full = lax.all_gather(up_bf, "dp", axis=0, tiled=True)
    down_full = lax.all_gather(down_bf, "dp", axis=0, tiled=True)
    moments = (up_first[0], down_first[0], up_second[0], down_second[0])
    picked = exploit_gather(pack_tiles(moments, members), source, 1)
    up_full, down_full, picked = lax.optimization_barrier((up_full, down_full, picked))

    batch_total = tokens.shape[1] * shards
    up_gradient, down_gradient = local_gradients(
        tokens[0], labels[0], up_full, down_full, classifier, batch_total
    )
    up_term = up_gradient.astype(jnp.bfloat16)
    down_term = down_gradient.astype(jnp.bfloat16)
    up_term, down_term, picked = lax.optimization_barrier((up_term, down_term, picked))
    up_share = lax.psum_scatter(up_term, "dp", scatter_dimension=0, tiled=True)
    down_share = lax.psum_scatter(down_term, "dp", scatter_dimension=0, tiled=True)
    up_mom, down_mom, up_var_bf, down_var_bf = unpack_tiles(exploit_scatter(picked, 2), moments)
    up_share = up_share.astype(jnp.float32)
    down_share = down_share.astype(jnp.float32)

    up_now = jnp.where(own, up_param[0], up_bf.astype(jnp.float32))
    down_now = jnp.where(own, down_param[0], down_bf.astype(jnp.float32))
    up_var = jnp.where(own, up_second[0], up_var_bf.astype(jnp.float32))
    down_var = jnp.where(own, down_second[0], down_var_bf.astype(jnp.float32))

    rate_value = learn_rate[0]
    decay_value = weight_decay[0]
    up_new = adamw_step(up_now, up_mom, up_var, up_share, rate_value, decay_value)
    down_new = adamw_step(down_now, down_mom, down_var, down_share, rate_value, decay_value)
    return tuple(value[None] for value in up_new + down_new)


def solution(mesh):
    placed = (
        P("member", "dp", None, None),
        P("member", "dp"),
        P(),
        P("member"),
        P("member"),
        P(),
        P("member", "dp", None),
        P("member", "dp", None),
        P("member", "dp", None),
        P("member", "dp", None),
        P("member", "dp", None),
        P("member", "dp", None),
    )
    return jax.shard_map(
        per_device,
        mesh=mesh,
        in_specs=placed,
        out_specs=(P("member", "dp", None),) * 6,
        check_vma=False,
    )
```

```python
import functools

import jax
import jax.numpy as jnp
from jax import lax
from jax.experimental import pallas as pl
from jax.experimental.pallas import tpu as pltpu
from jax.sharding import PartitionSpec as P

MESH_ID = pl.DeviceIdType.MESH

STEP = 1000


def local_gradients(tokens, labels, up_weight, down_weight, classifier, batch_total):
    images, patches, features = tokens.shape
    hidden_units = up_weight.shape[1]
    token_rows = tokens.reshape(images * patches, features).astype(jnp.float32)
    center = token_rows - jnp.mean(token_rows, axis=1, keepdims=True)
    normed = (center * lax.rsqrt(jnp.mean(center * center, axis=1, keepdims=True) + 1e-06)).astype(
        jnp.bfloat16
    )
    preact = jnp.dot(normed, up_weight, preferred_element_type=jnp.float32) * features ** (-0.5)
    activated = (0.5 * preact * (1.0 + lax.erf(preact * 0.7071067811865476))).astype(jnp.bfloat16)
    residual = token_rows + jnp.dot(
        activated, down_weight, preferred_element_type=jnp.float32
    ) * hidden_units ** (-0.5)
    out_center = residual - jnp.mean(residual, axis=1, keepdims=True)
    inverse = lax.rsqrt(jnp.mean(out_center * out_center, axis=1, keepdims=True) + 1e-06)
    out_normed = out_center * inverse
    pooled = jnp.mean(out_normed.reshape(images, patches, features), axis=1).astype(jnp.bfloat16)
    logits = jnp.dot(pooled, classifier, preferred_element_type=jnp.float32)
    powered = jnp.exp(logits)
    softmax_out = powered / jnp.sum(powered, axis=1, keepdims=True)
    onehot = (labels[:, None] == jnp.arange(classifier.shape[1], dtype=jnp.int32)[None, :]).astype(
        jnp.float32
    )
    logit_delta = ((softmax_out - onehot) / batch_total).astype(jnp.bfloat16)
    pool_delta = (
        lax.dot_general(
            logit_delta, classifier, (((1,), (1,)), ((), ())), preferred_element_type=jnp.float32
        )
        / patches
    )
    token_delta = jnp.broadcast_to(pool_delta[:, None, :], (images, patches, features)).reshape(
        images * patches, features
    )
    residual_delta = inverse * (
        token_delta
        - jnp.mean(token_delta, axis=1, keepdims=True)
        - out_normed * jnp.mean(token_delta * out_normed, axis=1, keepdims=True)
    )
    residual_delta = residual_delta.astype(jnp.bfloat16)
    down_scale = hidden_units ** (-0.5)
    down_gradient = (
        lax.dot_general(
            activated, residual_delta, (((0,), (0,)), ((), ())), preferred_element_type=jnp.float32
        )
        * down_scale
    )
    hidden_delta = (
        lax.dot_general(
            residual_delta,
            down_weight,
            (((1,), (1,)), ((), ())),
            preferred_element_type=jnp.float32,
        )
        * down_scale
    )
    derivative = (
        0.5 * (1.0 + lax.erf(preact * 0.7071067811865476))
        + preact * jnp.exp(-0.5 * preact * preact) * 0.3989422804014327
    )
    preact_delta = (hidden_delta * derivative).astype(jnp.bfloat16)
    up_gradient = lax.dot_general(
        normed, preact_delta, (((0,), (0,)), ((), ())), preferred_element_type=jnp.float32
    ) * features ** (-0.5)
    return (up_gradient, down_gradient)


def adamw_step(param, first, second, gradient, rate_value, decay_value):
    moment = 0.9 * first.astype(jnp.float32) + 0.1 * gradient
    variance = 0.999 * second + 0.001 * gradient * gradient
    update = (
        moment / (1.0 - 0.9**STEP) / (jnp.sqrt(variance / (1.0 - 0.999**STEP)) + 1e-08)
        + decay_value * param
    )
    return (param - rate_value * update, moment.astype(jnp.bfloat16), variance)


def enter(n, me):
    barrier = pltpu.get_barrier_semaphore()

    def greet(k, carry):
        pl.semaphore_signal(
            barrier, inc=1, device_id={"member": lax.rem(me + k, n)}, device_id_type=MESH_ID
        )
        return carry

    lax.fori_loop(1, n, greet, 0)
    pl.semaphore_wait(barrier, n - 1)


def transpose(n, me, src, dst, send_sem, recv_sem):
    def copy(k):
        target = lax.rem(me + k, n)
        return pltpu.make_async_remote_copy(
            src_ref=src.at[target],
            dst_ref=dst.at[me],
            send_sem=send_sem.at[k],
            recv_sem=recv_sem.at[k],
            device_id={"member": target},
            device_id_type=MESH_ID,
        )

    def start(k, carry):
        copy(k).start()
        return carry

    def finish(k, carry):
        copy(k).wait()
        return carry

    lax.fori_loop(1, n, start, 0)
    dst[me] = src[me]
    lax.fori_loop(1, n, finish, 0)


def pick_rows(n, source_ref, held, picked):
    def pick(i, carry):
        picked[i] = held[source_ref[i]]
        return carry

    lax.fori_loop(0, n, pick, 0)


def exploit_kernel(n, source_ref, send_ref, out_ref, held, picked, send1, recv1, send2, recv2):
    me = lax.axis_index("member")
    enter(n, me)
    transpose(n, me, send_ref, held, send1, recv1)
    pick_rows(n, source_ref, held, picked)
    transpose(n, me, picked, out_ref, send2, recv2)


def gather_kernel(n, source_ref, send_ref, out_ref, held, send1, recv1):
    me = lax.axis_index("member")
    enter(n, me)
    transpose(n, me, send_ref, held, send1, recv1)
    pick_rows(n, source_ref, held, out_ref)


def scatter_kernel(n, send_ref, out_ref, send1, recv1):
    me = lax.axis_index("member")
    enter(n, me)
    transpose(n, me, send_ref, out_ref, send1, recv1)


def block_gradients(tokens, labels_ref, up_weight, down_weight, classifier, batch_total, patches):
    tokens_n, features = tokens.shape
    hidden_units = up_weight.shape[1]
    classes = classifier.shape[1]
    images = tokens_n // patches
    token_rows = tokens.astype(jnp.float32)
    center = token_rows - jnp.mean(token_rows, axis=1, keepdims=True)
    normed = (center * lax.rsqrt(jnp.mean(center * center, axis=1, keepdims=True) + 1e-06)).astype(
        jnp.bfloat16
    )
    preact = jnp.dot(normed, up_weight, preferred_element_type=jnp.float32) * features ** (-0.5)
    activated = (0.5 * preact * (1.0 + lax.erf(preact * 0.7071067811865476))).astype(jnp.bfloat16)
    residual = token_rows + jnp.dot(
        activated, down_weight, preferred_element_type=jnp.float32
    ) * hidden_units ** (-0.5)
    out_center = residual - jnp.mean(residual, axis=1, keepdims=True)
    inverse = lax.rsqrt(jnp.mean(out_center * out_center, axis=1, keepdims=True) + 1e-06)
    out_normed = out_center * inverse
    image_of_row = lax.broadcasted_iota(jnp.int32, (tokens_n, 1), 0) // patches
    pooled = jnp.concatenate(
        [
            jnp.sum(jnp.where(image_of_row == i, out_normed, 0.0), axis=0, keepdims=True)
            for i in range(images)
        ],
        axis=0,
    ) / patches
    pooled = pooled.astype(jnp.bfloat16)
    logits = jnp.dot(pooled, classifier, preferred_element_type=jnp.float32)
    powered = jnp.exp(logits)
    softmax_out = powered / jnp.sum(powered, axis=1, keepdims=True)
    row = lax.broadcasted_iota(jnp.int32, (images, classes), 0)
    column = lax.broadcasted_iota(jnp.int32, (images, classes), 1)
    label = jnp.zeros((images, classes), jnp.int32)
    for i in range(images):
        label = jnp.where(row == i, labels_ref[i], label)
    onehot = (column == label).astype(jnp.float32)
    logit_delta = ((softmax_out - onehot) / batch_total).astype(jnp.bfloat16)
    pool_delta = (
        lax.dot_general(
            logit_delta, classifier, (((1,), (1,)), ((), ())), preferred_element_type=jnp.float32
        )
        / patches
    )
    token_delta = jnp.zeros((tokens_n, features), jnp.float32)
    for i in range(images):
        token_delta = jnp.where(image_of_row == i, pool_delta[i:i + 1, :], token_delta)
    residual_delta = inverse * (
        token_delta
        - jnp.mean(token_delta, axis=1, keepdims=True)
        - out_normed * jnp.mean(token_delta * out_normed, axis=1, keepdims=True)
    )
    residual_delta = residual_delta.astype(jnp.bfloat16)
    down_scale = hidden_units ** (-0.5)
    down_gradient = (
        lax.dot_general(
            activated, residual_delta, (((0,), (0,)), ((), ())), preferred_element_type=jnp.float32
        )
        * down_scale
    )
    hidden_delta = (
        lax.dot_general(
            residual_delta, down_weight, (((1,), (1,)), ((), ())), preferred_element_type=jnp.float32
        )
        * down_scale
    )
    derivative = (
        0.5 * (1.0 + lax.erf(preact * 0.7071067811865476))
        + preact * jnp.exp(-0.5 * preact * preact) * 0.3989422804014327
    )
    preact_delta = (hidden_delta * derivative).astype(jnp.bfloat16)
    up_gradient = lax.dot_general(
        normed, preact_delta, (((0,), (0,)), ((), ())), preferred_element_type=jnp.float32
    ) * features ** (-0.5)
    return up_gradient, down_gradient


def scatter_compute_kernel(
    n, batch_total, patches, labels_ref, send_ref, tokens_ref, up_ref, down_ref, classifier_ref,
    out_ref, up_grad_ref, down_grad_ref, send_sem, recv_sem,
):
    me = lax.axis_index("member")
    enter(n, me)

    def copy(k):
        target = lax.rem(me + k, n)
        return pltpu.make_async_remote_copy(
            src_ref=send_ref.at[target],
            dst_ref=out_ref.at[me],
            send_sem=send_sem.at[k],
            recv_sem=recv_sem.at[k],
            device_id={"member": target},
            device_id_type=MESH_ID,
        )

    def start(k, carry):
        copy(k).start()
        return carry

    def finish(k, carry):
        copy(k).wait()
        return carry

    lax.fori_loop(1, n, start, 0)
    out_ref[me] = send_ref[me]
    up_gradient, down_gradient = block_gradients(
        tokens_ref[...], labels_ref, up_ref[...], down_ref[...], classifier_ref[...],
        batch_total, patches,
    )
    up_grad_ref[...] = up_gradient.astype(up_grad_ref.dtype)
    down_grad_ref[...] = down_gradient.astype(down_grad_ref.dtype)
    lax.fori_loop(1, n, finish, 0)


def scatter_with_gradients(picked, tokens, labels, up_full, down_full, classifier, batch_total,
                           kernel_id):
    n = picked.shape[0]
    images, patches, features = tokens.shape
    vmem = pl.BlockSpec(memory_space=pltpu.VMEM)
    moved = picked.size * picked.dtype.itemsize
    flops = 12 * images * patches * features * up_full.shape[1]
    return pl.pallas_call(
        functools.partial(scatter_compute_kernel, n, batch_total, patches),
        out_shape=(
            jax.ShapeDtypeStruct(picked.shape, picked.dtype),
            jax.ShapeDtypeStruct(up_full.shape, jnp.bfloat16),
            jax.ShapeDtypeStruct(down_full.shape, jnp.bfloat16),
        ),
        in_specs=[pl.BlockSpec(memory_space=pltpu.SMEM)] + [vmem] * 5,
        out_specs=(vmem, vmem, vmem),
        scratch_shapes=[pltpu.SemaphoreType.DMA((n,)), pltpu.SemaphoreType.DMA((n,))],
        compiler_params=pltpu.CompilerParams(
            collective_id=kernel_id, has_side_effects=True, vmem_limit_bytes=63 * 1024 * 1024
        ),
        cost_estimate=pl.CostEstimate(flops=flops, transcendentals=0, bytes_accessed=moved * 20),
    )(labels, picked, tokens.reshape(images * patches, features), up_full, down_full, classifier)


def member_call(body, packed, operands, scratch, kernel_id):
    n, rows, lanes = packed.shape
    moved = packed.size * packed.dtype.itemsize
    smem = [pl.BlockSpec(memory_space=pltpu.SMEM)] * (len(operands) - 1)
    return pl.pallas_call(
        functools.partial(body, n),
        out_shape=jax.ShapeDtypeStruct(packed.shape, packed.dtype),
        in_specs=smem + [pl.BlockSpec(memory_space=pltpu.VMEM)],
        out_specs=pl.BlockSpec(memory_space=pltpu.VMEM),
        scratch_shapes=scratch,
        compiler_params=pltpu.CompilerParams(
            collective_id=kernel_id, has_side_effects=True, vmem_limit_bytes=48 * 1024 * 1024
        ),
        cost_estimate=pl.CostEstimate(flops=0, transcendentals=0, bytes_accessed=moved * 20),
    )(*operands)


def exploit_transfer(packed, source, kernel_id):
    n, rows, lanes = packed.shape
    block = pltpu.VMEM((n, rows, lanes), packed.dtype)
    sems = [pltpu.SemaphoreType.DMA((n,))] * 4
    return member_call(exploit_kernel, packed, (source, packed), [block, block] + sems, kernel_id)


def exploit_gather(packed, source, kernel_id):
    n, rows, lanes = packed.shape
    block = pltpu.VMEM((n, rows, lanes), packed.dtype)
    sems = [pltpu.SemaphoreType.DMA((n,))] * 2
    return member_call(gather_kernel, packed, (source, packed), [block] + sems, kernel_id)


def exploit_scatter(packed, kernel_id):
    n = packed.shape[0]
    sems = [pltpu.SemaphoreType.DMA((n,))] * 2
    return member_call(scatter_kernel, packed, (packed,), sems, kernel_id)


def lane_major(part, lanes):
    rows, cols = part.shape
    return part.reshape(rows, cols // lanes, lanes).transpose(1, 0, 2).reshape(-1, lanes)


def from_lane_major(flat, shape, lanes):
    rows, cols = shape
    return flat.reshape(cols // lanes, rows, lanes).transpose(1, 0, 2).reshape(rows, cols)


def exploit_rows(parts, source, members, kernel_id):
    lanes = 128
    rows = [part.size // (members * lanes) for part in parts]
    pad = -sum(rows) % 16
    pieces = [part.astype(jnp.bfloat16).reshape(members, -1, lanes) for part in parts]
    if pad:
        pieces.append(jnp.zeros((members, pad, lanes), jnp.bfloat16))
    back = exploit_transfer(jnp.concatenate(pieces, axis=1), source, kernel_id)
    out = []
    start = 0
    for part, count in zip(parts, rows):
        out.append(back[:, start:start + count].reshape(part.shape))
        start += count
    return out


def pack_tiles(parts, members):
    lanes = 128
    flat = jnp.concatenate([lane_major(part.astype(jnp.bfloat16), lanes) for part in parts])
    return flat.reshape(members, -1, flat.shape[-1])


def unpack_tiles(back, parts):
    lanes = back.shape[-1]
    back = back.reshape(-1, lanes)
    out = []
    start = 0
    for part in parts:
        count = part.size // lanes
        out.append(from_lane_major(back[start:start + count], part.shape, lanes))
        start += count
    return out


def per_device(
    tokens,
    labels,
    source,
    learn_rate,
    weight_decay,
    classifier,
    up_param,
    up_first,
    up_second,
    down_param,
    down_first,
    down_second,
):
    members = lax.axis_size("member")
    shards = lax.axis_size("dp")
    me = lax.axis_index("member")
    own = source[me] == me

    up_bf, down_bf = exploit_rows((up_param[0], down_param[0]), source, members, 0)
    up_full = lax.all_gather(up_bf, "dp", axis=0, tiled=True)
    down_full = lax.all_gather(down_bf, "dp", axis=0, tiled=True)
    moments = (up_first[0], down_first[0], up_second[0], down_second[0])
    picked = exploit_gather(pack_tiles(moments, members), source, 1)
    up_full, down_full, picked = lax.optimization_barrier((up_full, down_full, picked))

    batch_total = tokens.shape[1] * shards
    back, up_term, down_term = scatter_with_gradients(
        picked, tokens[0], labels[0], up_full, down_full, classifier, batch_total, 2
    )
    up_share = lax.psum_scatter(up_term, "dp", scatter_dimension=0, tiled=True)
    down_share = lax.psum_scatter(down_term, "dp", scatter_dimension=0, tiled=True)
    up_mom, down_mom, up_var_bf, down_var_bf = unpack_tiles(back, moments)
    up_share = up_share.astype(jnp.float32)
    down_share = down_share.astype(jnp.float32)

    up_now = jnp.where(own, up_param[0], up_bf.astype(jnp.float32))
    down_now = jnp.where(own, down_param[0], down_bf.astype(jnp.float32))
    up_var = jnp.where(own, up_second[0], up_var_bf.astype(jnp.float32))
    down_var = jnp.where(own, down_second[0], down_var_bf.astype(jnp.float32))

    rate_value = learn_rate[0]
    decay_value = weight_decay[0]
    up_new = adamw_step(up_now, up_mom, up_var, up_share, rate_value, decay_value)
    down_new = adamw_step(down_now, down_mom, down_var, down_share, rate_value, decay_value)
    return tuple(value[None] for value in up_new + down_new)


def solution(mesh):
    placed = (
        P("member", "dp", None, None),
        P("member", "dp"),
        P(),
        P("member"),
        P("member"),
        P(),
        P("member", "dp", None),
        P("member", "dp", None),
        P("member", "dp", None),
        P("member", "dp", None),
        P("member", "dp", None),
        P("member", "dp", None),
    )
    return jax.shard_map(
        per_device,
        mesh=mesh,
        in_specs=placed,
        out_specs=(P("member", "dp", None),) * 6,
        check_vma=False,
    )
```

```python
import functools

import jax
import jax.numpy as jnp
from jax import lax
from jax.experimental import pallas as pl
from jax.experimental.pallas import tpu as pltpu
from jax.sharding import PartitionSpec as P

MESH_ID = pl.DeviceIdType.MESH

STEP = 1000


def local_gradients(tokens, labels, up_weight, down_weight, classifier, batch_total):
    images, patches, features = tokens.shape
    hidden_units = up_weight.shape[1]
    token_rows = tokens.reshape(images * patches, features).astype(jnp.float32)
    center = token_rows - jnp.mean(token_rows, axis=1, keepdims=True)
    normed = (center * lax.rsqrt(jnp.mean(center * center, axis=1, keepdims=True) + 1e-06)).astype(
        jnp.bfloat16
    )
    preact = jnp.dot(normed, up_weight, preferred_element_type=jnp.float32) * features ** (-0.5)
    activated = (0.5 * preact * (1.0 + lax.erf(preact * 0.7071067811865476))).astype(jnp.bfloat16)
    residual = token_rows + jnp.dot(
        activated, down_weight, preferred_element_type=jnp.float32
    ) * hidden_units ** (-0.5)
    out_center = residual - jnp.mean(residual, axis=1, keepdims=True)
    inverse = lax.rsqrt(jnp.mean(out_center * out_center, axis=1, keepdims=True) + 1e-06)
    out_normed = out_center * inverse
    pooled = jnp.mean(out_normed.reshape(images, patches, features), axis=1).astype(jnp.bfloat16)
    logits = jnp.dot(pooled, classifier, preferred_element_type=jnp.float32)
    powered = jnp.exp(logits)
    softmax_out = powered / jnp.sum(powered, axis=1, keepdims=True)
    onehot = (labels[:, None] == jnp.arange(classifier.shape[1], dtype=jnp.int32)[None, :]).astype(
        jnp.float32
    )
    logit_delta = ((softmax_out - onehot) / batch_total).astype(jnp.bfloat16)
    pool_delta = (
        lax.dot_general(
            logit_delta, classifier, (((1,), (1,)), ((), ())), preferred_element_type=jnp.float32
        )
        / patches
    )
    token_delta = jnp.broadcast_to(pool_delta[:, None, :], (images, patches, features)).reshape(
        images * patches, features
    )
    residual_delta = inverse * (
        token_delta
        - jnp.mean(token_delta, axis=1, keepdims=True)
        - out_normed * jnp.mean(token_delta * out_normed, axis=1, keepdims=True)
    )
    residual_delta = residual_delta.astype(jnp.bfloat16)
    down_scale = hidden_units ** (-0.5)
    down_gradient = (
        lax.dot_general(
            activated, residual_delta, (((0,), (0,)), ((), ())), preferred_element_type=jnp.float32
        )
        * down_scale
    )
    hidden_delta = (
        lax.dot_general(
            residual_delta,
            down_weight,
            (((1,), (1,)), ((), ())),
            preferred_element_type=jnp.float32,
        )
        * down_scale
    )
    derivative = (
        0.5 * (1.0 + lax.erf(preact * 0.7071067811865476))
        + preact * jnp.exp(-0.5 * preact * preact) * 0.3989422804014327
    )
    preact_delta = (hidden_delta * derivative).astype(jnp.bfloat16)
    up_gradient = lax.dot_general(
        normed, preact_delta, (((0,), (0,)), ((), ())), preferred_element_type=jnp.float32
    ) * features ** (-0.5)
    return (up_gradient, down_gradient)


def adamw_step(param, first, second, gradient, rate_value, decay_value):
    moment = 0.9 * first.astype(jnp.float32) + 0.1 * gradient
    variance = 0.999 * second + 0.001 * gradient * gradient
    update = (
        moment / (1.0 - 0.9**STEP) / (jnp.sqrt(variance / (1.0 - 0.999**STEP)) + 1e-08)
        + decay_value * param
    )
    return (param - rate_value * update, moment.astype(jnp.bfloat16), variance)


def enter(n, me):
    barrier = pltpu.get_barrier_semaphore()

    def greet(k, carry):
        pl.semaphore_signal(
            barrier, inc=1, device_id={"member": lax.rem(me + k, n)}, device_id_type=MESH_ID
        )
        return carry

    lax.fori_loop(1, n, greet, 0)
    pl.semaphore_wait(barrier, n - 1)


def transpose(n, me, src, dst, send_sem, recv_sem):
    def copy(k):
        target = lax.rem(me + k, n)
        return pltpu.make_async_remote_copy(
            src_ref=src.at[target],
            dst_ref=dst.at[me],
            send_sem=send_sem.at[k],
            recv_sem=recv_sem.at[k],
            device_id={"member": target},
            device_id_type=MESH_ID,
        )

    def start(k, carry):
        copy(k).start()
        return carry

    def finish(k, carry):
        copy(k).wait()
        return carry

    lax.fori_loop(1, n, start, 0)
    dst[me] = src[me]
    lax.fori_loop(1, n, finish, 0)


def pick_rows(n, source_ref, held, picked):
    def pick(i, carry):
        picked[i] = held[source_ref[i]]
        return carry

    lax.fori_loop(0, n, pick, 0)


def exploit_kernel(n, source_ref, send_ref, out_ref, held, picked, send1, recv1, send2, recv2):
    me = lax.axis_index("member")
    enter(n, me)
    transpose(n, me, send_ref, held, send1, recv1)
    pick_rows(n, source_ref, held, picked)
    transpose(n, me, picked, out_ref, send2, recv2)


def gather_kernel(n, source_ref, send_ref, out_ref, held, send1, recv1):
    me = lax.axis_index("member")
    enter(n, me)
    transpose(n, me, send_ref, held, send1, recv1)
    pick_rows(n, source_ref, held, out_ref)


def scatter_kernel(n, send_ref, out_ref, send1, recv1):
    me = lax.axis_index("member")
    enter(n, me)
    transpose(n, me, send_ref, out_ref, send1, recv1)


def block_gradients(tokens, labels_ref, up_weight, down_weight, classifier, batch_total, patches):
    tokens_n, features = tokens.shape
    hidden_units = up_weight.shape[1]
    classes = classifier.shape[1]
    images = tokens_n // patches
    token_rows = tokens.astype(jnp.float32)
    center = token_rows - jnp.mean(token_rows, axis=1, keepdims=True)
    normed = (center * lax.rsqrt(jnp.mean(center * center, axis=1, keepdims=True) + 1e-06)).astype(
        jnp.bfloat16
    )
    preact = jnp.dot(normed, up_weight, preferred_element_type=jnp.float32) * features ** (-0.5)
    activated = (0.5 * preact * (1.0 + lax.erf(preact * 0.7071067811865476))).astype(jnp.bfloat16)
    residual = token_rows + jnp.dot(
        activated, down_weight, preferred_element_type=jnp.float32
    ) * hidden_units ** (-0.5)
    out_center = residual - jnp.mean(residual, axis=1, keepdims=True)
    inverse = lax.rsqrt(jnp.mean(out_center * out_center, axis=1, keepdims=True) + 1e-06)
    out_normed = out_center * inverse
    image_of_row = lax.broadcasted_iota(jnp.int32, (tokens_n, 1), 0) // patches
    pooled = jnp.concatenate(
        [
            jnp.sum(jnp.where(image_of_row == i, out_normed, 0.0), axis=0, keepdims=True)
            for i in range(images)
        ],
        axis=0,
    ) / patches
    pooled = pooled.astype(jnp.bfloat16)
    logits = jnp.dot(pooled, classifier, preferred_element_type=jnp.float32)
    powered = jnp.exp(logits)
    softmax_out = powered / jnp.sum(powered, axis=1, keepdims=True)
    row = lax.broadcasted_iota(jnp.int32, (images, classes), 0)
    column = lax.broadcasted_iota(jnp.int32, (images, classes), 1)
    label = jnp.zeros((images, classes), jnp.int32)
    for i in range(images):
        label = jnp.where(row == i, labels_ref[i], label)
    onehot = (column == label).astype(jnp.float32)
    logit_delta = ((softmax_out - onehot) / batch_total).astype(jnp.bfloat16)
    pool_delta = (
        lax.dot_general(
            logit_delta, classifier, (((1,), (1,)), ((), ())), preferred_element_type=jnp.float32
        )
        / patches
    )
    token_delta = jnp.zeros((tokens_n, features), jnp.float32)
    for i in range(images):
        token_delta = jnp.where(image_of_row == i, pool_delta[i:i + 1, :], token_delta)
    residual_delta = inverse * (
        token_delta
        - jnp.mean(token_delta, axis=1, keepdims=True)
        - out_normed * jnp.mean(token_delta * out_normed, axis=1, keepdims=True)
    )
    residual_delta = residual_delta.astype(jnp.bfloat16)
    down_scale = hidden_units ** (-0.5)
    down_gradient = (
        lax.dot_general(
            activated, residual_delta, (((0,), (0,)), ((), ())), preferred_element_type=jnp.float32
        )
        * down_scale
    )
    hidden_delta = (
        lax.dot_general(
            residual_delta, down_weight, (((1,), (1,)), ((), ())), preferred_element_type=jnp.float32
        )
        * down_scale
    )
    derivative = (
        0.5 * (1.0 + lax.erf(preact * 0.7071067811865476))
        + preact * jnp.exp(-0.5 * preact * preact) * 0.3989422804014327
    )
    preact_delta = (hidden_delta * derivative).astype(jnp.bfloat16)
    up_gradient = lax.dot_general(
        normed, preact_delta, (((0,), (0,)), ((), ())), preferred_element_type=jnp.float32
    ) * features ** (-0.5)
    return up_gradient, down_gradient


def scatter_compute_kernel(
    n, batch_total, patches, labels_ref, send_ref, tokens_ref, up_ref, down_ref, classifier_ref,
    out_ref, up_share_ref, down_share_ref,
    up_term, down_term, up_near, down_near, up_part, down_part, up_far, down_far,
    send_sem, recv_sem, near_send, near_recv, far_send, far_recv,
):
    me = lax.axis_index("member")
    shard = lax.axis_index("dp")
    core = shard % 2
    chip = shard // 2
    partner = chip * 2 + (1 - core)
    across = (1 - chip) * 2 + core
    diagonal = (1 - chip) * 2 + (1 - core)

    barrier = pltpu.get_barrier_semaphore()

    def greet(k, carry):
        pl.semaphore_signal(
            barrier, inc=1, device_id={"member": lax.rem(me + k, n)}, device_id_type=MESH_ID
        )
        return carry

    lax.fori_loop(1, n, greet, 0)
    for peer in (partner, across, diagonal):
        pl.semaphore_signal(barrier, inc=1, device_id={"dp": peer}, device_id_type=MESH_ID)
    pl.semaphore_wait(barrier, n - 1 + 3)

    def copy(k):
        target = lax.rem(me + k, n)
        return pltpu.make_async_remote_copy(
            src_ref=send_ref.at[target],
            dst_ref=out_ref.at[me],
            send_sem=send_sem.at[k],
            recv_sem=recv_sem.at[k],
            device_id={"member": target},
            device_id_type=MESH_ID,
        )

    def start(k, carry):
        copy(k).start()
        return carry

    def finish(k, carry):
        copy(k).wait()
        return carry

    lax.fori_loop(1, n, start, 0)
    out_ref[me] = send_ref[me]
    up_gradient, down_gradient = block_gradients(
        tokens_ref[...], labels_ref, up_ref[...], down_ref[...], classifier_ref[...],
        batch_total, patches,
    )
    up_term[...] = up_gradient.astype(jnp.bfloat16)
    down_term[...] = down_gradient.astype(jnp.bfloat16)

    def rows(term, index):
        size = term.shape[0] // 4
        return term.at[pl.ds(pl.multiple_of(index * size, size), size)]

    near = []
    slot = 0
    for term, near_buf in ((up_term, up_near), (down_term, down_near)):
        for which, index in ((0, diagonal), (1, partner)):
            near.append(
                pltpu.make_async_remote_copy(
                    src_ref=rows(term, index),
                    dst_ref=near_buf.at[which],
                    send_sem=near_send.at[slot],
                    recv_sem=near_recv.at[slot],
                    device_id={"dp": partner},
                    device_id_type=MESH_ID,
                )
            )
            slot += 1
    for item in near:
        item.start()
    for item in near:
        item.wait()

    far = []
    slot = 0
    for term, near_buf, part, far_buf in (
        (up_term, up_near, up_part, up_far),
        (down_term, down_near, down_part, down_far),
    ):
        part[...] = (
            rows(term, across)[...].astype(jnp.float32) + near_buf[0].astype(jnp.float32)
        ).astype(jnp.bfloat16)
        far.append(
            pltpu.make_async_remote_copy(
                src_ref=part,
                dst_ref=far_buf,
                send_sem=far_send.at[slot],
                recv_sem=far_recv.at[slot],
                device_id={"dp": across},
                device_id_type=MESH_ID,
            )
        )
        slot += 1
    for item in far:
        item.start()
    for item in far:
        item.wait()

    for term, near_buf, far_buf, share in (
        (up_term, up_near, up_far, up_share_ref),
        (down_term, down_near, down_far, down_share_ref),
    ):
        share[...] = (
            rows(term, shard)[...].astype(jnp.float32)
            + near_buf[1].astype(jnp.float32)
            + far_buf[...].astype(jnp.float32)
        )
    lax.fori_loop(1, n, finish, 0)


def scatter_with_gradients(picked, tokens, labels, up_full, down_full, classifier, batch_total,
                           kernel_id):
    n = picked.shape[0]
    images, patches, features = tokens.shape
    vmem = pl.BlockSpec(memory_space=pltpu.VMEM)
    moved = picked.size * picked.dtype.itemsize
    flops = 12 * images * patches * features * up_full.shape[1]
    up_rows = (up_full.shape[0] // 4, up_full.shape[1])
    down_rows = (down_full.shape[0] // 4, down_full.shape[1])
    bf16 = jnp.bfloat16
    return pl.pallas_call(
        functools.partial(scatter_compute_kernel, n, batch_total, patches),
        out_shape=(
            jax.ShapeDtypeStruct(picked.shape, picked.dtype),
            jax.ShapeDtypeStruct(up_rows, jnp.float32),
            jax.ShapeDtypeStruct(down_rows, jnp.float32),
        ),
        in_specs=[pl.BlockSpec(memory_space=pltpu.SMEM)] + [vmem] * 5,
        out_specs=(vmem, vmem, vmem),
        scratch_shapes=[
            pltpu.VMEM(up_full.shape, bf16),
            pltpu.VMEM(down_full.shape, bf16),
            pltpu.VMEM((2,) + up_rows, bf16),
            pltpu.VMEM((2,) + down_rows, bf16),
            pltpu.VMEM(up_rows, bf16),
            pltpu.VMEM(down_rows, bf16),
            pltpu.VMEM(up_rows, bf16),
            pltpu.VMEM(down_rows, bf16),
            pltpu.SemaphoreType.DMA((n,)),
            pltpu.SemaphoreType.DMA((n,)),
            pltpu.SemaphoreType.DMA((4,)),
            pltpu.SemaphoreType.DMA((4,)),
            pltpu.SemaphoreType.DMA((2,)),
            pltpu.SemaphoreType.DMA((2,)),
        ],
        compiler_params=pltpu.CompilerParams(
            collective_id=kernel_id, has_side_effects=True, vmem_limit_bytes=63 * 1024 * 1024
        ),
        cost_estimate=pl.CostEstimate(flops=flops, transcendentals=0, bytes_accessed=moved * 20),
    )(labels, picked, tokens.reshape(images * patches, features), up_full, down_full, classifier)


def member_call(body, packed, operands, scratch, kernel_id):
    n, rows, lanes = packed.shape
    moved = packed.size * packed.dtype.itemsize
    smem = [pl.BlockSpec(memory_space=pltpu.SMEM)] * (len(operands) - 1)
    return pl.pallas_call(
        functools.partial(body, n),
        out_shape=jax.ShapeDtypeStruct(packed.shape, packed.dtype),
        in_specs=smem + [pl.BlockSpec(memory_space=pltpu.VMEM)],
        out_specs=pl.BlockSpec(memory_space=pltpu.VMEM),
        scratch_shapes=scratch,
        compiler_params=pltpu.CompilerParams(
            collective_id=kernel_id, has_side_effects=True, vmem_limit_bytes=48 * 1024 * 1024
        ),
        cost_estimate=pl.CostEstimate(flops=0, transcendentals=0, bytes_accessed=moved * 20),
    )(*operands)


def exploit_transfer(packed, source, kernel_id):
    n, rows, lanes = packed.shape
    block = pltpu.VMEM((n, rows, lanes), packed.dtype)
    sems = [pltpu.SemaphoreType.DMA((n,))] * 4
    return member_call(exploit_kernel, packed, (source, packed), [block, block] + sems, kernel_id)


def exploit_gather(packed, source, kernel_id):
    n, rows, lanes = packed.shape
    block = pltpu.VMEM((n, rows, lanes), packed.dtype)
    sems = [pltpu.SemaphoreType.DMA((n,))] * 2
    return member_call(gather_kernel, packed, (source, packed), [block] + sems, kernel_id)


def exploit_scatter(packed, kernel_id):
    n = packed.shape[0]
    sems = [pltpu.SemaphoreType.DMA((n,))] * 2
    return member_call(scatter_kernel, packed, (packed,), sems, kernel_id)


def lane_major(part, lanes):
    rows, cols = part.shape
    return part.reshape(rows, cols // lanes, lanes).transpose(1, 0, 2).reshape(-1, lanes)


def from_lane_major(flat, shape, lanes):
    rows, cols = shape
    return flat.reshape(cols // lanes, rows, lanes).transpose(1, 0, 2).reshape(rows, cols)


def exploit_rows(parts, source, members, kernel_id):
    lanes = 128
    rows = [part.size // (members * lanes) for part in parts]
    pad = -sum(rows) % 16
    pieces = [part.astype(jnp.bfloat16).reshape(members, -1, lanes) for part in parts]
    if pad:
        pieces.append(jnp.zeros((members, pad, lanes), jnp.bfloat16))
    back = exploit_transfer(jnp.concatenate(pieces, axis=1), source, kernel_id)
    out = []
    start = 0
    for part, count in zip(parts, rows):
        out.append(back[:, start:start + count].reshape(part.shape))
        start += count
    return out


def pack_tiles(parts, members):
    lanes = 128
    flat = jnp.concatenate([lane_major(part.astype(jnp.bfloat16), lanes) for part in parts])
    return flat.reshape(members, -1, flat.shape[-1])


def unpack_tiles(back, parts):
    lanes = back.shape[-1]
    back = back.reshape(-1, lanes)
    out = []
    start = 0
    for part in parts:
        count = part.size // lanes
        out.append(from_lane_major(back[start:start + count], part.shape, lanes))
        start += count
    return out


def per_device(
    tokens,
    labels,
    source,
    learn_rate,
    weight_decay,
    classifier,
    up_param,
    up_first,
    up_second,
    down_param,
    down_first,
    down_second,
):
    members = lax.axis_size("member")
    shards = lax.axis_size("dp")
    me = lax.axis_index("member")
    own = source[me] == me

    up_bf, down_bf = exploit_rows((up_param[0], down_param[0]), source, members, 0)
    up_full = lax.all_gather(up_bf, "dp", axis=0, tiled=True)
    down_full = lax.all_gather(down_bf, "dp", axis=0, tiled=True)
    moments = (up_first[0], down_first[0], up_second[0], down_second[0])
    picked = exploit_gather(pack_tiles(moments, members), source, 1)
    up_full, down_full, picked = lax.optimization_barrier((up_full, down_full, picked))

    batch_total = tokens.shape[1] * shards
    back, up_share, down_share = scatter_with_gradients(
        picked, tokens[0], labels[0], up_full, down_full, classifier, batch_total, 2
    )
    up_mom, down_mom, up_var_bf, down_var_bf = unpack_tiles(back, moments)

    up_now = jnp.where(own, up_param[0], up_bf.astype(jnp.float32))
    down_now = jnp.where(own, down_param[0], down_bf.astype(jnp.float32))
    up_var = jnp.where(own, up_second[0], up_var_bf.astype(jnp.float32))
    down_var = jnp.where(own, down_second[0], down_var_bf.astype(jnp.float32))

    rate_value = learn_rate[0]
    decay_value = weight_decay[0]
    up_new = adamw_step(up_now, up_mom, up_var, up_share, rate_value, decay_value)
    down_new = adamw_step(down_now, down_mom, down_var, down_share, rate_value, decay_value)
    return tuple(value[None] for value in up_new + down_new)


def solution(mesh):
    placed = (
        P("member", "dp", None, None),
        P("member", "dp"),
        P(),
        P("member"),
        P("member"),
        P(),
        P("member", "dp", None),
        P("member", "dp", None),
        P("member", "dp", None),
        P("member", "dp", None),
        P("member", "dp", None),
        P("member", "dp", None),
    )
    return jax.shard_map(
        per_device,
        mesh=mesh,
        in_specs=placed,
        out_specs=(P("member", "dp", None),) * 6,
        check_vma=False,
    )
```

```python
import functools

import jax
import jax.numpy as jnp
from jax import lax
from jax.experimental import pallas as pl
from jax.experimental.pallas import tpu as pltpu
from jax.sharding import PartitionSpec as P

MESH_ID = pl.DeviceIdType.MESH

STEP = 1000


def local_gradients(tokens, labels, up_weight, down_weight, classifier, batch_total):
    images, patches, features = tokens.shape
    hidden_units = up_weight.shape[1]
    token_rows = tokens.reshape(images * patches, features).astype(jnp.float32)
    center = token_rows - jnp.mean(token_rows, axis=1, keepdims=True)
    normed = (center * lax.rsqrt(jnp.mean(center * center, axis=1, keepdims=True) + 1e-06)).astype(
        jnp.bfloat16
    )
    preact = jnp.dot(normed, up_weight, preferred_element_type=jnp.float32) * features ** (-0.5)
    activated = (0.5 * preact * (1.0 + lax.erf(preact * 0.7071067811865476))).astype(jnp.bfloat16)
    residual = token_rows + jnp.dot(
        activated, down_weight, preferred_element_type=jnp.float32
    ) * hidden_units ** (-0.5)
    out_center = residual - jnp.mean(residual, axis=1, keepdims=True)
    inverse = lax.rsqrt(jnp.mean(out_center * out_center, axis=1, keepdims=True) + 1e-06)
    out_normed = out_center * inverse
    pooled = jnp.mean(out_normed.reshape(images, patches, features), axis=1).astype(jnp.bfloat16)
    logits = jnp.dot(pooled, classifier, preferred_element_type=jnp.float32)
    powered = jnp.exp(logits)
    softmax_out = powered / jnp.sum(powered, axis=1, keepdims=True)
    onehot = (labels[:, None] == jnp.arange(classifier.shape[1], dtype=jnp.int32)[None, :]).astype(
        jnp.float32
    )
    logit_delta = ((softmax_out - onehot) / batch_total).astype(jnp.bfloat16)
    pool_delta = (
        lax.dot_general(
            logit_delta, classifier, (((1,), (1,)), ((), ())), preferred_element_type=jnp.float32
        )
        / patches
    )
    token_delta = jnp.broadcast_to(pool_delta[:, None, :], (images, patches, features)).reshape(
        images * patches, features
    )
    residual_delta = inverse * (
        token_delta
        - jnp.mean(token_delta, axis=1, keepdims=True)
        - out_normed * jnp.mean(token_delta * out_normed, axis=1, keepdims=True)
    )
    residual_delta = residual_delta.astype(jnp.bfloat16)
    down_scale = hidden_units ** (-0.5)
    down_gradient = (
        lax.dot_general(
            activated, residual_delta, (((0,), (0,)), ((), ())), preferred_element_type=jnp.float32
        )
        * down_scale
    )
    hidden_delta = (
        lax.dot_general(
            residual_delta,
            down_weight,
            (((1,), (1,)), ((), ())),
            preferred_element_type=jnp.float32,
        )
        * down_scale
    )
    derivative = (
        0.5 * (1.0 + lax.erf(preact * 0.7071067811865476))
        + preact * jnp.exp(-0.5 * preact * preact) * 0.3989422804014327
    )
    preact_delta = (hidden_delta * derivative).astype(jnp.bfloat16)
    up_gradient = lax.dot_general(
        normed, preact_delta, (((0,), (0,)), ((), ())), preferred_element_type=jnp.float32
    ) * features ** (-0.5)
    return (up_gradient, down_gradient)


def adamw_step(param, first, second, gradient, rate_value, decay_value):
    moment = 0.9 * first.astype(jnp.float32) + 0.1 * gradient
    variance = 0.999 * second + 0.001 * gradient * gradient
    update = (
        moment / (1.0 - 0.9**STEP) / (jnp.sqrt(variance / (1.0 - 0.999**STEP)) + 1e-08)
        + decay_value * param
    )
    return (param - rate_value * update, moment.astype(jnp.bfloat16), variance)


def enter(n, me):
    barrier = pltpu.get_barrier_semaphore()

    def greet(k, carry):
        pl.semaphore_signal(
            barrier, inc=1, device_id={"member": lax.rem(me + k, n)}, device_id_type=MESH_ID
        )
        return carry

    lax.fori_loop(1, n, greet, 0)
    pl.semaphore_wait(barrier, n - 1)


def transpose(n, me, src, dst, send_sem, recv_sem):
    def copy(k):
        target = lax.rem(me + k, n)
        return pltpu.make_async_remote_copy(
            src_ref=src.at[target],
            dst_ref=dst.at[me],
            send_sem=send_sem.at[k],
            recv_sem=recv_sem.at[k],
            device_id={"member": target},
            device_id_type=MESH_ID,
        )

    def start(k, carry):
        copy(k).start()
        return carry

    def finish(k, carry):
        copy(k).wait()
        return carry

    lax.fori_loop(1, n, start, 0)
    dst[me] = src[me]
    lax.fori_loop(1, n, finish, 0)


def pick_rows(n, source_ref, held, picked):
    def pick(i, carry):
        picked[i] = held[source_ref[i]]
        return carry

    lax.fori_loop(0, n, pick, 0)


def exploit_kernel(n, source_ref, send_ref, out_ref, held, picked, send1, recv1, send2, recv2):
    me = lax.axis_index("member")
    enter(n, me)
    transpose(n, me, send_ref, held, send1, recv1)
    pick_rows(n, source_ref, held, picked)
    transpose(n, me, picked, out_ref, send2, recv2)


def gather_kernel(n, source_ref, *refs):
    parts, (out_ref, flat, held, send1, recv1) = refs[:-5], refs[-5:]
    me = lax.axis_index("member")
    lanes = flat.shape[1]
    chunk = held.shape[1]
    offset = 0
    for part in parts:
        rows, cols = part.shape
        for block in range(cols // lanes):
            flat[pl.ds(offset, rows), :] = part[:, pl.ds(block * lanes, lanes)].astype(flat.dtype)
            offset += rows
    enter(n, me)

    def copy(k):
        target = lax.rem(me + k, n)
        return pltpu.make_async_remote_copy(
            src_ref=flat.at[pl.ds(pl.multiple_of(target * chunk, 16), chunk)],
            dst_ref=held.at[me],
            send_sem=send1.at[k],
            recv_sem=recv1.at[k],
            device_id={"member": target},
            device_id_type=MESH_ID,
        )

    def start(k, carry):
        copy(k).start()
        return carry

    def finish(k, carry):
        copy(k).wait()
        return carry

    lax.fori_loop(1, n, start, 0)
    held[me] = flat[pl.ds(pl.multiple_of(me * chunk, 16), chunk)]
    lax.fori_loop(1, n, finish, 0)
    pick_rows(n, source_ref, held, out_ref)


def scatter_kernel(n, send_ref, out_ref, send1, recv1):
    me = lax.axis_index("member")
    enter(n, me)
    transpose(n, me, send_ref, out_ref, send1, recv1)


def block_gradients(tokens, labels_ref, up_weight, down_weight, classifier, batch_total, patches):
    tokens_n, features = tokens.shape
    hidden_units = up_weight.shape[1]
    classes = classifier.shape[1]
    images = tokens_n // patches
    token_rows = tokens.astype(jnp.float32)
    center = token_rows - jnp.mean(token_rows, axis=1, keepdims=True)
    normed = (center * lax.rsqrt(jnp.mean(center * center, axis=1, keepdims=True) + 1e-06)).astype(
        jnp.bfloat16
    )
    preact = jnp.dot(normed, up_weight, preferred_element_type=jnp.float32) * features ** (-0.5)
    activated = (0.5 * preact * (1.0 + lax.erf(preact * 0.7071067811865476))).astype(jnp.bfloat16)
    residual = token_rows + jnp.dot(
        activated, down_weight, preferred_element_type=jnp.float32
    ) * hidden_units ** (-0.5)
    out_center = residual - jnp.mean(residual, axis=1, keepdims=True)
    inverse = lax.rsqrt(jnp.mean(out_center * out_center, axis=1, keepdims=True) + 1e-06)
    out_normed = out_center * inverse
    image_of_row = lax.broadcasted_iota(jnp.int32, (tokens_n, 1), 0) // patches
    pooled = jnp.concatenate(
        [
            jnp.sum(jnp.where(image_of_row == i, out_normed, 0.0), axis=0, keepdims=True)
            for i in range(images)
        ],
        axis=0,
    ) / patches
    pooled = pooled.astype(jnp.bfloat16)
    logits = jnp.dot(pooled, classifier, preferred_element_type=jnp.float32)
    powered = jnp.exp(logits)
    softmax_out = powered / jnp.sum(powered, axis=1, keepdims=True)
    row = lax.broadcasted_iota(jnp.int32, (images, classes), 0)
    column = lax.broadcasted_iota(jnp.int32, (images, classes), 1)
    label = jnp.zeros((images, classes), jnp.int32)
    for i in range(images):
        label = jnp.where(row == i, labels_ref[i], label)
    onehot = (column == label).astype(jnp.float32)
    logit_delta = ((softmax_out - onehot) / batch_total).astype(jnp.bfloat16)
    pool_delta = (
        lax.dot_general(
            logit_delta, classifier, (((1,), (1,)), ((), ())), preferred_element_type=jnp.float32
        )
        / patches
    )
    token_delta = jnp.zeros((tokens_n, features), jnp.float32)
    for i in range(images):
        token_delta = jnp.where(image_of_row == i, pool_delta[i:i + 1, :], token_delta)
    residual_delta = inverse * (
        token_delta
        - jnp.mean(token_delta, axis=1, keepdims=True)
        - out_normed * jnp.mean(token_delta * out_normed, axis=1, keepdims=True)
    )
    residual_delta = residual_delta.astype(jnp.bfloat16)
    down_scale = hidden_units ** (-0.5)
    down_gradient = (
        lax.dot_general(
            activated, residual_delta, (((0,), (0,)), ((), ())), preferred_element_type=jnp.float32
        )
        * down_scale
    )
    hidden_delta = (
        lax.dot_general(
            residual_delta, down_weight, (((1,), (1,)), ((), ())), preferred_element_type=jnp.float32
        )
        * down_scale
    )
    derivative = (
        0.5 * (1.0 + lax.erf(preact * 0.7071067811865476))
        + preact * jnp.exp(-0.5 * preact * preact) * 0.3989422804014327
    )
    preact_delta = (hidden_delta * derivative).astype(jnp.bfloat16)
    up_gradient = lax.dot_general(
        normed, preact_delta, (((0,), (0,)), ((), ())), preferred_element_type=jnp.float32
    ) * features ** (-0.5)
    return up_gradient, down_gradient


def scatter_compute_kernel(
    n, batch_total, patches, labels_ref, send_ref, tokens_ref, up_ref, down_ref, classifier_ref,
    up_share_ref, down_share_ref, up_first_ref, down_first_ref, up_second_ref, down_second_ref,
    flat, up_term, down_term, up_near, down_near, up_part, down_part, up_far, down_far,
    send_sem, recv_sem, near_send, near_recv, far_send, far_recv,
):
    me = lax.axis_index("member")
    shard = lax.axis_index("dp")
    core = shard % 2
    chip = shard // 2
    partner = chip * 2 + (1 - core)
    across = (1 - chip) * 2 + core
    diagonal = (1 - chip) * 2 + (1 - core)

    barrier = pltpu.get_barrier_semaphore()

    def greet(k, carry):
        pl.semaphore_signal(
            barrier, inc=1, device_id={"member": lax.rem(me + k, n)}, device_id_type=MESH_ID
        )
        return carry

    lax.fori_loop(1, n, greet, 0)
    for peer in (partner, across, diagonal):
        pl.semaphore_signal(barrier, inc=1, device_id={"dp": peer}, device_id_type=MESH_ID)
    pl.semaphore_wait(barrier, n - 1 + 3)

    chunk = send_ref.shape[1]

    def copy(k):
        target = lax.rem(me + k, n)
        return pltpu.make_async_remote_copy(
            src_ref=send_ref.at[target],
            dst_ref=flat.at[pl.ds(pl.multiple_of(me * chunk, 16), chunk)],
            send_sem=send_sem.at[k],
            recv_sem=recv_sem.at[k],
            device_id={"member": target},
            device_id_type=MESH_ID,
        )

    def start(k, carry):
        copy(k).start()
        return carry

    def finish(k, carry):
        copy(k).wait()
        return carry

    lax.fori_loop(1, n, start, 0)
    flat[pl.ds(pl.multiple_of(me * chunk, 16), chunk)] = send_ref[me]
    up_gradient, down_gradient = block_gradients(
        tokens_ref[...], labels_ref, up_ref[...], down_ref[...], classifier_ref[...],
        batch_total, patches,
    )
    up_term[...] = up_gradient.astype(jnp.bfloat16)
    down_term[...] = down_gradient.astype(jnp.bfloat16)

    def rows(term, index):
        size = term.shape[0] // 4
        return term.at[pl.ds(pl.multiple_of(index * size, size), size)]

    near = []
    slot = 0
    for term, near_buf in ((up_term, up_near), (down_term, down_near)):
        for which, index in ((0, diagonal), (1, partner)):
            near.append(
                pltpu.make_async_remote_copy(
                    src_ref=rows(term, index),
                    dst_ref=near_buf.at[which],
                    send_sem=near_send.at[slot],
                    recv_sem=near_recv.at[slot],
                    device_id={"dp": partner},
                    device_id_type=MESH_ID,
                )
            )
            slot += 1
    for item in near:
        item.start()
    for item in near:
        item.wait()

    far = []
    slot = 0
    for term, near_buf, part, far_buf in (
        (up_term, up_near, up_part, up_far),
        (down_term, down_near, down_part, down_far),
    ):
        part[...] = (
            rows(term, across)[...].astype(jnp.float32) + near_buf[0].astype(jnp.float32)
        ).astype(jnp.bfloat16)
        far.append(
            pltpu.make_async_remote_copy(
                src_ref=part,
                dst_ref=far_buf,
                send_sem=far_send.at[slot],
                recv_sem=far_recv.at[slot],
                device_id={"dp": across},
                device_id_type=MESH_ID,
            )
        )
        slot += 1
    for item in far:
        item.start()
    for item in far:
        item.wait()

    for term, near_buf, far_buf, share in (
        (up_term, up_near, up_far, up_share_ref),
        (down_term, down_near, down_far, down_share_ref),
    ):
        share[...] = (
            rows(term, shard)[...].astype(jnp.float32)
            + near_buf[1].astype(jnp.float32)
            + far_buf[...].astype(jnp.float32)
        )
    lax.fori_loop(1, n, finish, 0)
    lanes = flat.shape[1]
    offset = 0
    for part in (up_first_ref, down_first_ref, up_second_ref, down_second_ref):
        rows, cols = part.shape
        for block in range(cols // lanes):
            part[:, pl.ds(block * lanes, lanes)] = flat[pl.ds(offset, rows), :]
            offset += rows


def scatter_with_gradients(picked, tokens, labels, up_full, down_full, classifier, batch_total,
                           kernel_id):
    n = picked.shape[0]
    images, patches, features = tokens.shape
    vmem = pl.BlockSpec(memory_space=pltpu.VMEM)
    moved = picked.size * picked.dtype.itemsize
    flops = 12 * images * patches * features * up_full.shape[1]
    up_rows = (up_full.shape[0] // 4, up_full.shape[1])
    down_rows = (down_full.shape[0] // 4, down_full.shape[1])
    bf16 = jnp.bfloat16
    return pl.pallas_call(
        functools.partial(scatter_compute_kernel, n, batch_total, patches),
        out_shape=(
            jax.ShapeDtypeStruct(up_rows, jnp.float32),
            jax.ShapeDtypeStruct(down_rows, jnp.float32),
        ) + tuple(jax.ShapeDtypeStruct(shape, bf16) for shape in (up_rows, down_rows) * 2),
        in_specs=[pl.BlockSpec(memory_space=pltpu.SMEM)] + [vmem] * 5,
        out_specs=(vmem,) * 6,
        scratch_shapes=[
            pltpu.VMEM((picked.shape[0] * picked.shape[1], picked.shape[2]), bf16),
            pltpu.VMEM(up_full.shape, bf16),
            pltpu.VMEM(down_full.shape, bf16),
            pltpu.VMEM((2,) + up_rows, bf16),
            pltpu.VMEM((2,) + down_rows, bf16),
            pltpu.VMEM(up_rows, bf16),
            pltpu.VMEM(down_rows, bf16),
            pltpu.VMEM(up_rows, bf16),
            pltpu.VMEM(down_rows, bf16),
            pltpu.SemaphoreType.DMA((n,)),
            pltpu.SemaphoreType.DMA((n,)),
            pltpu.SemaphoreType.DMA((4,)),
            pltpu.SemaphoreType.DMA((4,)),
            pltpu.SemaphoreType.DMA((2,)),
            pltpu.SemaphoreType.DMA((2,)),
        ],
        compiler_params=pltpu.CompilerParams(
            collective_id=kernel_id, has_side_effects=True, vmem_limit_bytes=63 * 1024 * 1024
        ),
        cost_estimate=pl.CostEstimate(flops=flops, transcendentals=0, bytes_accessed=moved * 20),
    )(labels, picked, tokens.reshape(images * patches, features), up_full, down_full, classifier)


def member_call(body, packed, operands, scratch, kernel_id):
    n, rows, lanes = packed.shape
    moved = packed.size * packed.dtype.itemsize
    smem = [pl.BlockSpec(memory_space=pltpu.SMEM)] * (len(operands) - 1)
    return pl.pallas_call(
        functools.partial(body, n),
        out_shape=jax.ShapeDtypeStruct(packed.shape, packed.dtype),
        in_specs=smem + [pl.BlockSpec(memory_space=pltpu.VMEM)],
        out_specs=pl.BlockSpec(memory_space=pltpu.VMEM),
        scratch_shapes=scratch,
        compiler_params=pltpu.CompilerParams(
            collective_id=kernel_id, has_side_effects=True, vmem_limit_bytes=48 * 1024 * 1024
        ),
        cost_estimate=pl.CostEstimate(flops=0, transcendentals=0, bytes_accessed=moved * 20),
    )(*operands)


def exploit_transfer(packed, source, kernel_id):
    n, rows, lanes = packed.shape
    block = pltpu.VMEM((n, rows, lanes), packed.dtype)
    sems = [pltpu.SemaphoreType.DMA((n,))] * 4
    return member_call(exploit_kernel, packed, (source, packed), [block, block] + sems, kernel_id)


def exploit_gather(parts, source, members, kernel_id):
    lanes = 128
    total = sum(part.size for part in parts) // lanes
    shape = (members, total // members, lanes)
    vmem = pl.BlockSpec(memory_space=pltpu.VMEM)
    moved = total * lanes * 2
    return pl.pallas_call(
        functools.partial(gather_kernel, members),
        out_shape=jax.ShapeDtypeStruct(shape, jnp.bfloat16),
        in_specs=[pl.BlockSpec(memory_space=pltpu.SMEM)] + [vmem] * len(parts),
        out_specs=vmem,
        scratch_shapes=[
            pltpu.VMEM((total, lanes), jnp.bfloat16),
            pltpu.VMEM(shape, jnp.bfloat16),
            pltpu.SemaphoreType.DMA((members,)),
            pltpu.SemaphoreType.DMA((members,)),
        ],
        compiler_params=pltpu.CompilerParams(
            collective_id=kernel_id, has_side_effects=True, vmem_limit_bytes=48 * 1024 * 1024
        ),
        cost_estimate=pl.CostEstimate(flops=0, transcendentals=0, bytes_accessed=moved * 20),
    )(source, *parts)


def exploit_scatter(packed, kernel_id):
    n = packed.shape[0]
    sems = [pltpu.SemaphoreType.DMA((n,))] * 2
    return member_call(scatter_kernel, packed, (packed,), sems, kernel_id)


def lane_major(part, lanes):
    rows, cols = part.shape
    return part.reshape(rows, cols // lanes, lanes).transpose(1, 0, 2).reshape(-1, lanes)


def from_lane_major(flat, shape, lanes):
    rows, cols = shape
    return flat.reshape(cols // lanes, rows, lanes).transpose(1, 0, 2).reshape(rows, cols)


def exploit_rows(parts, source, members, kernel_id):
    lanes = 128
    rows = [part.size // (members * lanes) for part in parts]
    pad = -sum(rows) % 16
    pieces = [part.astype(jnp.bfloat16).reshape(members, -1, lanes) for part in parts]
    if pad:
        pieces.append(jnp.zeros((members, pad, lanes), jnp.bfloat16))
    back = exploit_transfer(jnp.concatenate(pieces, axis=1), source, kernel_id)
    out = []
    start = 0
    for part, count in zip(parts, rows):
        out.append(back[:, start:start + count].reshape(part.shape))
        start += count
    return out


def pack_tiles(parts, members):
    lanes = 128
    flat = jnp.concatenate([lane_major(part.astype(jnp.bfloat16), lanes) for part in parts])
    return flat.reshape(members, -1, flat.shape[-1])


def unpack_tiles(back, parts):
    lanes = back.shape[-1]
    back = back.reshape(-1, lanes)
    out = []
    start = 0
    for part in parts:
        count = part.size // lanes
        out.append(from_lane_major(back[start:start + count], part.shape, lanes))
        start += count
    return out


def per_device(
    tokens,
    labels,
    source,
    learn_rate,
    weight_decay,
    classifier,
    up_param,
    up_first,
    up_second,
    down_param,
    down_first,
    down_second,
):
    members = lax.axis_size("member")
    shards = lax.axis_size("dp")
    me = lax.axis_index("member")
    own = source[me] == me

    up_bf, down_bf = exploit_rows((up_param[0], down_param[0]), source, members, 0)
    up_full = lax.all_gather(up_bf, "dp", axis=0, tiled=True)
    down_full = lax.all_gather(down_bf, "dp", axis=0, tiled=True)
    moments = (up_first[0], down_first[0], up_second[0], down_second[0])
    picked = exploit_gather(moments, source, members, 1)
    up_full, down_full, picked = lax.optimization_barrier((up_full, down_full, picked))

    batch_total = tokens.shape[1] * shards
    up_share, down_share, up_mom, down_mom, up_var_bf, down_var_bf = scatter_with_gradients(
        picked, tokens[0], labels[0], up_full, down_full, classifier, batch_total, 2
    )

    up_now = jnp.where(own, up_param[0], up_bf.astype(jnp.float32))
    down_now = jnp.where(own, down_param[0], down_bf.astype(jnp.float32))
    up_var = jnp.where(own, up_second[0], up_var_bf.astype(jnp.float32))
    down_var = jnp.where(own, down_second[0], down_var_bf.astype(jnp.float32))

    rate_value = learn_rate[0]
    decay_value = weight_decay[0]
    up_new = adamw_step(up_now, up_mom, up_var, up_share, rate_value, decay_value)
    down_new = adamw_step(down_now, down_mom, down_var, down_share, rate_value, decay_value)
    return tuple(value[None] for value in up_new + down_new)


def solution(mesh):
    placed = (
        P("member", "dp", None, None),
        P("member", "dp"),
        P(),
        P("member"),
        P("member"),
        P(),
        P("member", "dp", None),
        P("member", "dp", None),
        P("member", "dp", None),
        P("member", "dp", None),
        P("member", "dp", None),
        P("member", "dp", None),
    )
    return jax.shard_map(
        per_device,
        mesh=mesh,
        in_specs=placed,
        out_specs=(P("member", "dp", None),) * 6,
        check_vma=False,
    )
```

```python
import functools

import jax
import jax.numpy as jnp
from jax import lax
from jax.experimental import pallas as pl
from jax.experimental.pallas import tpu as pltpu
from jax.sharding import PartitionSpec as P

MESH_ID = pl.DeviceIdType.MESH

STEP = 1000


def local_gradients(tokens, labels, up_weight, down_weight, classifier, batch_total):
    images, patches, features = tokens.shape
    hidden_units = up_weight.shape[1]
    token_rows = tokens.reshape(images * patches, features).astype(jnp.float32)
    center = token_rows - jnp.mean(token_rows, axis=1, keepdims=True)
    normed = (center * lax.rsqrt(jnp.mean(center * center, axis=1, keepdims=True) + 1e-06)).astype(
        jnp.bfloat16
    )
    preact = jnp.dot(normed, up_weight, preferred_element_type=jnp.float32) * features ** (-0.5)
    activated = (0.5 * preact * (1.0 + lax.erf(preact * 0.7071067811865476))).astype(jnp.bfloat16)
    residual = token_rows + jnp.dot(
        activated, down_weight, preferred_element_type=jnp.float32
    ) * hidden_units ** (-0.5)
    out_center = residual - jnp.mean(residual, axis=1, keepdims=True)
    inverse = lax.rsqrt(jnp.mean(out_center * out_center, axis=1, keepdims=True) + 1e-06)
    out_normed = out_center * inverse
    pooled = jnp.mean(out_normed.reshape(images, patches, features), axis=1).astype(jnp.bfloat16)
    logits = jnp.dot(pooled, classifier, preferred_element_type=jnp.float32)
    powered = jnp.exp(logits)
    softmax_out = powered / jnp.sum(powered, axis=1, keepdims=True)
    onehot = (labels[:, None] == jnp.arange(classifier.shape[1], dtype=jnp.int32)[None, :]).astype(
        jnp.float32
    )
    logit_delta = ((softmax_out - onehot) / batch_total).astype(jnp.bfloat16)
    pool_delta = (
        lax.dot_general(
            logit_delta, classifier, (((1,), (1,)), ((), ())), preferred_element_type=jnp.float32
        )
        / patches
    )
    token_delta = jnp.broadcast_to(pool_delta[:, None, :], (images, patches, features)).reshape(
        images * patches, features
    )
    residual_delta = inverse * (
        token_delta
        - jnp.mean(token_delta, axis=1, keepdims=True)
        - out_normed * jnp.mean(token_delta * out_normed, axis=1, keepdims=True)
    )
    residual_delta = residual_delta.astype(jnp.bfloat16)
    down_scale = hidden_units ** (-0.5)
    down_gradient = (
        lax.dot_general(
            activated, residual_delta, (((0,), (0,)), ((), ())), preferred_element_type=jnp.float32
        )
        * down_scale
    )
    hidden_delta = (
        lax.dot_general(
            residual_delta,
            down_weight,
            (((1,), (1,)), ((), ())),
            preferred_element_type=jnp.float32,
        )
        * down_scale
    )
    derivative = (
        0.5 * (1.0 + lax.erf(preact * 0.7071067811865476))
        + preact * jnp.exp(-0.5 * preact * preact) * 0.3989422804014327
    )
    preact_delta = (hidden_delta * derivative).astype(jnp.bfloat16)
    up_gradient = lax.dot_general(
        normed, preact_delta, (((0,), (0,)), ((), ())), preferred_element_type=jnp.float32
    ) * features ** (-0.5)
    return (up_gradient, down_gradient)


def adamw_step(param, first, second, gradient, rate_value, decay_value):
    moment = 0.9 * first.astype(jnp.float32) + 0.1 * gradient
    variance = 0.999 * second + 0.001 * gradient * gradient
    update = (
        moment / (1.0 - 0.9**STEP) / (jnp.sqrt(variance / (1.0 - 0.999**STEP)) + 1e-08)
        + decay_value * param
    )
    return (param - rate_value * update, moment.astype(jnp.bfloat16), variance)


def enter(n, me):
    barrier = pltpu.get_barrier_semaphore()

    def greet(k, carry):
        pl.semaphore_signal(
            barrier, inc=1, device_id={"member": lax.rem(me + k, n)}, device_id_type=MESH_ID
        )
        return carry

    lax.fori_loop(1, n, greet, 0)
    pl.semaphore_wait(barrier, n - 1)


def transpose(n, me, src, dst, send_sem, recv_sem):
    def copy(k):
        target = lax.rem(me + k, n)
        return pltpu.make_async_remote_copy(
            src_ref=src.at[target],
            dst_ref=dst.at[me],
            send_sem=send_sem.at[k],
            recv_sem=recv_sem.at[k],
            device_id={"member": target},
            device_id_type=MESH_ID,
        )

    def start(k, carry):
        copy(k).start()
        return carry

    def finish(k, carry):
        copy(k).wait()
        return carry

    lax.fori_loop(1, n, start, 0)
    dst[me] = src[me]
    lax.fori_loop(1, n, finish, 0)


def pick_rows(n, source_ref, held, picked):
    def pick(i, carry):
        picked[i] = held[source_ref[i]]
        return carry

    lax.fori_loop(0, n, pick, 0)


def exploit_kernel(n, source_ref, send_ref, out_ref, held, picked, send1, recv1, send2, recv2):
    me = lax.axis_index("member")
    enter(n, me)
    transpose(n, me, send_ref, held, send1, recv1)
    pick_rows(n, source_ref, held, picked)
    transpose(n, me, picked, out_ref, send2, recv2)


def gather_kernel(n, source_ref, up_ref, down_ref, *refs):
    parts = refs[:-13]
    (out_ref, up_full, down_full, flat, held, send1, recv1,
     near_send, near_recv, far_send, far_recv, fwd_send, fwd_recv) = refs[-13:]
    me = lax.axis_index("member")
    shard = lax.axis_index("dp")
    core = shard % 2
    chip = shard // 2
    partner = chip * 2 + (1 - core)
    across = (1 - chip) * 2 + core
    lanes = flat.shape[1]
    chunk = held.shape[1]
    offset = 0
    for part in parts:
        rows, cols = part.shape
        for block in range(cols // lanes):
            flat[pl.ds(offset, rows), :] = part[:, pl.ds(block * lanes, lanes)].astype(flat.dtype)
            offset += rows

    barrier = pltpu.get_barrier_semaphore()

    def greet(k, carry):
        pl.semaphore_signal(
            barrier, inc=1, device_id={"member": lax.rem(me + k, n)}, device_id_type=MESH_ID
        )
        return carry

    lax.fori_loop(1, n, greet, 0)
    for peer in (partner, across):
        pl.semaphore_signal(barrier, inc=1, device_id={"dp": peer}, device_id_type=MESH_ID)
    pl.semaphore_wait(barrier, n - 1 + 2)

    def rows_of(full, index):
        size = full.shape[0] // 4
        return full.at[pl.ds(pl.multiple_of(index * size, size), size)]

    def dp_copy(src, dst, send, recv, slot, peer):
        return pltpu.make_async_remote_copy(
            src_ref=src, dst_ref=dst, send_sem=send.at[slot], recv_sem=recv.at[slot],
            device_id={"dp": peer}, device_id_type=MESH_ID,
        )

    shares = ((up_ref, up_full), (down_ref, down_full))
    far = [dp_copy(share, rows_of(full, shard), far_send, far_recv, slot, across)
           for slot, (share, full) in enumerate(shares)]
    near = [dp_copy(share, rows_of(full, shard), near_send, near_recv, slot, partner)
            for slot, (share, full) in enumerate(shares)]
    for item in far + near:
        item.start()

    def copy(k):
        target = lax.rem(me + k, n)
        return pltpu.make_async_remote_copy(
            src_ref=flat.at[pl.ds(pl.multiple_of(target * chunk, 16), chunk)],
            dst_ref=held.at[me],
            send_sem=send1.at[k],
            recv_sem=recv1.at[k],
            device_id={"member": target},
            device_id_type=MESH_ID,
        )

    def start(k, carry):
        copy(k).start()
        return carry

    def finish(k, carry):
        copy(k).wait()
        return carry

    lax.fori_loop(1, n, start, 0)
    held[me] = flat[pl.ds(pl.multiple_of(me * chunk, 16), chunk)]
    for share, full in shares:
        rows_of(full, shard)[...] = share[...]
    for item in far:
        item.wait()
    forward = [dp_copy(rows_of(full, across), rows_of(full, across), fwd_send, fwd_recv, slot,
                       partner)
               for slot, (share, full) in enumerate(shares)]
    for item in forward:
        item.start()
    lax.fori_loop(1, n, finish, 0)
    pick_rows(n, source_ref, held, out_ref)
    for item in near + forward:
        item.wait()


def scatter_kernel(n, send_ref, out_ref, send1, recv1):
    me = lax.axis_index("member")
    enter(n, me)
    transpose(n, me, send_ref, out_ref, send1, recv1)


def block_gradients(tokens, labels_ref, up_weight, down_weight, classifier, batch_total, patches):
    tokens_n, features = tokens.shape
    hidden_units = up_weight.shape[1]
    classes = classifier.shape[1]
    images = tokens_n // patches
    token_rows = tokens.astype(jnp.float32)
    center = token_rows - jnp.mean(token_rows, axis=1, keepdims=True)
    normed = (center * lax.rsqrt(jnp.mean(center * center, axis=1, keepdims=True) + 1e-06)).astype(
        jnp.bfloat16
    )
    preact = jnp.dot(normed, up_weight, preferred_element_type=jnp.float32) * features ** (-0.5)
    activated = (0.5 * preact * (1.0 + lax.erf(preact * 0.7071067811865476))).astype(jnp.bfloat16)
    residual = token_rows + jnp.dot(
        activated, down_weight, preferred_element_type=jnp.float32
    ) * hidden_units ** (-0.5)
    out_center = residual - jnp.mean(residual, axis=1, keepdims=True)
    inverse = lax.rsqrt(jnp.mean(out_center * out_center, axis=1, keepdims=True) + 1e-06)
    out_normed = out_center * inverse
    image_of_row = lax.broadcasted_iota(jnp.int32, (tokens_n, 1), 0) // patches
    pooled = jnp.concatenate(
        [
            jnp.sum(jnp.where(image_of_row == i, out_normed, 0.0), axis=0, keepdims=True)
            for i in range(images)
        ],
        axis=0,
    ) / patches
    pooled = pooled.astype(jnp.bfloat16)
    logits = jnp.dot(pooled, classifier, preferred_element_type=jnp.float32)
    powered = jnp.exp(logits)
    softmax_out = powered / jnp.sum(powered, axis=1, keepdims=True)
    row = lax.broadcasted_iota(jnp.int32, (images, classes), 0)
    column = lax.broadcasted_iota(jnp.int32, (images, classes), 1)
    label = jnp.zeros((images, classes), jnp.int32)
    for i in range(images):
        label = jnp.where(row == i, labels_ref[i], label)
    onehot = (column == label).astype(jnp.float32)
    logit_delta = ((softmax_out - onehot) / batch_total).astype(jnp.bfloat16)
    pool_delta = (
        lax.dot_general(
            logit_delta, classifier, (((1,), (1,)), ((), ())), preferred_element_type=jnp.float32
        )
        / patches
    )
    token_delta = jnp.zeros((tokens_n, features), jnp.float32)
    for i in range(images):
        token_delta = jnp.where(image_of_row == i, pool_delta[i:i + 1, :], token_delta)
    residual_delta = inverse * (
        token_delta
        - jnp.mean(token_delta, axis=1, keepdims=True)
        - out_normed * jnp.mean(token_delta * out_normed, axis=1, keepdims=True)
    )
    residual_delta = residual_delta.astype(jnp.bfloat16)
    down_scale = hidden_units ** (-0.5)
    down_gradient = (
        lax.dot_general(
            activated, residual_delta, (((0,), (0,)), ((), ())), preferred_element_type=jnp.float32
        )
        * down_scale
    )
    hidden_delta = (
        lax.dot_general(
            residual_delta, down_weight, (((1,), (1,)), ((), ())), preferred_element_type=jnp.float32
        )
        * down_scale
    )
    derivative = (
        0.5 * (1.0 + lax.erf(preact * 0.7071067811865476))
        + preact * jnp.exp(-0.5 * preact * preact) * 0.3989422804014327
    )
    preact_delta = (hidden_delta * derivative).astype(jnp.bfloat16)
    up_gradient = lax.dot_general(
        normed, preact_delta, (((0,), (0,)), ((), ())), preferred_element_type=jnp.float32
    ) * features ** (-0.5)
    return up_gradient, down_gradient


def scatter_compute_kernel(
    n, batch_total, patches, labels_ref, send_ref, tokens_ref, up_ref, down_ref, classifier_ref,
    up_share_ref, down_share_ref, up_first_ref, down_first_ref, up_second_ref, down_second_ref,
    flat, up_term, down_term, up_near, down_near, up_part, down_part, up_far, down_far,
    send_sem, recv_sem, near_send, near_recv, far_send, far_recv,
):
    me = lax.axis_index("member")
    shard = lax.axis_index("dp")
    core = shard % 2
    chip = shard // 2
    partner = chip * 2 + (1 - core)
    across = (1 - chip) * 2 + core
    diagonal = (1 - chip) * 2 + (1 - core)

    barrier = pltpu.get_barrier_semaphore()

    def greet(k, carry):
        pl.semaphore_signal(
            barrier, inc=1, device_id={"member": lax.rem(me + k, n)}, device_id_type=MESH_ID
        )
        return carry

    lax.fori_loop(1, n, greet, 0)
    for peer in (partner, across, diagonal):
        pl.semaphore_signal(barrier, inc=1, device_id={"dp": peer}, device_id_type=MESH_ID)
    pl.semaphore_wait(barrier, n - 1 + 3)

    chunk = send_ref.shape[1]

    def copy(k):
        target = lax.rem(me + k, n)
        return pltpu.make_async_remote_copy(
            src_ref=send_ref.at[target],
            dst_ref=flat.at[pl.ds(pl.multiple_of(me * chunk, 16), chunk)],
            send_sem=send_sem.at[k],
            recv_sem=recv_sem.at[k],
            device_id={"member": target},
            device_id_type=MESH_ID,
        )

    def start(k, carry):
        copy(k).start()
        return carry

    def finish(k, carry):
        copy(k).wait()
        return carry

    lax.fori_loop(1, n, start, 0)
    flat[pl.ds(pl.multiple_of(me * chunk, 16), chunk)] = send_ref[me]
    up_gradient, down_gradient = block_gradients(
        tokens_ref[...], labels_ref, up_ref[...], down_ref[...], classifier_ref[...],
        batch_total, patches,
    )
    up_term[...] = up_gradient.astype(jnp.bfloat16)
    down_term[...] = down_gradient.astype(jnp.bfloat16)

    def rows(term, index):
        size = term.shape[0] // 4
        return term.at[pl.ds(pl.multiple_of(index * size, size), size)]

    near = []
    slot = 0
    for term, near_buf in ((up_term, up_near), (down_term, down_near)):
        for which, index in ((0, diagonal), (1, partner)):
            near.append(
                pltpu.make_async_remote_copy(
                    src_ref=rows(term, index),
                    dst_ref=near_buf.at[which],
                    send_sem=near_send.at[slot],
                    recv_sem=near_recv.at[slot],
                    device_id={"dp": partner},
                    device_id_type=MESH_ID,
                )
            )
            slot += 1
    for item in near:
        item.start()
    for item in near:
        item.wait()

    far = []
    slot = 0
    for term, near_buf, part, far_buf in (
        (up_term, up_near, up_part, up_far),
        (down_term, down_near, down_part, down_far),
    ):
        part[...] = (
            rows(term, across)[...].astype(jnp.float32) + near_buf[0].astype(jnp.float32)
        ).astype(jnp.bfloat16)
        far.append(
            pltpu.make_async_remote_copy(
                src_ref=part,
                dst_ref=far_buf,
                send_sem=far_send.at[slot],
                recv_sem=far_recv.at[slot],
                device_id={"dp": across},
                device_id_type=MESH_ID,
            )
        )
        slot += 1
    for item in far:
        item.start()
    for item in far:
        item.wait()

    for term, near_buf, far_buf, share in (
        (up_term, up_near, up_far, up_share_ref),
        (down_term, down_near, down_far, down_share_ref),
    ):
        share[...] = (
            rows(term, shard)[...].astype(jnp.float32)
            + near_buf[1].astype(jnp.float32)
            + far_buf[...].astype(jnp.float32)
        )
    lax.fori_loop(1, n, finish, 0)
    lanes = flat.shape[1]
    offset = 0
    for part in (up_first_ref, down_first_ref, up_second_ref, down_second_ref):
        rows, cols = part.shape
        for block in range(cols // lanes):
            part[:, pl.ds(block * lanes, lanes)] = flat[pl.ds(offset, rows), :]
            offset += rows


def scatter_with_gradients(picked, tokens, labels, up_full, down_full, classifier, batch_total,
                           kernel_id):
    n = picked.shape[0]
    images, patches, features = tokens.shape
    vmem = pl.BlockSpec(memory_space=pltpu.VMEM)
    moved = picked.size * picked.dtype.itemsize
    flops = 12 * images * patches * features * up_full.shape[1]
    up_rows = (up_full.shape[0] // 4, up_full.shape[1])
    down_rows = (down_full.shape[0] // 4, down_full.shape[1])
    bf16 = jnp.bfloat16
    return pl.pallas_call(
        functools.partial(scatter_compute_kernel, n, batch_total, patches),
        out_shape=(
            jax.ShapeDtypeStruct(up_rows, jnp.float32),
            jax.ShapeDtypeStruct(down_rows, jnp.float32),
        ) + tuple(jax.ShapeDtypeStruct(shape, bf16) for shape in (up_rows, down_rows) * 2),
        in_specs=[pl.BlockSpec(memory_space=pltpu.SMEM)] + [vmem] * 5,
        out_specs=(vmem,) * 6,
        scratch_shapes=[
            pltpu.VMEM((picked.shape[0] * picked.shape[1], picked.shape[2]), bf16),
            pltpu.VMEM(up_full.shape, bf16),
            pltpu.VMEM(down_full.shape, bf16),
            pltpu.VMEM((2,) + up_rows, bf16),
            pltpu.VMEM((2,) + down_rows, bf16),
            pltpu.VMEM(up_rows, bf16),
            pltpu.VMEM(down_rows, bf16),
            pltpu.VMEM(up_rows, bf16),
            pltpu.VMEM(down_rows, bf16),
            pltpu.SemaphoreType.DMA((n,)),
            pltpu.SemaphoreType.DMA((n,)),
            pltpu.SemaphoreType.DMA((4,)),
            pltpu.SemaphoreType.DMA((4,)),
            pltpu.SemaphoreType.DMA((2,)),
            pltpu.SemaphoreType.DMA((2,)),
        ],
        compiler_params=pltpu.CompilerParams(
            collective_id=kernel_id, has_side_effects=True, vmem_limit_bytes=63 * 1024 * 1024
        ),
        cost_estimate=pl.CostEstimate(flops=flops, transcendentals=0, bytes_accessed=moved * 20),
    )(labels, picked, tokens.reshape(images * patches, features), up_full, down_full, classifier)


def member_call(body, packed, operands, scratch, kernel_id):
    n, rows, lanes = packed.shape
    moved = packed.size * packed.dtype.itemsize
    smem = [pl.BlockSpec(memory_space=pltpu.SMEM)] * (len(operands) - 1)
    return pl.pallas_call(
        functools.partial(body, n),
        out_shape=jax.ShapeDtypeStruct(packed.shape, packed.dtype),
        in_specs=smem + [pl.BlockSpec(memory_space=pltpu.VMEM)],
        out_specs=pl.BlockSpec(memory_space=pltpu.VMEM),
        scratch_shapes=scratch,
        compiler_params=pltpu.CompilerParams(
            collective_id=kernel_id, has_side_effects=True, vmem_limit_bytes=48 * 1024 * 1024
        ),
        cost_estimate=pl.CostEstimate(flops=0, transcendentals=0, bytes_accessed=moved * 20),
    )(*operands)


def exploit_transfer(packed, source, kernel_id):
    n, rows, lanes = packed.shape
    block = pltpu.VMEM((n, rows, lanes), packed.dtype)
    sems = [pltpu.SemaphoreType.DMA((n,))] * 4
    return member_call(exploit_kernel, packed, (source, packed), [block, block] + sems, kernel_id)


def exploit_gather(parts, shares, source, members, shards, kernel_id):
    lanes = 128
    total = sum(part.size for part in parts) // lanes
    shape = (members, total // members, lanes)
    vmem = pl.BlockSpec(memory_space=pltpu.VMEM)
    moved = total * lanes * 2
    fulls = [jax.ShapeDtypeStruct((share.shape[0] * shards, share.shape[1]), share.dtype)
             for share in shares]
    sems = [pltpu.SemaphoreType.DMA((len(shares),))] * 6
    return pl.pallas_call(
        functools.partial(gather_kernel, members),
        out_shape=(jax.ShapeDtypeStruct(shape, jnp.bfloat16), *fulls),
        in_specs=[pl.BlockSpec(memory_space=pltpu.SMEM)] + [vmem] * (len(shares) + len(parts)),
        out_specs=(vmem,) * 3,
        scratch_shapes=[
            pltpu.VMEM((total, lanes), jnp.bfloat16),
            pltpu.VMEM(shape, jnp.bfloat16),
            pltpu.SemaphoreType.DMA((members,)),
            pltpu.SemaphoreType.DMA((members,)),
        ] + sems,
        compiler_params=pltpu.CompilerParams(
            collective_id=kernel_id, has_side_effects=True, vmem_limit_bytes=48 * 1024 * 1024
        ),
        cost_estimate=pl.CostEstimate(flops=0, transcendentals=0, bytes_accessed=moved * 20),
    )(source, *shares, *parts)


def exploit_scatter(packed, kernel_id):
    n = packed.shape[0]
    sems = [pltpu.SemaphoreType.DMA((n,))] * 2
    return member_call(scatter_kernel, packed, (packed,), sems, kernel_id)


def lane_major(part, lanes):
    rows, cols = part.shape
    return part.reshape(rows, cols // lanes, lanes).transpose(1, 0, 2).reshape(-1, lanes)


def from_lane_major(flat, shape, lanes):
    rows, cols = shape
    return flat.reshape(cols // lanes, rows, lanes).transpose(1, 0, 2).reshape(rows, cols)


def exploit_rows(parts, source, members, kernel_id):
    lanes = 128
    rows = [part.size // (members * lanes) for part in parts]
    pad = -sum(rows) % 16
    pieces = [part.astype(jnp.bfloat16).reshape(members, -1, lanes) for part in parts]
    if pad:
        pieces.append(jnp.zeros((members, pad, lanes), jnp.bfloat16))
    back = exploit_transfer(jnp.concatenate(pieces, axis=1), source, kernel_id)
    out = []
    start = 0
    for part, count in zip(parts, rows):
        out.append(back[:, start:start + count].reshape(part.shape))
        start += count
    return out


def pack_tiles(parts, members):
    lanes = 128
    flat = jnp.concatenate([lane_major(part.astype(jnp.bfloat16), lanes) for part in parts])
    return flat.reshape(members, -1, flat.shape[-1])


def unpack_tiles(back, parts):
    lanes = back.shape[-1]
    back = back.reshape(-1, lanes)
    out = []
    start = 0
    for part in parts:
        count = part.size // lanes
        out.append(from_lane_major(back[start:start + count], part.shape, lanes))
        start += count
    return out


def per_device(
    tokens,
    labels,
    source,
    learn_rate,
    weight_decay,
    classifier,
    up_param,
    up_first,
    up_second,
    down_param,
    down_first,
    down_second,
):
    members = lax.axis_size("member")
    shards = lax.axis_size("dp")
    me = lax.axis_index("member")
    own = source[me] == me

    up_bf, down_bf = exploit_rows((up_param[0], down_param[0]), source, members, 0)
    moments = (up_first[0], down_first[0], up_second[0], down_second[0])
    picked, up_full, down_full = exploit_gather(
        moments, (up_bf, down_bf), source, members, shards, 1
    )

    batch_total = tokens.shape[1] * shards
    up_share, down_share, up_mom, down_mom, up_var_bf, down_var_bf = scatter_with_gradients(
        picked, tokens[0], labels[0], up_full, down_full, classifier, batch_total, 2
    )

    up_now = jnp.where(own, up_param[0], up_bf.astype(jnp.float32))
    down_now = jnp.where(own, down_param[0], down_bf.astype(jnp.float32))
    up_var = jnp.where(own, up_second[0], up_var_bf.astype(jnp.float32))
    down_var = jnp.where(own, down_second[0], down_var_bf.astype(jnp.float32))

    rate_value = learn_rate[0]
    decay_value = weight_decay[0]
    up_new = adamw_step(up_now, up_mom, up_var, up_share, rate_value, decay_value)
    down_new = adamw_step(down_now, down_mom, down_var, down_share, rate_value, decay_value)
    return tuple(value[None] for value in up_new + down_new)


def solution(mesh):
    placed = (
        P("member", "dp", None, None),
        P("member", "dp"),
        P(),
        P("member"),
        P("member"),
        P(),
        P("member", "dp", None),
        P("member", "dp", None),
        P("member", "dp", None),
        P("member", "dp", None),
        P("member", "dp", None),
        P("member", "dp", None),
    )
    return jax.shard_map(
        per_device,
        mesh=mesh,
        in_specs=placed,
        out_specs=(P("member", "dp", None),) * 6,
        check_vma=False,
    )
```

```python
import functools

import jax
import jax.numpy as jnp
from jax import lax
from jax.experimental import pallas as pl
from jax.experimental.pallas import tpu as pltpu
from jax.sharding import PartitionSpec as P

MESH_ID = pl.DeviceIdType.MESH

STEP = 1000


def local_gradients(tokens, labels, up_weight, down_weight, classifier, batch_total):
    images, patches, features = tokens.shape
    hidden_units = up_weight.shape[1]
    token_rows = tokens.reshape(images * patches, features).astype(jnp.float32)
    center = token_rows - jnp.mean(token_rows, axis=1, keepdims=True)
    normed = (center * lax.rsqrt(jnp.mean(center * center, axis=1, keepdims=True) + 1e-06)).astype(
        jnp.bfloat16
    )
    preact = jnp.dot(normed, up_weight, preferred_element_type=jnp.float32) * features ** (-0.5)
    activated = (0.5 * preact * (1.0 + lax.erf(preact * 0.7071067811865476))).astype(jnp.bfloat16)
    residual = token_rows + jnp.dot(
        activated, down_weight, preferred_element_type=jnp.float32
    ) * hidden_units ** (-0.5)
    out_center = residual - jnp.mean(residual, axis=1, keepdims=True)
    inverse = lax.rsqrt(jnp.mean(out_center * out_center, axis=1, keepdims=True) + 1e-06)
    out_normed = out_center * inverse
    pooled = jnp.mean(out_normed.reshape(images, patches, features), axis=1).astype(jnp.bfloat16)
    logits = jnp.dot(pooled, classifier, preferred_element_type=jnp.float32)
    powered = jnp.exp(logits)
    softmax_out = powered / jnp.sum(powered, axis=1, keepdims=True)
    onehot = (labels[:, None] == jnp.arange(classifier.shape[1], dtype=jnp.int32)[None, :]).astype(
        jnp.float32
    )
    logit_delta = ((softmax_out - onehot) / batch_total).astype(jnp.bfloat16)
    pool_delta = (
        lax.dot_general(
            logit_delta, classifier, (((1,), (1,)), ((), ())), preferred_element_type=jnp.float32
        )
        / patches
    )
    token_delta = jnp.broadcast_to(pool_delta[:, None, :], (images, patches, features)).reshape(
        images * patches, features
    )
    residual_delta = inverse * (
        token_delta
        - jnp.mean(token_delta, axis=1, keepdims=True)
        - out_normed * jnp.mean(token_delta * out_normed, axis=1, keepdims=True)
    )
    residual_delta = residual_delta.astype(jnp.bfloat16)
    down_scale = hidden_units ** (-0.5)
    down_gradient = (
        lax.dot_general(
            activated, residual_delta, (((0,), (0,)), ((), ())), preferred_element_type=jnp.float32
        )
        * down_scale
    )
    hidden_delta = (
        lax.dot_general(
            residual_delta,
            down_weight,
            (((1,), (1,)), ((), ())),
            preferred_element_type=jnp.float32,
        )
        * down_scale
    )
    derivative = (
        0.5 * (1.0 + lax.erf(preact * 0.7071067811865476))
        + preact * jnp.exp(-0.5 * preact * preact) * 0.3989422804014327
    )
    preact_delta = (hidden_delta * derivative).astype(jnp.bfloat16)
    up_gradient = lax.dot_general(
        normed, preact_delta, (((0,), (0,)), ((), ())), preferred_element_type=jnp.float32
    ) * features ** (-0.5)
    return (up_gradient, down_gradient)


def adamw_step(param, first, second, gradient, rate_value, decay_value):
    moment = 0.9 * first.astype(jnp.float32) + 0.1 * gradient
    variance = 0.999 * second + 0.001 * gradient * gradient
    update = (
        moment / (1.0 - 0.9**STEP) / (jnp.sqrt(variance / (1.0 - 0.999**STEP)) + 1e-08)
        + decay_value * param
    )
    return (param - rate_value * update, moment.astype(jnp.bfloat16), variance)


def enter(n, me):
    barrier = pltpu.get_barrier_semaphore()

    def greet(k, carry):
        pl.semaphore_signal(
            barrier, inc=1, device_id={"member": lax.rem(me + k, n)}, device_id_type=MESH_ID
        )
        return carry

    lax.fori_loop(1, n, greet, 0)
    pl.semaphore_wait(barrier, n - 1)


def transpose(n, me, src, dst, send_sem, recv_sem):
    def copy(k):
        target = lax.rem(me + k, n)
        return pltpu.make_async_remote_copy(
            src_ref=src.at[target],
            dst_ref=dst.at[me],
            send_sem=send_sem.at[k],
            recv_sem=recv_sem.at[k],
            device_id={"member": target},
            device_id_type=MESH_ID,
        )

    def start(k, carry):
        copy(k).start()
        return carry

    def finish(k, carry):
        copy(k).wait()
        return carry

    lax.fori_loop(1, n, start, 0)
    dst[me] = src[me]
    lax.fori_loop(1, n, finish, 0)


def pick_rows(n, source_ref, held, picked):
    def pick(i, carry):
        picked[i] = held[source_ref[i]]
        return carry

    lax.fori_loop(0, n, pick, 0)


def exploit_kernel(n, source_ref, send_ref, out_ref, held, picked, send1, recv1, send2, recv2):
    me = lax.axis_index("member")
    enter(n, me)
    transpose(n, me, send_ref, held, send1, recv1)
    pick_rows(n, source_ref, held, picked)
    transpose(n, me, picked, out_ref, send2, recv2)


def gather_kernel(n, batch_total, patches, source_ref, labels_ref, up_ref, down_ref, tokens_ref,
                  classifier_ref, *refs):
    parts = refs[:-17]
    (out_ref, up_full, down_full, normed_ref, preact_ref, act_ref, delta_ref,
     flat, held, send1, recv1,
     near_send, near_recv, far_send, far_recv, fwd_send, fwd_recv) = refs[-17:]
    me = lax.axis_index("member")
    shard = lax.axis_index("dp")
    core = shard % 2
    chip = shard // 2
    partner = chip * 2 + (1 - core)
    across = (1 - chip) * 2 + core
    lanes = flat.shape[1]
    chunk = held.shape[1]
    offset = 0
    for part in parts:
        rows, cols = part.shape
        for block in range(cols // lanes):
            flat[pl.ds(offset, rows), :] = part[:, pl.ds(block * lanes, lanes)].astype(flat.dtype)
            offset += rows

    barrier = pltpu.get_barrier_semaphore()

    def greet(k, carry):
        pl.semaphore_signal(
            barrier, inc=1, device_id={"member": lax.rem(me + k, n)}, device_id_type=MESH_ID
        )
        return carry

    lax.fori_loop(1, n, greet, 0)
    for peer in (partner, across):
        pl.semaphore_signal(barrier, inc=1, device_id={"dp": peer}, device_id_type=MESH_ID)
    pl.semaphore_wait(barrier, n - 1 + 2)

    def rows_of(full, index):
        size = full.shape[0] // 4
        return full.at[pl.ds(pl.multiple_of(index * size, size), size)]

    def dp_copy(src, dst, send, recv, slot, peer):
        return pltpu.make_async_remote_copy(
            src_ref=src, dst_ref=dst, send_sem=send.at[slot], recv_sem=recv.at[slot],
            device_id={"dp": peer}, device_id_type=MESH_ID,
        )

    shares = ((up_ref, up_full), (down_ref, down_full))
    far = [dp_copy(share, rows_of(full, shard), far_send, far_recv, slot, across)
           for slot, (share, full) in enumerate(shares)]
    near = [dp_copy(share, rows_of(full, shard), near_send, near_recv, slot, partner)
            for slot, (share, full) in enumerate(shares)]
    for item in far + near:
        item.start()

    def copy(k):
        target = lax.rem(me + k, n)
        return pltpu.make_async_remote_copy(
            src_ref=flat.at[pl.ds(pl.multiple_of(target * chunk, 16), chunk)],
            dst_ref=held.at[me],
            send_sem=send1.at[k],
            recv_sem=recv1.at[k],
            device_id={"member": target},
            device_id_type=MESH_ID,
        )

    def start(k, carry):
        copy(k).start()
        return carry

    def finish(k, carry):
        copy(k).wait()
        return carry

    lax.fori_loop(1, n, start, 0)
    held[me] = flat[pl.ds(pl.multiple_of(me * chunk, 16), chunk)]
    for share, full in shares:
        rows_of(full, shard)[...] = share[...]
    for item in far:
        item.wait()
    forward = [dp_copy(rows_of(full, across), rows_of(full, across), fwd_send, fwd_recv, slot,
                       partner)
               for slot, (share, full) in enumerate(shares)]
    for item in forward:
        item.start()
    for item in near + forward:
        item.wait()
    normed, preact, activated, delta = forward_half(
        tokens_ref[...], labels_ref, up_full[...], down_full[...], classifier_ref[...],
        batch_total, patches,
    )
    normed_ref[...] = normed
    preact_ref[...] = preact
    act_ref[...] = activated
    delta_ref[...] = delta
    lax.fori_loop(1, n, finish, 0)
    pick_rows(n, source_ref, held, out_ref)


def scatter_kernel(n, send_ref, out_ref, send1, recv1):
    me = lax.axis_index("member")
    enter(n, me)
    transpose(n, me, send_ref, out_ref, send1, recv1)


def forward_half(tokens, labels_ref, up_weight, down_weight, classifier, batch_total, patches):
    tokens_n, features = tokens.shape
    hidden_units = up_weight.shape[1]
    classes = classifier.shape[1]
    images = tokens_n // patches
    token_rows = tokens.astype(jnp.float32)
    center = token_rows - jnp.mean(token_rows, axis=1, keepdims=True)
    normed = (center * lax.rsqrt(jnp.mean(center * center, axis=1, keepdims=True) + 1e-06)).astype(
        jnp.bfloat16
    )
    preact = jnp.dot(normed, up_weight, preferred_element_type=jnp.float32) * features ** (-0.5)
    activated = (0.5 * preact * (1.0 + lax.erf(preact * 0.7071067811865476))).astype(jnp.bfloat16)
    residual = token_rows + jnp.dot(
        activated, down_weight, preferred_element_type=jnp.float32
    ) * hidden_units ** (-0.5)
    out_center = residual - jnp.mean(residual, axis=1, keepdims=True)
    inverse = lax.rsqrt(jnp.mean(out_center * out_center, axis=1, keepdims=True) + 1e-06)
    out_normed = out_center * inverse
    image_of_row = lax.broadcasted_iota(jnp.int32, (tokens_n, 1), 0) // patches
    pooled = jnp.concatenate(
        [
            jnp.sum(jnp.where(image_of_row == i, out_normed, 0.0), axis=0, keepdims=True)
            for i in range(images)
        ],
        axis=0,
    ) / patches
    pooled = pooled.astype(jnp.bfloat16)
    logits = jnp.dot(pooled, classifier, preferred_element_type=jnp.float32)
    powered = jnp.exp(logits)
    softmax_out = powered / jnp.sum(powered, axis=1, keepdims=True)
    row = lax.broadcasted_iota(jnp.int32, (images, classes), 0)
    column = lax.broadcasted_iota(jnp.int32, (images, classes), 1)
    label = jnp.zeros((images, classes), jnp.int32)
    for i in range(images):
        label = jnp.where(row == i, labels_ref[i], label)
    onehot = (column == label).astype(jnp.float32)
    logit_delta = ((softmax_out - onehot) / batch_total).astype(jnp.bfloat16)
    pool_delta = (
        lax.dot_general(
            logit_delta, classifier, (((1,), (1,)), ((), ())), preferred_element_type=jnp.float32
        )
        / patches
    )
    token_delta = jnp.zeros((tokens_n, features), jnp.float32)
    for i in range(images):
        token_delta = jnp.where(image_of_row == i, pool_delta[i:i + 1, :], token_delta)
    residual_delta = inverse * (
        token_delta
        - jnp.mean(token_delta, axis=1, keepdims=True)
        - out_normed * jnp.mean(token_delta * out_normed, axis=1, keepdims=True)
    )
    residual_delta = residual_delta.astype(jnp.bfloat16)
    return normed, preact, activated, residual_delta


def backward_half(normed, preact, activated, residual_delta, down_weight):
    features = normed.shape[1]
    hidden_units = preact.shape[1]
    down_scale = hidden_units ** (-0.5)
    down_gradient = (
        lax.dot_general(
            activated, residual_delta, (((0,), (0,)), ((), ())), preferred_element_type=jnp.float32
        )
        * down_scale
    )
    hidden_delta = (
        lax.dot_general(
            residual_delta, down_weight, (((1,), (1,)), ((), ())), preferred_element_type=jnp.float32
        )
        * down_scale
    )
    derivative = (
        0.5 * (1.0 + lax.erf(preact * 0.7071067811865476))
        + preact * jnp.exp(-0.5 * preact * preact) * 0.3989422804014327
    )
    preact_delta = (hidden_delta * derivative).astype(jnp.bfloat16)
    up_gradient = lax.dot_general(
        normed, preact_delta, (((0,), (0,)), ((), ())), preferred_element_type=jnp.float32
    ) * features ** (-0.5)
    return up_gradient, down_gradient


def scatter_compute_kernel(
    n, send_ref, normed_ref, preact_ref, act_ref, delta_ref, down_ref,
    up_share_ref, down_share_ref, up_first_ref, down_first_ref, up_second_ref, down_second_ref,
    flat, up_term, down_term, up_near, down_near, up_part, down_part, up_far, down_far,
    send_sem, recv_sem, near_send, near_recv, far_send, far_recv,
):
    me = lax.axis_index("member")
    shard = lax.axis_index("dp")
    core = shard % 2
    chip = shard // 2
    partner = chip * 2 + (1 - core)
    across = (1 - chip) * 2 + core
    diagonal = (1 - chip) * 2 + (1 - core)

    barrier = pltpu.get_barrier_semaphore()

    def greet(k, carry):
        pl.semaphore_signal(
            barrier, inc=1, device_id={"member": lax.rem(me + k, n)}, device_id_type=MESH_ID
        )
        return carry

    lax.fori_loop(1, n, greet, 0)
    for peer in (partner, across, diagonal):
        pl.semaphore_signal(barrier, inc=1, device_id={"dp": peer}, device_id_type=MESH_ID)
    pl.semaphore_wait(barrier, n - 1 + 3)

    chunk = send_ref.shape[1]

    def copy(k):
        target = lax.rem(me + k, n)
        return pltpu.make_async_remote_copy(
            src_ref=send_ref.at[target],
            dst_ref=flat.at[pl.ds(pl.multiple_of(me * chunk, 16), chunk)],
            send_sem=send_sem.at[k],
            recv_sem=recv_sem.at[k],
            device_id={"member": target},
            device_id_type=MESH_ID,
        )

    def start(k, carry):
        copy(k).start()
        return carry

    def finish(k, carry):
        copy(k).wait()
        return carry

    lax.fori_loop(1, n, start, 0)
    flat[pl.ds(pl.multiple_of(me * chunk, 16), chunk)] = send_ref[me]
    up_gradient, down_gradient = backward_half(
        normed_ref[...], preact_ref[...], act_ref[...], delta_ref[...], down_ref[...]
    )
    up_term[...] = up_gradient.astype(jnp.bfloat16)
    down_term[...] = down_gradient.astype(jnp.bfloat16)

    def rows(term, index):
        size = term.shape[0] // 4
        return term.at[pl.ds(pl.multiple_of(index * size, size), size)]

    near = []
    slot = 0
    for term, near_buf in ((up_term, up_near), (down_term, down_near)):
        for which, index in ((0, diagonal), (1, partner)):
            near.append(
                pltpu.make_async_remote_copy(
                    src_ref=rows(term, index),
                    dst_ref=near_buf.at[which],
                    send_sem=near_send.at[slot],
                    recv_sem=near_recv.at[slot],
                    device_id={"dp": partner},
                    device_id_type=MESH_ID,
                )
            )
            slot += 1
    for item in near:
        item.start()
    for item in near:
        item.wait()

    far = []
    slot = 0
    for term, near_buf, part, far_buf in (
        (up_term, up_near, up_part, up_far),
        (down_term, down_near, down_part, down_far),
    ):
        part[...] = (
            rows(term, across)[...].astype(jnp.float32) + near_buf[0].astype(jnp.float32)
        ).astype(jnp.bfloat16)
        far.append(
            pltpu.make_async_remote_copy(
                src_ref=part,
                dst_ref=far_buf,
                send_sem=far_send.at[slot],
                recv_sem=far_recv.at[slot],
                device_id={"dp": across},
                device_id_type=MESH_ID,
            )
        )
        slot += 1
    for item in far:
        item.start()
    for item in far:
        item.wait()

    for term, near_buf, far_buf, share in (
        (up_term, up_near, up_far, up_share_ref),
        (down_term, down_near, down_far, down_share_ref),
    ):
        share[...] = (
            rows(term, shard)[...].astype(jnp.float32)
            + near_buf[1].astype(jnp.float32)
            + far_buf[...].astype(jnp.float32)
        )
    lax.fori_loop(1, n, finish, 0)
    lanes = flat.shape[1]
    offset = 0
    for part in (up_first_ref, down_first_ref, up_second_ref, down_second_ref):
        rows, cols = part.shape
        for block in range(cols // lanes):
            part[:, pl.ds(block * lanes, lanes)] = flat[pl.ds(offset, rows), :]
            offset += rows


def scatter_with_gradients(picked, normed, preact, activated, delta, up_full, down_full,
                           kernel_id):
    n = picked.shape[0]
    tokens_n, features = normed.shape
    vmem = pl.BlockSpec(memory_space=pltpu.VMEM)
    moved = picked.size * picked.dtype.itemsize
    flops = 6 * tokens_n * features * up_full.shape[1]
    up_rows = (up_full.shape[0] // 4, up_full.shape[1])
    down_rows = (down_full.shape[0] // 4, down_full.shape[1])
    bf16 = jnp.bfloat16
    return pl.pallas_call(
        functools.partial(scatter_compute_kernel, n),
        out_shape=(
            jax.ShapeDtypeStruct(up_rows, jnp.float32),
            jax.ShapeDtypeStruct(down_rows, jnp.float32),
        ) + tuple(jax.ShapeDtypeStruct(shape, bf16) for shape in (up_rows, down_rows) * 2),
        in_specs=[vmem] * 6,
        out_specs=(vmem,) * 6,
        scratch_shapes=[
            pltpu.VMEM((picked.shape[0] * picked.shape[1], picked.shape[2]), bf16),
            pltpu.VMEM(up_full.shape, bf16),
            pltpu.VMEM(down_full.shape, bf16),
            pltpu.VMEM((2,) + up_rows, bf16),
            pltpu.VMEM((2,) + down_rows, bf16),
            pltpu.VMEM(up_rows, bf16),
            pltpu.VMEM(down_rows, bf16),
            pltpu.VMEM(up_rows, bf16),
            pltpu.VMEM(down_rows, bf16),
            pltpu.SemaphoreType.DMA((n,)),
            pltpu.SemaphoreType.DMA((n,)),
            pltpu.SemaphoreType.DMA((4,)),
            pltpu.SemaphoreType.DMA((4,)),
            pltpu.SemaphoreType.DMA((2,)),
            pltpu.SemaphoreType.DMA((2,)),
        ],
        compiler_params=pltpu.CompilerParams(
            collective_id=kernel_id, has_side_effects=True, vmem_limit_bytes=63 * 1024 * 1024
        ),
        cost_estimate=pl.CostEstimate(flops=flops, transcendentals=0, bytes_accessed=moved * 20),
    )(picked, normed, preact, activated, delta, down_full)


def member_call(body, packed, operands, scratch, kernel_id):
    n, rows, lanes = packed.shape
    moved = packed.size * packed.dtype.itemsize
    smem = [pl.BlockSpec(memory_space=pltpu.SMEM)] * (len(operands) - 1)
    return pl.pallas_call(
        functools.partial(body, n),
        out_shape=jax.ShapeDtypeStruct(packed.shape, packed.dtype),
        in_specs=smem + [pl.BlockSpec(memory_space=pltpu.VMEM)],
        out_specs=pl.BlockSpec(memory_space=pltpu.VMEM),
        scratch_shapes=scratch,
        compiler_params=pltpu.CompilerParams(
            collective_id=kernel_id, has_side_effects=True, vmem_limit_bytes=48 * 1024 * 1024
        ),
        cost_estimate=pl.CostEstimate(flops=0, transcendentals=0, bytes_accessed=moved * 20),
    )(*operands)


def exploit_transfer(packed, source, kernel_id):
    n, rows, lanes = packed.shape
    block = pltpu.VMEM((n, rows, lanes), packed.dtype)
    sems = [pltpu.SemaphoreType.DMA((n,))] * 4
    return member_call(exploit_kernel, packed, (source, packed), [block, block] + sems, kernel_id)


def exploit_gather(parts, shares, source, tokens, labels, classifier, batch_total, members,
                   shards, kernel_id):
    images, patches, features = tokens.shape
    tokens_n = images * patches
    hidden = shares[0].shape[1]
    lanes = 128
    total = sum(part.size for part in parts) // lanes
    shape = (members, total // members, lanes)
    vmem = pl.BlockSpec(memory_space=pltpu.VMEM)
    moved = total * lanes * 2
    fulls = [jax.ShapeDtypeStruct((share.shape[0] * shards, share.shape[1]), share.dtype)
             for share in shares]
    sems = [pltpu.SemaphoreType.DMA((len(shares),))] * 6
    return pl.pallas_call(
        functools.partial(gather_kernel, members, batch_total, patches),
        out_shape=(
            jax.ShapeDtypeStruct(shape, jnp.bfloat16),
            *fulls,
            jax.ShapeDtypeStruct((tokens_n, features), jnp.bfloat16),
            jax.ShapeDtypeStruct((tokens_n, hidden), jnp.float32),
            jax.ShapeDtypeStruct((tokens_n, hidden), jnp.bfloat16),
            jax.ShapeDtypeStruct((tokens_n, features), jnp.bfloat16),
        ),
        in_specs=[pl.BlockSpec(memory_space=pltpu.SMEM)] * 2
        + [vmem] * (len(shares) + 2 + len(parts)),
        out_specs=(vmem,) * 7,
        scratch_shapes=[
            pltpu.VMEM((total, lanes), jnp.bfloat16),
            pltpu.VMEM(shape, jnp.bfloat16),
            pltpu.SemaphoreType.DMA((members,)),
            pltpu.SemaphoreType.DMA((members,)),
        ] + sems,
        compiler_params=pltpu.CompilerParams(
            collective_id=kernel_id, has_side_effects=True, vmem_limit_bytes=63 * 1024 * 1024
        ),
        cost_estimate=pl.CostEstimate(flops=0, transcendentals=0, bytes_accessed=moved * 20),
    )(source, labels, *shares, tokens.reshape(tokens_n, features), classifier, *parts)


def exploit_scatter(packed, kernel_id):
    n = packed.shape[0]
    sems = [pltpu.SemaphoreType.DMA((n,))] * 2
    return member_call(scatter_kernel, packed, (packed,), sems, kernel_id)


def lane_major(part, lanes):
    rows, cols = part.shape
    return part.reshape(rows, cols // lanes, lanes).transpose(1, 0, 2).reshape(-1, lanes)


def from_lane_major(flat, shape, lanes):
    rows, cols = shape
    return flat.reshape(cols // lanes, rows, lanes).transpose(1, 0, 2).reshape(rows, cols)


def exploit_rows(parts, source, members, kernel_id):
    lanes = 128
    rows = [part.size // (members * lanes) for part in parts]
    pad = -sum(rows) % 16
    pieces = [part.astype(jnp.bfloat16).reshape(members, -1, lanes) for part in parts]
    if pad:
        pieces.append(jnp.zeros((members, pad, lanes), jnp.bfloat16))
    back = exploit_transfer(jnp.concatenate(pieces, axis=1), source, kernel_id)
    out = []
    start = 0
    for part, count in zip(parts, rows):
        out.append(back[:, start:start + count].reshape(part.shape))
        start += count
    return out


def pack_tiles(parts, members):
    lanes = 128
    flat = jnp.concatenate([lane_major(part.astype(jnp.bfloat16), lanes) for part in parts])
    return flat.reshape(members, -1, flat.shape[-1])


def unpack_tiles(back, parts):
    lanes = back.shape[-1]
    back = back.reshape(-1, lanes)
    out = []
    start = 0
    for part in parts:
        count = part.size // lanes
        out.append(from_lane_major(back[start:start + count], part.shape, lanes))
        start += count
    return out


def per_device(
    tokens,
    labels,
    source,
    learn_rate,
    weight_decay,
    classifier,
    up_param,
    up_first,
    up_second,
    down_param,
    down_first,
    down_second,
):
    members = lax.axis_size("member")
    shards = lax.axis_size("dp")
    me = lax.axis_index("member")
    own = source[me] == me

    up_bf, down_bf = exploit_rows((up_param[0], down_param[0]), source, members, 0)
    moments = (up_first[0], down_first[0], up_second[0], down_second[0])
    batch_total = tokens.shape[1] * shards
    picked, up_full, down_full, normed, preact, activated, delta = exploit_gather(
        moments, (up_bf, down_bf), source, tokens[0], labels[0], classifier, batch_total,
        members, shards, 1,
    )
    up_share, down_share, up_mom, down_mom, up_var_bf, down_var_bf = scatter_with_gradients(
        picked, normed, preact, activated, delta, up_full, down_full, 2
    )

    up_now = jnp.where(own, up_param[0], up_bf.astype(jnp.float32))
    down_now = jnp.where(own, down_param[0], down_bf.astype(jnp.float32))
    up_var = jnp.where(own, up_second[0], up_var_bf.astype(jnp.float32))
    down_var = jnp.where(own, down_second[0], down_var_bf.astype(jnp.float32))

    rate_value = learn_rate[0]
    decay_value = weight_decay[0]
    up_new = adamw_step(up_now, up_mom, up_var, up_share, rate_value, decay_value)
    down_new = adamw_step(down_now, down_mom, down_var, down_share, rate_value, decay_value)
    return tuple(value[None] for value in up_new + down_new)


def solution(mesh):
    placed = (
        P("member", "dp", None, None),
        P("member", "dp"),
        P(),
        P("member"),
        P("member"),
        P(),
        P("member", "dp", None),
        P("member", "dp", None),
        P("member", "dp", None),
        P("member", "dp", None),
        P("member", "dp", None),
        P("member", "dp", None),
    )
    return jax.shard_map(
        per_device,
        mesh=mesh,
        in_specs=placed,
        out_specs=(P("member", "dp", None),) * 6,
        check_vma=False,
    )
```

```python
import functools

import jax
import jax.numpy as jnp
from jax import lax
from jax.experimental import pallas as pl
from jax.experimental.pallas import tpu as pltpu
from jax.sharding import PartitionSpec as P

MESH_ID = pl.DeviceIdType.MESH

STEP = 1000


def local_gradients(tokens, labels, up_weight, down_weight, classifier, batch_total):
    images, patches, features = tokens.shape
    hidden_units = up_weight.shape[1]
    token_rows = tokens.reshape(images * patches, features).astype(jnp.float32)
    center = token_rows - jnp.mean(token_rows, axis=1, keepdims=True)
    normed = (center * lax.rsqrt(jnp.mean(center * center, axis=1, keepdims=True) + 1e-06)).astype(
        jnp.bfloat16
    )
    preact = jnp.dot(normed, up_weight, preferred_element_type=jnp.float32) * features ** (-0.5)
    activated = (0.5 * preact * (1.0 + lax.erf(preact * 0.7071067811865476))).astype(jnp.bfloat16)
    residual = token_rows + jnp.dot(
        activated, down_weight, preferred_element_type=jnp.float32
    ) * hidden_units ** (-0.5)
    out_center = residual - jnp.mean(residual, axis=1, keepdims=True)
    inverse = lax.rsqrt(jnp.mean(out_center * out_center, axis=1, keepdims=True) + 1e-06)
    out_normed = out_center * inverse
    pooled = jnp.mean(out_normed.reshape(images, patches, features), axis=1).astype(jnp.bfloat16)
    logits = jnp.dot(pooled, classifier, preferred_element_type=jnp.float32)
    powered = jnp.exp(logits)
    softmax_out = powered / jnp.sum(powered, axis=1, keepdims=True)
    onehot = (labels[:, None] == jnp.arange(classifier.shape[1], dtype=jnp.int32)[None, :]).astype(
        jnp.float32
    )
    logit_delta = ((softmax_out - onehot) / batch_total).astype(jnp.bfloat16)
    pool_delta = (
        lax.dot_general(
            logit_delta, classifier, (((1,), (1,)), ((), ())), preferred_element_type=jnp.float32
        )
        / patches
    )
    token_delta = jnp.broadcast_to(pool_delta[:, None, :], (images, patches, features)).reshape(
        images * patches, features
    )
    residual_delta = inverse * (
        token_delta
        - jnp.mean(token_delta, axis=1, keepdims=True)
        - out_normed * jnp.mean(token_delta * out_normed, axis=1, keepdims=True)
    )
    residual_delta = residual_delta.astype(jnp.bfloat16)
    down_scale = hidden_units ** (-0.5)
    down_gradient = (
        lax.dot_general(
            activated, residual_delta, (((0,), (0,)), ((), ())), preferred_element_type=jnp.float32
        )
        * down_scale
    )
    hidden_delta = (
        lax.dot_general(
            residual_delta,
            down_weight,
            (((1,), (1,)), ((), ())),
            preferred_element_type=jnp.float32,
        )
        * down_scale
    )
    derivative = (
        0.5 * (1.0 + lax.erf(preact * 0.7071067811865476))
        + preact * jnp.exp(-0.5 * preact * preact) * 0.3989422804014327
    )
    preact_delta = (hidden_delta * derivative).astype(jnp.bfloat16)
    up_gradient = lax.dot_general(
        normed, preact_delta, (((0,), (0,)), ((), ())), preferred_element_type=jnp.float32
    ) * features ** (-0.5)
    return (up_gradient, down_gradient)


def adamw_step(param, first, second, gradient, rate_value, decay_value):
    moment = 0.9 * first.astype(jnp.float32) + 0.1 * gradient
    variance = 0.999 * second + 0.001 * gradient * gradient
    update = (
        moment / (1.0 - 0.9**STEP) / (jnp.sqrt(variance / (1.0 - 0.999**STEP)) + 1e-08)
        + decay_value * param
    )
    return (param - rate_value * update, moment.astype(jnp.bfloat16), variance)


def enter(n, me):
    barrier = pltpu.get_barrier_semaphore()

    def greet(k, carry):
        pl.semaphore_signal(
            barrier, inc=1, device_id={"member": lax.rem(me + k, n)}, device_id_type=MESH_ID
        )
        return carry

    lax.fori_loop(1, n, greet, 0)
    pl.semaphore_wait(barrier, n - 1)


def transpose(n, me, src, dst, send_sem, recv_sem):
    def copy(k):
        target = lax.rem(me + k, n)
        return pltpu.make_async_remote_copy(
            src_ref=src.at[target],
            dst_ref=dst.at[me],
            send_sem=send_sem.at[k],
            recv_sem=recv_sem.at[k],
            device_id={"member": target},
            device_id_type=MESH_ID,
        )

    def start(k, carry):
        copy(k).start()
        return carry

    def finish(k, carry):
        copy(k).wait()
        return carry

    lax.fori_loop(1, n, start, 0)
    dst[me] = src[me]
    lax.fori_loop(1, n, finish, 0)


def pick_rows(n, source_ref, held, picked):
    def pick(i, carry):
        picked[i] = held[source_ref[i]]
        return carry

    lax.fori_loop(0, n, pick, 0)


def exploit_kernel(n, source_ref, send_ref, out_ref, held, picked, send1, recv1, send2, recv2):
    me = lax.axis_index("member")
    enter(n, me)
    transpose(n, me, send_ref, held, send1, recv1)
    pick_rows(n, source_ref, held, picked)
    transpose(n, me, picked, out_ref, send2, recv2)


def gather_kernel(n, batch_total, patches, source_ref, labels_ref, up_ref, down_ref, tokens_ref,
                  classifier_ref, *refs):
    parts = refs[:-17]
    (out_ref, up_full, down_full, normed_ref, preact_ref, act_ref, delta_ref,
     flat, held, send1, recv1,
     near_send, near_recv, far_send, far_recv, fwd_send, fwd_recv) = refs[-17:]
    me = lax.axis_index("member")
    shard = lax.axis_index("dp")
    core = shard % 2
    chip = shard // 2
    partner = chip * 2 + (1 - core)
    across = (1 - chip) * 2 + core
    lanes = flat.shape[1]
    chunk = held.shape[1]
    offset = 0
    for part in parts:
        rows, cols = part.shape
        for block in range(cols // lanes):
            flat[pl.ds(offset, rows), :] = part[:, pl.ds(block * lanes, lanes)].astype(flat.dtype)
            offset += rows

    barrier = pltpu.get_barrier_semaphore()

    def greet(k, carry):
        pl.semaphore_signal(
            barrier, inc=1, device_id={"member": lax.rem(me + k, n)}, device_id_type=MESH_ID
        )
        return carry

    lax.fori_loop(1, n, greet, 0)
    for peer in (partner, across):
        pl.semaphore_signal(barrier, inc=1, device_id={"dp": peer}, device_id_type=MESH_ID)
    pl.semaphore_wait(barrier, n - 1 + 2)

    def rows_of(full, index):
        size = full.shape[0] // 4
        return full.at[pl.ds(pl.multiple_of(index * size, size), size)]

    def dp_copy(src, dst, send, recv, slot, peer):
        return pltpu.make_async_remote_copy(
            src_ref=src, dst_ref=dst, send_sem=send.at[slot], recv_sem=recv.at[slot],
            device_id={"dp": peer}, device_id_type=MESH_ID,
        )

    shares = ((up_ref, up_full), (down_ref, down_full))
    far = [dp_copy(share, rows_of(full, shard), far_send, far_recv, slot, across)
           for slot, (share, full) in enumerate(shares)]
    near = [dp_copy(share, rows_of(full, shard), near_send, near_recv, slot, partner)
            for slot, (share, full) in enumerate(shares)]
    for item in far + near:
        item.start()

    def copy(k):
        target = lax.rem(me + k, n)
        return pltpu.make_async_remote_copy(
            src_ref=flat.at[pl.ds(pl.multiple_of(target * chunk, 16), chunk)],
            dst_ref=held.at[me],
            send_sem=send1.at[k],
            recv_sem=recv1.at[k],
            device_id={"member": target},
            device_id_type=MESH_ID,
        )

    def start(k, carry):
        copy(k).start()
        return carry

    def finish(k, carry):
        copy(k).wait()
        return carry

    lax.fori_loop(1, n, start, 0)
    held[me] = flat[pl.ds(pl.multiple_of(me * chunk, 16), chunk)]
    for share, full in shares:
        rows_of(full, shard)[...] = share[...]
    for item in far:
        item.wait()
    forward = [dp_copy(rows_of(full, across), rows_of(full, across), fwd_send, fwd_recv, slot,
                       partner)
               for slot, (share, full) in enumerate(shares)]
    for item in forward:
        item.start()
    for item in near + forward:
        item.wait()
    normed, preact, activated, delta = forward_half(
        tokens_ref[...], labels_ref, up_full[...], down_full[...], classifier_ref[...],
        batch_total, patches,
    )
    normed_ref[...] = normed
    preact_ref[...] = preact
    act_ref[...] = activated
    delta_ref[...] = delta
    lax.fori_loop(1, n, finish, 0)
    pick_rows(n, source_ref, held, out_ref)


def scatter_kernel(n, send_ref, out_ref, send1, recv1):
    me = lax.axis_index("member")
    enter(n, me)
    transpose(n, me, send_ref, out_ref, send1, recv1)


def forward_half(tokens, labels_ref, up_weight, down_weight, classifier, batch_total, patches):
    tokens_n, features = tokens.shape
    hidden_units = up_weight.shape[1]
    classes = classifier.shape[1]
    images = tokens_n // patches
    token_rows = tokens.astype(jnp.float32)
    center = token_rows - jnp.mean(token_rows, axis=1, keepdims=True)
    normed = (center * lax.rsqrt(jnp.mean(center * center, axis=1, keepdims=True) + 1e-06)).astype(
        jnp.bfloat16
    )
    preact = jnp.dot(normed, up_weight, preferred_element_type=jnp.float32) * features ** (-0.5)
    activated = (0.5 * preact * (1.0 + lax.erf(preact * 0.7071067811865476))).astype(jnp.bfloat16)
    residual = token_rows + jnp.dot(
        activated, down_weight, preferred_element_type=jnp.float32
    ) * hidden_units ** (-0.5)
    out_center = residual - jnp.mean(residual, axis=1, keepdims=True)
    inverse = lax.rsqrt(jnp.mean(out_center * out_center, axis=1, keepdims=True) + 1e-06)
    out_normed = out_center * inverse
    image_of_row = lax.broadcasted_iota(jnp.int32, (tokens_n, 1), 0) // patches
    pooled = jnp.concatenate(
        [
            jnp.sum(jnp.where(image_of_row == i, out_normed, 0.0), axis=0, keepdims=True)
            for i in range(images)
        ],
        axis=0,
    ) / patches
    pooled = pooled.astype(jnp.bfloat16)
    logits = jnp.dot(pooled, classifier, preferred_element_type=jnp.float32)
    powered = jnp.exp(logits)
    softmax_out = powered / jnp.sum(powered, axis=1, keepdims=True)
    row = lax.broadcasted_iota(jnp.int32, (images, classes), 0)
    column = lax.broadcasted_iota(jnp.int32, (images, classes), 1)
    label = jnp.zeros((images, classes), jnp.int32)
    for i in range(images):
        label = jnp.where(row == i, labels_ref[i], label)
    onehot = (column == label).astype(jnp.float32)
    logit_delta = ((softmax_out - onehot) / batch_total).astype(jnp.bfloat16)
    pool_delta = (
        lax.dot_general(
            logit_delta, classifier, (((1,), (1,)), ((), ())), preferred_element_type=jnp.float32
        )
        / patches
    )
    token_delta = jnp.zeros((tokens_n, features), jnp.float32)
    for i in range(images):
        token_delta = jnp.where(image_of_row == i, pool_delta[i:i + 1, :], token_delta)
    residual_delta = inverse * (
        token_delta
        - jnp.mean(token_delta, axis=1, keepdims=True)
        - out_normed * jnp.mean(token_delta * out_normed, axis=1, keepdims=True)
    )
    residual_delta = residual_delta.astype(jnp.bfloat16)
    return normed, preact, activated, residual_delta


def backward_half(normed, preact, activated, residual_delta, down_weight):
    features = normed.shape[1]
    hidden_units = preact.shape[1]
    down_scale = hidden_units ** (-0.5)
    down_gradient = (
        lax.dot_general(
            activated, residual_delta, (((0,), (0,)), ((), ())), preferred_element_type=jnp.float32
        )
        * down_scale
    )
    hidden_delta = (
        lax.dot_general(
            residual_delta, down_weight, (((1,), (1,)), ((), ())), preferred_element_type=jnp.float32
        )
        * down_scale
    )
    derivative = (
        0.5 * (1.0 + lax.erf(preact * 0.7071067811865476))
        + preact * jnp.exp(-0.5 * preact * preact) * 0.3989422804014327
    )
    preact_delta = (hidden_delta * derivative).astype(jnp.bfloat16)
    up_gradient = lax.dot_general(
        normed, preact_delta, (((0,), (0,)), ((), ())), preferred_element_type=jnp.float32
    ) * features ** (-0.5)
    return up_gradient, down_gradient


def scatter_compute_kernel(
    n, send_ref, normed_ref, preact_ref, act_ref, delta_ref, down_ref,
    up_share_ref, down_share_ref, up_first_ref, down_first_ref, up_second_ref, down_second_ref,
    flat, up_term, down_term, up_near, down_near, up_part, down_part, up_far, down_far,
    send_sem, recv_sem, near_send, near_recv, far_send, far_recv,
):
    me = lax.axis_index("member")
    shard = lax.axis_index("dp")
    core = shard % 2
    chip = shard // 2
    partner = chip * 2 + (1 - core)
    across = (1 - chip) * 2 + core
    diagonal = (1 - chip) * 2 + (1 - core)

    barrier = pltpu.get_barrier_semaphore()

    def greet(k, carry):
        pl.semaphore_signal(
            barrier, inc=1, device_id={"member": lax.rem(me + k, n)}, device_id_type=MESH_ID
        )
        return carry

    lax.fori_loop(1, n, greet, 0)
    for peer in (partner, across, diagonal):
        pl.semaphore_signal(barrier, inc=1, device_id={"dp": peer}, device_id_type=MESH_ID)
    pl.semaphore_wait(barrier, n - 1 + 3)

    chunk = send_ref.shape[1]

    def copy(k):
        target = lax.rem(me + k, n)
        return pltpu.make_async_remote_copy(
            src_ref=send_ref.at[target],
            dst_ref=flat.at[pl.ds(pl.multiple_of(me * chunk, 16), chunk)],
            send_sem=send_sem.at[k],
            recv_sem=recv_sem.at[k],
            device_id={"member": target},
            device_id_type=MESH_ID,
        )

    def start(k, carry):
        copy(k).start()
        return carry

    def finish(k, carry):
        copy(k).wait()
        return carry

    lax.fori_loop(1, n // 2, start, 0)
    flat[pl.ds(pl.multiple_of(me * chunk, 16), chunk)] = send_ref[me]
    up_gradient, down_gradient = backward_half(
        normed_ref[...], preact_ref[...], act_ref[...], delta_ref[...], down_ref[...]
    )
    up_term[...] = up_gradient.astype(jnp.bfloat16)
    down_term[...] = down_gradient.astype(jnp.bfloat16)

    def rows(term, index):
        size = term.shape[0] // 4
        return term.at[pl.ds(pl.multiple_of(index * size, size), size)]

    near = []
    slot = 0
    for term, near_buf in ((up_term, up_near), (down_term, down_near)):
        for which, index in ((0, diagonal), (1, partner)):
            near.append(
                pltpu.make_async_remote_copy(
                    src_ref=rows(term, index),
                    dst_ref=near_buf.at[which],
                    send_sem=near_send.at[slot],
                    recv_sem=near_recv.at[slot],
                    device_id={"dp": partner},
                    device_id_type=MESH_ID,
                )
            )
            slot += 1
    for item in near:
        item.start()
    for item in near:
        item.wait()

    far = []
    slot = 0
    for term, near_buf, part, far_buf in (
        (up_term, up_near, up_part, up_far),
        (down_term, down_near, down_part, down_far),
    ):
        part[...] = (
            rows(term, across)[...].astype(jnp.float32) + near_buf[0].astype(jnp.float32)
        ).astype(jnp.bfloat16)
        far.append(
            pltpu.make_async_remote_copy(
                src_ref=part,
                dst_ref=far_buf,
                send_sem=far_send.at[slot],
                recv_sem=far_recv.at[slot],
                device_id={"dp": across},
                device_id_type=MESH_ID,
            )
        )
        slot += 1
    for item in far:
        item.start()
    lax.fori_loop(n // 2, n, start, 0)
    for item in far:
        item.wait()

    for term, near_buf, far_buf, share in (
        (up_term, up_near, up_far, up_share_ref),
        (down_term, down_near, down_far, down_share_ref),
    ):
        share[...] = (
            rows(term, shard)[...].astype(jnp.float32)
            + near_buf[1].astype(jnp.float32)
            + far_buf[...].astype(jnp.float32)
        )
    lax.fori_loop(1, n, finish, 0)
    lanes = flat.shape[1]
    offset = 0
    for part in (up_first_ref, down_first_ref, up_second_ref, down_second_ref):
        rows, cols = part.shape
        for block in range(cols // lanes):
            part[:, pl.ds(block * lanes, lanes)] = flat[pl.ds(offset, rows), :]
            offset += rows


def scatter_with_gradients(picked, normed, preact, activated, delta, up_full, down_full,
                           kernel_id):
    n = picked.shape[0]
    tokens_n, features = normed.shape
    vmem = pl.BlockSpec(memory_space=pltpu.VMEM)
    moved = picked.size * picked.dtype.itemsize
    flops = 6 * tokens_n * features * up_full.shape[1]
    up_rows = (up_full.shape[0] // 4, up_full.shape[1])
    down_rows = (down_full.shape[0] // 4, down_full.shape[1])
    bf16 = jnp.bfloat16
    return pl.pallas_call(
        functools.partial(scatter_compute_kernel, n),
        out_shape=(
            jax.ShapeDtypeStruct(up_rows, jnp.float32),
            jax.ShapeDtypeStruct(down_rows, jnp.float32),
        ) + tuple(jax.ShapeDtypeStruct(shape, bf16) for shape in (up_rows, down_rows) * 2),
        in_specs=[vmem] * 6,
        out_specs=(vmem,) * 6,
        scratch_shapes=[
            pltpu.VMEM((picked.shape[0] * picked.shape[1], picked.shape[2]), bf16),
            pltpu.VMEM(up_full.shape, bf16),
            pltpu.VMEM(down_full.shape, bf16),
            pltpu.VMEM((2,) + up_rows, bf16),
            pltpu.VMEM((2,) + down_rows, bf16),
            pltpu.VMEM(up_rows, bf16),
            pltpu.VMEM(down_rows, bf16),
            pltpu.VMEM(up_rows, bf16),
            pltpu.VMEM(down_rows, bf16),
            pltpu.SemaphoreType.DMA((n,)),
            pltpu.SemaphoreType.DMA((n,)),
            pltpu.SemaphoreType.DMA((4,)),
            pltpu.SemaphoreType.DMA((4,)),
            pltpu.SemaphoreType.DMA((2,)),
            pltpu.SemaphoreType.DMA((2,)),
        ],
        compiler_params=pltpu.CompilerParams(
            collective_id=kernel_id, has_side_effects=True, vmem_limit_bytes=63 * 1024 * 1024
        ),
        cost_estimate=pl.CostEstimate(flops=flops, transcendentals=0, bytes_accessed=moved * 20),
    )(picked, normed, preact, activated, delta, down_full)


def member_call(body, packed, operands, scratch, kernel_id):
    n, rows, lanes = packed.shape
    moved = packed.size * packed.dtype.itemsize
    smem = [pl.BlockSpec(memory_space=pltpu.SMEM)] * (len(operands) - 1)
    return pl.pallas_call(
        functools.partial(body, n),
        out_shape=jax.ShapeDtypeStruct(packed.shape, packed.dtype),
        in_specs=smem + [pl.BlockSpec(memory_space=pltpu.VMEM)],
        out_specs=pl.BlockSpec(memory_space=pltpu.VMEM),
        scratch_shapes=scratch,
        compiler_params=pltpu.CompilerParams(
            collective_id=kernel_id, has_side_effects=True, vmem_limit_bytes=48 * 1024 * 1024
        ),
        cost_estimate=pl.CostEstimate(flops=0, transcendentals=0, bytes_accessed=moved * 20),
    )(*operands)


def exploit_transfer(packed, source, kernel_id):
    n, rows, lanes = packed.shape
    block = pltpu.VMEM((n, rows, lanes), packed.dtype)
    sems = [pltpu.SemaphoreType.DMA((n,))] * 4
    return member_call(exploit_kernel, packed, (source, packed), [block, block] + sems, kernel_id)


def exploit_gather(parts, shares, source, tokens, labels, classifier, batch_total, members,
                   shards, kernel_id):
    images, patches, features = tokens.shape
    tokens_n = images * patches
    hidden = shares[0].shape[1]
    lanes = 128
    total = sum(part.size for part in parts) // lanes
    shape = (members, total // members, lanes)
    vmem = pl.BlockSpec(memory_space=pltpu.VMEM)
    moved = total * lanes * 2
    fulls = [jax.ShapeDtypeStruct((share.shape[0] * shards, share.shape[1]), share.dtype)
             for share in shares]
    sems = [pltpu.SemaphoreType.DMA((len(shares),))] * 6
    return pl.pallas_call(
        functools.partial(gather_kernel, members, batch_total, patches),
        out_shape=(
            jax.ShapeDtypeStruct(shape, jnp.bfloat16),
            *fulls,
            jax.ShapeDtypeStruct((tokens_n, features), jnp.bfloat16),
            jax.ShapeDtypeStruct((tokens_n, hidden), jnp.float32),
            jax.ShapeDtypeStruct((tokens_n, hidden), jnp.bfloat16),
            jax.ShapeDtypeStruct((tokens_n, features), jnp.bfloat16),
        ),
        in_specs=[pl.BlockSpec(memory_space=pltpu.SMEM)] * 2
        + [vmem] * (len(shares) + 2 + len(parts)),
        out_specs=(vmem,) * 7,
        scratch_shapes=[
            pltpu.VMEM((total, lanes), jnp.bfloat16),
            pltpu.VMEM(shape, jnp.bfloat16),
            pltpu.SemaphoreType.DMA((members,)),
            pltpu.SemaphoreType.DMA((members,)),
        ] + sems,
        compiler_params=pltpu.CompilerParams(
            collective_id=kernel_id, has_side_effects=True, vmem_limit_bytes=63 * 1024 * 1024
        ),
        cost_estimate=pl.CostEstimate(flops=0, transcendentals=0, bytes_accessed=moved * 20),
    )(source, labels, *shares, tokens.reshape(tokens_n, features), classifier, *parts)


def exploit_scatter(packed, kernel_id):
    n = packed.shape[0]
    sems = [pltpu.SemaphoreType.DMA((n,))] * 2
    return member_call(scatter_kernel, packed, (packed,), sems, kernel_id)


def lane_major(part, lanes):
    rows, cols = part.shape
    return part.reshape(rows, cols // lanes, lanes).transpose(1, 0, 2).reshape(-1, lanes)


def from_lane_major(flat, shape, lanes):
    rows, cols = shape
    return flat.reshape(cols // lanes, rows, lanes).transpose(1, 0, 2).reshape(rows, cols)


def exploit_rows(parts, source, members, kernel_id):
    lanes = 128
    rows = [part.size // (members * lanes) for part in parts]
    pad = -sum(rows) % 16
    pieces = [part.astype(jnp.bfloat16).reshape(members, -1, lanes) for part in parts]
    if pad:
        pieces.append(jnp.zeros((members, pad, lanes), jnp.bfloat16))
    back = exploit_transfer(jnp.concatenate(pieces, axis=1), source, kernel_id)
    out = []
    start = 0
    for part, count in zip(parts, rows):
        out.append(back[:, start:start + count].reshape(part.shape))
        start += count
    return out


def pack_tiles(parts, members):
    lanes = 128
    flat = jnp.concatenate([lane_major(part.astype(jnp.bfloat16), lanes) for part in parts])
    return flat.reshape(members, -1, flat.shape[-1])


def unpack_tiles(back, parts):
    lanes = back.shape[-1]
    back = back.reshape(-1, lanes)
    out = []
    start = 0
    for part in parts:
        count = part.size // lanes
        out.append(from_lane_major(back[start:start + count], part.shape, lanes))
        start += count
    return out


def per_device(
    tokens,
    labels,
    source,
    learn_rate,
    weight_decay,
    classifier,
    up_param,
    up_first,
    up_second,
    down_param,
    down_first,
    down_second,
):
    members = lax.axis_size("member")
    shards = lax.axis_size("dp")
    me = lax.axis_index("member")
    own = source[me] == me

    up_bf, down_bf = exploit_rows((up_param[0], down_param[0]), source, members, 0)
    moments = (up_first[0], down_first[0], up_second[0], down_second[0])
    batch_total = tokens.shape[1] * shards
    picked, up_full, down_full, normed, preact, activated, delta = exploit_gather(
        moments, (up_bf, down_bf), source, tokens[0], labels[0], classifier, batch_total,
        members, shards, 1,
    )
    up_share, down_share, up_mom, down_mom, up_var_bf, down_var_bf = scatter_with_gradients(
        picked, normed, preact, activated, delta, up_full, down_full, 2
    )

    up_now = jnp.where(own, up_param[0], up_bf.astype(jnp.float32))
    down_now = jnp.where(own, down_param[0], down_bf.astype(jnp.float32))
    up_var = jnp.where(own, up_second[0], up_var_bf.astype(jnp.float32))
    down_var = jnp.where(own, down_second[0], down_var_bf.astype(jnp.float32))

    rate_value = learn_rate[0]
    decay_value = weight_decay[0]
    up_new = adamw_step(up_now, up_mom, up_var, up_share, rate_value, decay_value)
    down_new = adamw_step(down_now, down_mom, down_var, down_share, rate_value, decay_value)
    return tuple(value[None] for value in up_new + down_new)


def solution(mesh):
    placed = (
        P("member", "dp", None, None),
        P("member", "dp"),
        P(),
        P("member"),
        P("member"),
        P(),
        P("member", "dp", None),
        P("member", "dp", None),
        P("member", "dp", None),
        P("member", "dp", None),
        P("member", "dp", None),
        P("member", "dp", None),
    )
    return jax.shard_map(
        per_device,
        mesh=mesh,
        in_specs=placed,
        out_specs=(P("member", "dp", None),) * 6,
        check_vma=False,
    )
```

```python
import functools

import jax
import jax.numpy as jnp
from jax import lax
from jax.experimental import pallas as pl
from jax.experimental.pallas import tpu as pltpu
from jax.sharding import PartitionSpec as P

MESH_ID = pl.DeviceIdType.MESH

STEP = 1000


def local_gradients(tokens, labels, up_weight, down_weight, classifier, batch_total):
    images, patches, features = tokens.shape
    hidden_units = up_weight.shape[1]
    token_rows = tokens.reshape(images * patches, features).astype(jnp.float32)
    center = token_rows - jnp.mean(token_rows, axis=1, keepdims=True)
    normed = (center * lax.rsqrt(jnp.mean(center * center, axis=1, keepdims=True) + 1e-06)).astype(
        jnp.bfloat16
    )
    preact = jnp.dot(normed, up_weight, preferred_element_type=jnp.float32) * features ** (-0.5)
    activated = (0.5 * preact * (1.0 + lax.erf(preact * 0.7071067811865476))).astype(jnp.bfloat16)
    residual = token_rows + jnp.dot(
        activated, down_weight, preferred_element_type=jnp.float32
    ) * hidden_units ** (-0.5)
    out_center = residual - jnp.mean(residual, axis=1, keepdims=True)
    inverse = lax.rsqrt(jnp.mean(out_center * out_center, axis=1, keepdims=True) + 1e-06)
    out_normed = out_center * inverse
    pooled = jnp.mean(out_normed.reshape(images, patches, features), axis=1).astype(jnp.bfloat16)
    logits = jnp.dot(pooled, classifier, preferred_element_type=jnp.float32)
    powered = jnp.exp(logits)
    softmax_out = powered / jnp.sum(powered, axis=1, keepdims=True)
    onehot = (labels[:, None] == jnp.arange(classifier.shape[1], dtype=jnp.int32)[None, :]).astype(
        jnp.float32
    )
    logit_delta = ((softmax_out - onehot) / batch_total).astype(jnp.bfloat16)
    pool_delta = (
        lax.dot_general(
            logit_delta, classifier, (((1,), (1,)), ((), ())), preferred_element_type=jnp.float32
        )
        / patches
    )
    token_delta = jnp.broadcast_to(pool_delta[:, None, :], (images, patches, features)).reshape(
        images * patches, features
    )
    residual_delta = inverse * (
        token_delta
        - jnp.mean(token_delta, axis=1, keepdims=True)
        - out_normed * jnp.mean(token_delta * out_normed, axis=1, keepdims=True)
    )
    residual_delta = residual_delta.astype(jnp.bfloat16)
    down_scale = hidden_units ** (-0.5)
    down_gradient = (
        lax.dot_general(
            activated, residual_delta, (((0,), (0,)), ((), ())), preferred_element_type=jnp.float32
        )
        * down_scale
    )
    hidden_delta = (
        lax.dot_general(
            residual_delta,
            down_weight,
            (((1,), (1,)), ((), ())),
            preferred_element_type=jnp.float32,
        )
        * down_scale
    )
    derivative = (
        0.5 * (1.0 + lax.erf(preact * 0.7071067811865476))
        + preact * jnp.exp(-0.5 * preact * preact) * 0.3989422804014327
    )
    preact_delta = (hidden_delta * derivative).astype(jnp.bfloat16)
    up_gradient = lax.dot_general(
        normed, preact_delta, (((0,), (0,)), ((), ())), preferred_element_type=jnp.float32
    ) * features ** (-0.5)
    return (up_gradient, down_gradient)


def adamw_step(param, first, second, gradient, rate_value, decay_value):
    moment = 0.9 * first.astype(jnp.float32) + 0.1 * gradient
    variance = 0.999 * second + 0.001 * gradient * gradient
    update = (
        moment / (1.0 - 0.9**STEP) / (jnp.sqrt(variance / (1.0 - 0.999**STEP)) + 1e-08)
        + decay_value * param
    )
    return (param - rate_value * update, moment.astype(jnp.bfloat16), variance)


def enter(n, me):
    barrier = pltpu.get_barrier_semaphore()

    def greet(k, carry):
        pl.semaphore_signal(
            barrier, inc=1, device_id={"member": lax.rem(me + k, n)}, device_id_type=MESH_ID
        )
        return carry

    lax.fori_loop(1, n, greet, 0)
    pl.semaphore_wait(barrier, n - 1)


def transpose(n, me, src, dst, send_sem, recv_sem):
    def copy(k):
        target = lax.rem(me + k, n)
        return pltpu.make_async_remote_copy(
            src_ref=src.at[target],
            dst_ref=dst.at[me],
            send_sem=send_sem.at[k],
            recv_sem=recv_sem.at[k],
            device_id={"member": target},
            device_id_type=MESH_ID,
        )

    def start(k, carry):
        copy(k).start()
        return carry

    def finish(k, carry):
        copy(k).wait()
        return carry

    lax.fori_loop(1, n, start, 0)
    dst[me] = src[me]
    lax.fori_loop(1, n, finish, 0)


def pick_rows(n, source_ref, held, picked):
    def pick(i, carry):
        picked[i] = held[source_ref[i]]
        return carry

    lax.fori_loop(0, n, pick, 0)


def exploit_kernel(n, source_ref, send_ref, out_ref, held, picked, send1, recv1, send2, recv2):
    me = lax.axis_index("member")
    enter(n, me)
    transpose(n, me, send_ref, held, send1, recv1)
    pick_rows(n, source_ref, held, picked)
    transpose(n, me, picked, out_ref, send2, recv2)


def gather_kernel(n, batch_total, patches, source_ref, labels_ref, up_ref, down_ref, tokens_ref,
                  classifier_ref, *refs):
    parts = refs[:-17]
    (out_ref, up_full, down_full, normed_ref, preact_ref, act_ref, delta_ref,
     flat, held, send1, recv1,
     near_send, near_recv, far_send, far_recv, fwd_send, fwd_recv) = refs[-17:]
    me = lax.axis_index("member")
    shard = lax.axis_index("dp")
    core = shard % 2
    chip = shard // 2
    partner = chip * 2 + (1 - core)
    across = (1 - chip) * 2 + core
    lanes = flat.shape[1]
    chunk = held.shape[1]
    offset = 0
    for part in parts:
        rows, cols = part.shape
        for block in range(cols // lanes):
            flat[pl.ds(offset, rows), :] = part[:, pl.ds(block * lanes, lanes)].astype(flat.dtype)
            offset += rows

    barrier = pltpu.get_barrier_semaphore()

    def greet(k, carry):
        pl.semaphore_signal(
            barrier, inc=1, device_id={"member": lax.rem(me + k, n)}, device_id_type=MESH_ID
        )
        return carry

    lax.fori_loop(1, n, greet, 0)
    for peer in (partner, across):
        pl.semaphore_signal(barrier, inc=1, device_id={"dp": peer}, device_id_type=MESH_ID)
    pl.semaphore_wait(barrier, n - 1 + 2)

    def rows_of(full, index):
        size = full.shape[0] // 4
        return full.at[pl.ds(pl.multiple_of(index * size, size), size)]

    def dp_copy(src, dst, send, recv, slot, peer):
        return pltpu.make_async_remote_copy(
            src_ref=src, dst_ref=dst, send_sem=send.at[slot], recv_sem=recv.at[slot],
            device_id={"dp": peer}, device_id_type=MESH_ID,
        )

    shares = ((up_ref, up_full), (down_ref, down_full))
    far = [dp_copy(share, rows_of(full, shard), far_send, far_recv, slot, across)
           for slot, (share, full) in enumerate(shares)]
    near = [dp_copy(share, rows_of(full, shard), near_send, near_recv, slot, partner)
            for slot, (share, full) in enumerate(shares)]
    for item in far + near:
        item.start()

    def copy(k):
        target = lax.rem(me + k, n)
        return pltpu.make_async_remote_copy(
            src_ref=flat.at[pl.ds(pl.multiple_of(target * chunk, 16), chunk)],
            dst_ref=held.at[me],
            send_sem=send1.at[k],
            recv_sem=recv1.at[k],
            device_id={"member": target},
            device_id_type=MESH_ID,
        )

    def start(k, carry):
        copy(k).start()
        return carry

    def finish(k, carry):
        copy(k).wait()
        return carry

    lax.fori_loop(1, n, start, 0)
    held[me] = flat[pl.ds(pl.multiple_of(me * chunk, 16), chunk)]
    for share, full in shares:
        rows_of(full, shard)[...] = share[...]
    for item in far:
        item.wait()
    forward = [dp_copy(rows_of(full, across), rows_of(full, across), fwd_send, fwd_recv, slot,
                       partner)
               for slot, (share, full) in enumerate(shares)]
    for item in forward:
        item.start()
    for item in near + forward:
        item.wait()
    normed, preact, activated, delta = forward_half(
        tokens_ref[...], labels_ref, up_full[...], down_full[...], classifier_ref[...],
        batch_total, patches,
    )
    normed_ref[...] = normed
    preact_ref[...] = preact
    act_ref[...] = activated
    delta_ref[...] = delta
    lax.fori_loop(1, n, finish, 0)
    pick_rows(n, source_ref, held, out_ref)


def scatter_kernel(n, send_ref, out_ref, send1, recv1):
    me = lax.axis_index("member")
    enter(n, me)
    transpose(n, me, send_ref, out_ref, send1, recv1)


def forward_half(tokens, labels_ref, up_weight, down_weight, classifier, batch_total, patches):
    tokens_n, features = tokens.shape
    hidden_units = up_weight.shape[1]
    classes = classifier.shape[1]
    images = tokens_n // patches
    token_rows = tokens.astype(jnp.float32)
    center = token_rows - jnp.mean(token_rows, axis=1, keepdims=True)
    normed = (center * lax.rsqrt(jnp.mean(center * center, axis=1, keepdims=True) + 1e-06)).astype(
        jnp.bfloat16
    )
    preact = jnp.dot(normed, up_weight, preferred_element_type=jnp.float32) * features ** (-0.5)
    activated = (0.5 * preact * (1.0 + lax.erf(preact * 0.7071067811865476))).astype(jnp.bfloat16)
    residual = token_rows + jnp.dot(
        activated, down_weight, preferred_element_type=jnp.float32
    ) * hidden_units ** (-0.5)
    out_center = residual - jnp.mean(residual, axis=1, keepdims=True)
    inverse = lax.rsqrt(jnp.mean(out_center * out_center, axis=1, keepdims=True) + 1e-06)
    out_normed = out_center * inverse
    image_of_row = lax.broadcasted_iota(jnp.int32, (tokens_n, 1), 0) // patches
    pooled = jnp.concatenate(
        [
            jnp.sum(jnp.where(image_of_row == i, out_normed, 0.0), axis=0, keepdims=True)
            for i in range(images)
        ],
        axis=0,
    ) / patches
    pooled = pooled.astype(jnp.bfloat16)
    logits = jnp.dot(pooled, classifier, preferred_element_type=jnp.float32)
    powered = jnp.exp(logits)
    softmax_out = powered / jnp.sum(powered, axis=1, keepdims=True)
    row = lax.broadcasted_iota(jnp.int32, (images, classes), 0)
    column = lax.broadcasted_iota(jnp.int32, (images, classes), 1)
    label = jnp.zeros((images, classes), jnp.int32)
    for i in range(images):
        label = jnp.where(row == i, labels_ref[i], label)
    onehot = (column == label).astype(jnp.float32)
    logit_delta = ((softmax_out - onehot) / batch_total).astype(jnp.bfloat16)
    pool_delta = (
        lax.dot_general(
            logit_delta, classifier, (((1,), (1,)), ((), ())), preferred_element_type=jnp.float32
        )
        / patches
    )
    token_delta = jnp.zeros((tokens_n, features), jnp.float32)
    for i in range(images):
        token_delta = jnp.where(image_of_row == i, pool_delta[i:i + 1, :], token_delta)
    residual_delta = inverse * (
        token_delta
        - jnp.mean(token_delta, axis=1, keepdims=True)
        - out_normed * jnp.mean(token_delta * out_normed, axis=1, keepdims=True)
    )
    residual_delta = residual_delta.astype(jnp.bfloat16)
    return normed, preact, activated, residual_delta


def backward_half(normed, preact, activated, residual_delta, down_weight):
    features = normed.shape[1]
    hidden_units = preact.shape[1]
    down_scale = hidden_units ** (-0.5)
    down_gradient = (
        lax.dot_general(
            activated, residual_delta, (((0,), (0,)), ((), ())), preferred_element_type=jnp.float32
        )
        * down_scale
    )
    hidden_delta = (
        lax.dot_general(
            residual_delta, down_weight, (((1,), (1,)), ((), ())), preferred_element_type=jnp.float32
        )
        * down_scale
    )
    derivative = (
        0.5 * (1.0 + lax.erf(preact * 0.7071067811865476))
        + preact * jnp.exp(-0.5 * preact * preact) * 0.3989422804014327
    )
    preact_delta = (hidden_delta * derivative).astype(jnp.bfloat16)
    up_gradient = lax.dot_general(
        normed, preact_delta, (((0,), (0,)), ((), ())), preferred_element_type=jnp.float32
    ) * features ** (-0.5)
    return up_gradient, down_gradient


def scatter_compute_kernel(
    n, send_ref, normed_ref, preact_ref, act_ref, delta_ref, down_ref,
    up_share_ref, down_share_ref, up_first_ref, down_first_ref, up_second_ref, down_second_ref,
    flat, up_term, down_term, up_near, down_near, up_part, down_part, up_far, down_far,
    send_sem, recv_sem, near_send, near_recv, far_send, far_recv,
):
    me = lax.axis_index("member")
    shard = lax.axis_index("dp")
    core = shard % 2
    chip = shard // 2
    partner = chip * 2 + (1 - core)
    across = (1 - chip) * 2 + core
    diagonal = (1 - chip) * 2 + (1 - core)

    barrier = pltpu.get_barrier_semaphore()

    def greet(k, carry):
        pl.semaphore_signal(
            barrier, inc=1, device_id={"member": lax.rem(me + k, n)}, device_id_type=MESH_ID
        )
        return carry

    lax.fori_loop(1, n, greet, 0)
    for peer in (partner, across, diagonal):
        pl.semaphore_signal(barrier, inc=1, device_id={"dp": peer}, device_id_type=MESH_ID)
    pl.semaphore_wait(barrier, n - 1 + 3)

    chunk = send_ref.shape[1]

    def copy(k):
        target = lax.rem(me + k, n)
        return pltpu.make_async_remote_copy(
            src_ref=send_ref.at[target],
            dst_ref=flat.at[pl.ds(pl.multiple_of(me * chunk, 16), chunk)],
            send_sem=send_sem.at[k],
            recv_sem=recv_sem.at[k],
            device_id={"member": target},
            device_id_type=MESH_ID,
        )

    def start(k, carry):
        copy(k).start()
        return carry

    def finish(k, carry):
        copy(k).wait()
        return carry

    lax.fori_loop(1, n, start, 0)
    flat[pl.ds(pl.multiple_of(me * chunk, 16), chunk)] = send_ref[me]
    up_gradient, down_gradient = backward_half(
        normed_ref[...], preact_ref[...], act_ref[...], delta_ref[...], down_ref[...]
    )
    up_term[...] = up_gradient.astype(jnp.bfloat16)
    down_term[...] = down_gradient.astype(jnp.bfloat16)

    def rows(term, index):
        size = term.shape[0] // 4
        return term.at[pl.ds(pl.multiple_of(index * size, size), size)]

    near = []
    slot = 0
    for term, near_buf in ((up_term, up_near), (down_term, down_near)):
        for which, index in ((0, diagonal), (1, partner)):
            near.append(
                pltpu.make_async_remote_copy(
                    src_ref=rows(term, index),
                    dst_ref=near_buf.at[which],
                    send_sem=near_send.at[slot],
                    recv_sem=near_recv.at[slot],
                    device_id={"dp": partner},
                    device_id_type=MESH_ID,
                )
            )
            slot += 1
    for item in near:
        item.start()
    for item in near:
        item.wait()

    far = []
    slot = 0
    for term, near_buf, part, far_buf in (
        (up_term, up_near, up_part, up_far),
        (down_term, down_near, down_part, down_far),
    ):
        part[...] = (
            rows(term, across)[...].astype(jnp.float32) + near_buf[0].astype(jnp.float32)
        ).astype(jnp.bfloat16)
        far.append(
            pltpu.make_async_remote_copy(
                src_ref=part,
                dst_ref=far_buf,
                send_sem=far_send.at[slot],
                recv_sem=far_recv.at[slot],
                device_id={"dp": across},
                device_id_type=MESH_ID,
            )
        )
        slot += 1
    for item in far:
        item.start()
    for item in far:
        item.wait()

    for term, near_buf, far_buf, share in (
        (up_term, up_near, up_far, up_share_ref),
        (down_term, down_near, down_far, down_share_ref),
    ):
        share[...] = (
            rows(term, shard)[...].astype(jnp.float32)
            + near_buf[1].astype(jnp.float32)
            + far_buf[...].astype(jnp.float32)
        )
    lax.fori_loop(1, n, finish, 0)
    lanes = flat.shape[1]
    offset = 0
    for part in (up_first_ref, down_first_ref, up_second_ref, down_second_ref):
        rows, cols = part.shape
        for block in range(cols // lanes):
            part[:, pl.ds(block * lanes, lanes)] = flat[pl.ds(offset, rows), :]
            offset += rows


def scatter_with_gradients(picked, normed, preact, activated, delta, up_full, down_full,
                           kernel_id):
    n = picked.shape[0]
    tokens_n, features = normed.shape
    vmem = pl.BlockSpec(memory_space=pltpu.VMEM)
    moved = picked.size * picked.dtype.itemsize
    flops = 6 * tokens_n * features * up_full.shape[1]
    up_rows = (up_full.shape[0] // 4, up_full.shape[1])
    down_rows = (down_full.shape[0] // 4, down_full.shape[1])
    bf16 = jnp.bfloat16
    return pl.pallas_call(
        functools.partial(scatter_compute_kernel, n),
        out_shape=(
            jax.ShapeDtypeStruct(up_rows, jnp.float32),
            jax.ShapeDtypeStruct(down_rows, jnp.float32),
        ) + tuple(jax.ShapeDtypeStruct(shape, bf16) for shape in (up_rows, down_rows) * 2),
        in_specs=[vmem] * 6,
        out_specs=(vmem,) * 6,
        scratch_shapes=[
            pltpu.VMEM((picked.shape[0] * picked.shape[1], picked.shape[2]), bf16),
            pltpu.VMEM(up_full.shape, bf16),
            pltpu.VMEM(down_full.shape, bf16),
            pltpu.VMEM((2,) + up_rows, bf16),
            pltpu.VMEM((2,) + down_rows, bf16),
            pltpu.VMEM(up_rows, bf16),
            pltpu.VMEM(down_rows, bf16),
            pltpu.VMEM(up_rows, bf16),
            pltpu.VMEM(down_rows, bf16),
            pltpu.SemaphoreType.DMA((n,)),
            pltpu.SemaphoreType.DMA((n,)),
            pltpu.SemaphoreType.DMA((4,)),
            pltpu.SemaphoreType.DMA((4,)),
            pltpu.SemaphoreType.DMA((2,)),
            pltpu.SemaphoreType.DMA((2,)),
        ],
        compiler_params=pltpu.CompilerParams(
            collective_id=kernel_id, has_side_effects=True, vmem_limit_bytes=63 * 1024 * 1024
        ),
        cost_estimate=pl.CostEstimate(flops=flops, transcendentals=0, bytes_accessed=moved * 20),
    )(picked, normed, preact, activated, delta, down_full)


def member_call(body, packed, operands, scratch, kernel_id):
    n, rows, lanes = packed.shape
    moved = packed.size * packed.dtype.itemsize
    smem = [pl.BlockSpec(memory_space=pltpu.SMEM)] * (len(operands) - 1)
    return pl.pallas_call(
        functools.partial(body, n),
        out_shape=jax.ShapeDtypeStruct(packed.shape, packed.dtype),
        in_specs=smem + [pl.BlockSpec(memory_space=pltpu.VMEM)],
        out_specs=pl.BlockSpec(memory_space=pltpu.VMEM),
        scratch_shapes=scratch,
        compiler_params=pltpu.CompilerParams(
            collective_id=kernel_id, has_side_effects=True, vmem_limit_bytes=48 * 1024 * 1024
        ),
        cost_estimate=pl.CostEstimate(flops=0, transcendentals=0, bytes_accessed=moved * 20),
    )(*operands)


def exploit_transfer(packed, source, kernel_id):
    n, rows, lanes = packed.shape
    block = pltpu.VMEM((n, rows, lanes), packed.dtype)
    sems = [pltpu.SemaphoreType.DMA((n,))] * 4
    return member_call(exploit_kernel, packed, (source, packed), [block, block] + sems, kernel_id)


def exploit_gather(parts, shares, source, tokens, labels, classifier, batch_total, members,
                   shards, kernel_id):
    images, patches, features = tokens.shape
    tokens_n = images * patches
    hidden = shares[0].shape[1]
    lanes = 128
    total = sum(part.size for part in parts) // lanes
    shape = (members, total // members, lanes)
    vmem = pl.BlockSpec(memory_space=pltpu.VMEM)
    moved = total * lanes * 2
    fulls = [jax.ShapeDtypeStruct((share.shape[0] * shards, share.shape[1]), share.dtype)
             for share in shares]
    sems = [pltpu.SemaphoreType.DMA((len(shares),))] * 6
    return pl.pallas_call(
        functools.partial(gather_kernel, members, batch_total, patches),
        out_shape=(
            jax.ShapeDtypeStruct(shape, jnp.bfloat16),
            *fulls,
            jax.ShapeDtypeStruct((tokens_n, features), jnp.bfloat16),
            jax.ShapeDtypeStruct((tokens_n, hidden), jnp.float32),
            jax.ShapeDtypeStruct((tokens_n, hidden), jnp.bfloat16),
            jax.ShapeDtypeStruct((tokens_n, features), jnp.bfloat16),
        ),
        in_specs=[pl.BlockSpec(memory_space=pltpu.SMEM)] * 2
        + [vmem] * (len(shares) + 2 + len(parts)),
        out_specs=(vmem,) * 7,
        scratch_shapes=[
            pltpu.VMEM((total, lanes), jnp.bfloat16),
            pltpu.VMEM(shape, jnp.bfloat16),
            pltpu.SemaphoreType.DMA((members,)),
            pltpu.SemaphoreType.DMA((members,)),
        ] + sems,
        compiler_params=pltpu.CompilerParams(
            collective_id=kernel_id, has_side_effects=True, vmem_limit_bytes=63 * 1024 * 1024
        ),
        cost_estimate=pl.CostEstimate(flops=0, transcendentals=0, bytes_accessed=moved * 20),
    )(source, labels, *shares, tokens.reshape(tokens_n, features), classifier, *parts)


def exploit_scatter(packed, kernel_id):
    n = packed.shape[0]
    sems = [pltpu.SemaphoreType.DMA((n,))] * 2
    return member_call(scatter_kernel, packed, (packed,), sems, kernel_id)


def lane_major(part, lanes):
    rows, cols = part.shape
    return part.reshape(rows, cols // lanes, lanes).transpose(1, 0, 2).reshape(-1, lanes)


def from_lane_major(flat, shape, lanes):
    rows, cols = shape
    return flat.reshape(cols // lanes, rows, lanes).transpose(1, 0, 2).reshape(rows, cols)


def exploit_rows(parts, source, members, kernel_id):
    lanes = 128
    rows = [part.size // (members * lanes) for part in parts]
    pad = 0
    pieces = [part.astype(jnp.bfloat16).reshape(members, -1, lanes) for part in parts]
    if pad:
        pieces.append(jnp.zeros((members, pad, lanes), jnp.bfloat16))
    back = exploit_transfer(jnp.concatenate(pieces, axis=1), source, kernel_id)
    out = []
    start = 0
    for part, count in zip(parts, rows):
        out.append(back[:, start:start + count].reshape(part.shape))
        start += count
    return out


def pack_tiles(parts, members):
    lanes = 128
    flat = jnp.concatenate([lane_major(part.astype(jnp.bfloat16), lanes) for part in parts])
    return flat.reshape(members, -1, flat.shape[-1])


def unpack_tiles(back, parts):
    lanes = back.shape[-1]
    back = back.reshape(-1, lanes)
    out = []
    start = 0
    for part in parts:
        count = part.size // lanes
        out.append(from_lane_major(back[start:start + count], part.shape, lanes))
        start += count
    return out


def per_device(
    tokens,
    labels,
    source,
    learn_rate,
    weight_decay,
    classifier,
    up_param,
    up_first,
    up_second,
    down_param,
    down_first,
    down_second,
):
    members = lax.axis_size("member")
    shards = lax.axis_size("dp")
    me = lax.axis_index("member")
    own = source[me] == me

    up_bf, down_bf = exploit_rows((up_param[0], down_param[0]), source, members, 0)
    moments = (up_first[0], down_first[0], up_second[0], down_second[0])
    batch_total = tokens.shape[1] * shards
    picked, up_full, down_full, normed, preact, activated, delta = exploit_gather(
        moments, (up_bf, down_bf), source, tokens[0], labels[0], classifier, batch_total,
        members, shards, 1,
    )
    up_share, down_share, up_mom, down_mom, up_var_bf, down_var_bf = scatter_with_gradients(
        picked, normed, preact, activated, delta, up_full, down_full, 2
    )

    up_now = jnp.where(own, up_param[0], up_bf.astype(jnp.float32))
    down_now = jnp.where(own, down_param[0], down_bf.astype(jnp.float32))
    up_var = jnp.where(own, up_second[0], up_var_bf.astype(jnp.float32))
    down_var = jnp.where(own, down_second[0], down_var_bf.astype(jnp.float32))

    rate_value = learn_rate[0]
    decay_value = weight_decay[0]
    up_new = adamw_step(up_now, up_mom, up_var, up_share, rate_value, decay_value)
    down_new = adamw_step(down_now, down_mom, down_var, down_share, rate_value, decay_value)
    return tuple(value[None] for value in up_new + down_new)


def solution(mesh):
    placed = (
        P("member", "dp", None, None),
        P("member", "dp"),
        P(),
        P("member"),
        P("member"),
        P(),
        P("member", "dp", None),
        P("member", "dp", None),
        P("member", "dp", None),
        P("member", "dp", None),
        P("member", "dp", None),
        P("member", "dp", None),
    )
    return jax.shard_map(
        per_device,
        mesh=mesh,
        in_specs=placed,
        out_specs=(P("member", "dp", None),) * 6,
        check_vma=False,
    )
```

```python
import functools

import jax
import jax.numpy as jnp
from jax import lax
from jax.experimental import pallas as pl
from jax.experimental.pallas import tpu as pltpu
from jax.sharding import PartitionSpec as P

MESH_ID = pl.DeviceIdType.MESH

STEP = 1000


def local_gradients(tokens, labels, up_weight, down_weight, classifier, batch_total):
    images, patches, features = tokens.shape
    hidden_units = up_weight.shape[1]
    token_rows = tokens.reshape(images * patches, features).astype(jnp.float32)
    center = token_rows - jnp.mean(token_rows, axis=1, keepdims=True)
    normed = (center * lax.rsqrt(jnp.mean(center * center, axis=1, keepdims=True) + 1e-06)).astype(
        jnp.bfloat16
    )
    preact = jnp.dot(normed, up_weight, preferred_element_type=jnp.float32) * features ** (-0.5)
    activated = (0.5 * preact * (1.0 + lax.erf(preact * 0.7071067811865476))).astype(jnp.bfloat16)
    residual = token_rows + jnp.dot(
        activated, down_weight, preferred_element_type=jnp.float32
    ) * hidden_units ** (-0.5)
    out_center = residual - jnp.mean(residual, axis=1, keepdims=True)
    inverse = lax.rsqrt(jnp.mean(out_center * out_center, axis=1, keepdims=True) + 1e-06)
    out_normed = out_center * inverse
    pooled = jnp.mean(out_normed.reshape(images, patches, features), axis=1).astype(jnp.bfloat16)
    logits = jnp.dot(pooled, classifier, preferred_element_type=jnp.float32)
    powered = jnp.exp(logits)
    softmax_out = powered / jnp.sum(powered, axis=1, keepdims=True)
    onehot = (labels[:, None] == jnp.arange(classifier.shape[1], dtype=jnp.int32)[None, :]).astype(
        jnp.float32
    )
    logit_delta = ((softmax_out - onehot) / batch_total).astype(jnp.bfloat16)
    pool_delta = (
        lax.dot_general(
            logit_delta, classifier, (((1,), (1,)), ((), ())), preferred_element_type=jnp.float32
        )
        / patches
    )
    token_delta = jnp.broadcast_to(pool_delta[:, None, :], (images, patches, features)).reshape(
        images * patches, features
    )
    residual_delta = inverse * (
        token_delta
        - jnp.mean(token_delta, axis=1, keepdims=True)
        - out_normed * jnp.mean(token_delta * out_normed, axis=1, keepdims=True)
    )
    residual_delta = residual_delta.astype(jnp.bfloat16)
    down_scale = hidden_units ** (-0.5)
    down_gradient = (
        lax.dot_general(
            activated, residual_delta, (((0,), (0,)), ((), ())), preferred_element_type=jnp.float32
        )
        * down_scale
    )
    hidden_delta = (
        lax.dot_general(
            residual_delta,
            down_weight,
            (((1,), (1,)), ((), ())),
            preferred_element_type=jnp.float32,
        )
        * down_scale
    )
    derivative = (
        0.5 * (1.0 + lax.erf(preact * 0.7071067811865476))
        + preact * jnp.exp(-0.5 * preact * preact) * 0.3989422804014327
    )
    preact_delta = (hidden_delta * derivative).astype(jnp.bfloat16)
    up_gradient = lax.dot_general(
        normed, preact_delta, (((0,), (0,)), ((), ())), preferred_element_type=jnp.float32
    ) * features ** (-0.5)
    return (up_gradient, down_gradient)


def adamw_step(param, first, second, gradient, rate_value, decay_value):
    moment = 0.9 * first.astype(jnp.float32) + 0.1 * gradient
    variance = 0.999 * second + 0.001 * gradient * gradient
    update = (
        moment / (1.0 - 0.9**STEP) / (jnp.sqrt(variance / (1.0 - 0.999**STEP)) + 1e-08)
        + decay_value * param
    )
    return (param - rate_value * update, moment.astype(jnp.bfloat16), variance)


def enter(n, me):
    barrier = pltpu.get_barrier_semaphore()

    def greet(k, carry):
        pl.semaphore_signal(
            barrier, inc=1, device_id={"member": lax.rem(me + k, n)}, device_id_type=MESH_ID
        )
        return carry

    lax.fori_loop(1, n, greet, 0)
    pl.semaphore_wait(barrier, n - 1)


def transpose(n, me, src, dst, send_sem, recv_sem):
    def copy(k):
        target = lax.rem(me + k, n)
        return pltpu.make_async_remote_copy(
            src_ref=src.at[target],
            dst_ref=dst.at[me],
            send_sem=send_sem.at[k],
            recv_sem=recv_sem.at[k],
            device_id={"member": target},
            device_id_type=MESH_ID,
        )

    def start(k, carry):
        copy(k).start()
        return carry

    def finish(k, carry):
        copy(k).wait()
        return carry

    lax.fori_loop(1, n, start, 0)
    dst[me] = src[me]
    lax.fori_loop(1, n, finish, 0)


def pick_rows(n, source_ref, held, picked):
    def pick(i, carry):
        picked[i] = held[source_ref[i]]
        return carry

    lax.fori_loop(0, n, pick, 0)


def exploit_kernel(n, source_ref, send_ref, out_ref, held, picked, send1, recv1, send2, recv2):
    me = lax.axis_index("member")
    enter(n, me)
    transpose(n, me, send_ref, held, send1, recv1)
    pick_rows(n, source_ref, held, picked)
    transpose(n, me, picked, out_ref, send2, recv2)


def gather_kernel(n, batch_total, patches, source_ref, labels_ref, up_ref, down_ref, tokens_ref,
                  classifier_ref, *refs):
    parts = refs[:-17]
    (out_ref, up_full, down_full, normed_ref, preact_ref, act_ref, delta_ref,
     flat, held, send1, recv1,
     near_send, near_recv, far_send, far_recv, fwd_send, fwd_recv) = refs[-17:]
    me = lax.axis_index("member")
    shard = lax.axis_index("dp")
    core = shard % 2
    chip = shard // 2
    partner = chip * 2 + (1 - core)
    across = (1 - chip) * 2 + core
    lanes = flat.shape[1]
    chunk = held.shape[1]
    offset = 0
    for part in parts:
        rows, cols = part.shape
        for block in range(cols // lanes):
            flat[pl.ds(offset, rows), :] = part[:, pl.ds(block * lanes, lanes)].astype(flat.dtype)
            offset += rows

    barrier = pltpu.get_barrier_semaphore()

    def greet(k, carry):
        pl.semaphore_signal(
            barrier, inc=1, device_id={"member": lax.rem(me + k, n)}, device_id_type=MESH_ID
        )
        return carry

    lax.fori_loop(1, n, greet, 0)
    for peer in (partner, across):
        pl.semaphore_signal(barrier, inc=1, device_id={"dp": peer}, device_id_type=MESH_ID)
    pl.semaphore_wait(barrier, n - 1 + 2)

    def rows_of(full, index):
        size = full.shape[0] // 4
        return full.at[pl.ds(pl.multiple_of(index * size, size), size)]

    def dp_copy(src, dst, send, recv, slot, peer):
        return pltpu.make_async_remote_copy(
            src_ref=src, dst_ref=dst, send_sem=send.at[slot], recv_sem=recv.at[slot],
            device_id={"dp": peer}, device_id_type=MESH_ID,
        )

    shares = ((up_ref, up_full), (down_ref, down_full))
    far = [dp_copy(share, rows_of(full, shard), far_send, far_recv, slot, across)
           for slot, (share, full) in enumerate(shares)]
    near = [dp_copy(share, rows_of(full, shard), near_send, near_recv, slot, partner)
            for slot, (share, full) in enumerate(shares)]
    for item in far + near:
        item.start()

    def copy(k):
        target = lax.rem(me + k, n)
        return pltpu.make_async_remote_copy(
            src_ref=flat.at[pl.ds(pl.multiple_of(target * chunk, 16), chunk)],
            dst_ref=held.at[me],
            send_sem=send1.at[k],
            recv_sem=recv1.at[k],
            device_id={"member": target},
            device_id_type=MESH_ID,
        )

    def start(k, carry):
        copy(k).start()
        return carry

    def finish(k, carry):
        copy(k).wait()
        return carry

    lax.fori_loop(1, n, start, 0)
    held[me] = flat[pl.ds(pl.multiple_of(me * chunk, 16), chunk)]
    for share, full in shares:
        rows_of(full, shard)[...] = share[...]
    for item in far:
        item.wait()
    forward = [dp_copy(rows_of(full, across), rows_of(full, across), fwd_send, fwd_recv, slot,
                       partner)
               for slot, (share, full) in enumerate(shares)]
    for item in forward:
        item.start()
    for item in near + forward:
        item.wait()
    normed, preact, activated, delta = forward_half(
        tokens_ref[...], labels_ref, up_full[...], down_full[...], classifier_ref[...],
        batch_total, patches,
    )
    normed_ref[...] = normed
    preact_ref[...] = preact
    act_ref[...] = activated
    delta_ref[...] = delta
    lax.fori_loop(1, n, finish, 0)
    pick_rows(n, source_ref, held, out_ref)


def scatter_kernel(n, send_ref, out_ref, send1, recv1):
    me = lax.axis_index("member")
    enter(n, me)
    transpose(n, me, send_ref, out_ref, send1, recv1)


def forward_half(tokens, labels_ref, up_weight, down_weight, classifier, batch_total, patches):
    tokens_n, features = tokens.shape
    hidden_units = up_weight.shape[1]
    classes = classifier.shape[1]
    images = tokens_n // patches
    token_rows = tokens.astype(jnp.float32)
    center = token_rows - jnp.mean(token_rows, axis=1, keepdims=True)
    normed = (center * lax.rsqrt(jnp.mean(center * center, axis=1, keepdims=True) + 1e-06)).astype(
        jnp.bfloat16
    )
    preact = jnp.dot(normed, up_weight, preferred_element_type=jnp.float32) * features ** (-0.5)
    activated = (0.5 * preact * (1.0 + lax.erf(preact * 0.7071067811865476))).astype(jnp.bfloat16)
    residual = token_rows + jnp.dot(
        activated, down_weight, preferred_element_type=jnp.float32
    ) * hidden_units ** (-0.5)
    out_center = residual - jnp.mean(residual, axis=1, keepdims=True)
    inverse = lax.rsqrt(jnp.mean(out_center * out_center, axis=1, keepdims=True) + 1e-06)
    out_normed = out_center * inverse
    image_of_row = lax.broadcasted_iota(jnp.int32, (tokens_n, 1), 0) // patches
    pooled = jnp.concatenate(
        [
            jnp.sum(jnp.where(image_of_row == i, out_normed, 0.0), axis=0, keepdims=True)
            for i in range(images)
        ],
        axis=0,
    ) / patches
    pooled = pooled.astype(jnp.bfloat16)
    logits = jnp.dot(pooled, classifier, preferred_element_type=jnp.float32)
    powered = jnp.exp(logits)
    softmax_out = powered / jnp.sum(powered, axis=1, keepdims=True)
    row = lax.broadcasted_iota(jnp.int32, (images, classes), 0)
    column = lax.broadcasted_iota(jnp.int32, (images, classes), 1)
    label = jnp.zeros((images, classes), jnp.int32)
    for i in range(images):
        label = jnp.where(row == i, labels_ref[i], label)
    onehot = (column == label).astype(jnp.float32)
    logit_delta = ((softmax_out - onehot) / batch_total).astype(jnp.bfloat16)
    pool_delta = (
        lax.dot_general(
            logit_delta, classifier, (((1,), (1,)), ((), ())), preferred_element_type=jnp.float32
        )
        / patches
    )
    token_delta = jnp.zeros((tokens_n, features), jnp.float32)
    for i in range(images):
        token_delta = jnp.where(image_of_row == i, pool_delta[i:i + 1, :], token_delta)
    residual_delta = inverse * (
        token_delta
        - jnp.mean(token_delta, axis=1, keepdims=True)
        - out_normed * jnp.mean(token_delta * out_normed, axis=1, keepdims=True)
    )
    residual_delta = residual_delta.astype(jnp.bfloat16)
    derivative = (
        0.5 * (1.0 + lax.erf(preact * 0.7071067811865476))
        + preact * jnp.exp(-0.5 * preact * preact) * 0.3989422804014327
    )
    return normed, derivative, activated, residual_delta


def backward_half(normed, derivative, activated, residual_delta, down_weight):
    features = normed.shape[1]
    hidden_units = derivative.shape[1]
    down_scale = hidden_units ** (-0.5)
    down_gradient = (
        lax.dot_general(
            activated, residual_delta, (((0,), (0,)), ((), ())), preferred_element_type=jnp.float32
        )
        * down_scale
    )
    hidden_delta = (
        lax.dot_general(
            residual_delta, down_weight, (((1,), (1,)), ((), ())), preferred_element_type=jnp.float32
        )
        * down_scale
    )
    preact_delta = (hidden_delta * derivative).astype(jnp.bfloat16)
    up_gradient = lax.dot_general(
        normed, preact_delta, (((0,), (0,)), ((), ())), preferred_element_type=jnp.float32
    ) * features ** (-0.5)
    return up_gradient, down_gradient


def scatter_compute_kernel(
    n, send_ref, normed_ref, preact_ref, act_ref, delta_ref, down_ref,
    up_share_ref, down_share_ref, up_first_ref, down_first_ref, up_second_ref, down_second_ref,
    flat, up_term, down_term, up_near, down_near, up_part, down_part, up_far, down_far,
    send_sem, recv_sem, near_send, near_recv, far_send, far_recv,
):
    me = lax.axis_index("member")
    shard = lax.axis_index("dp")
    core = shard % 2
    chip = shard // 2
    partner = chip * 2 + (1 - core)
    across = (1 - chip) * 2 + core
    diagonal = (1 - chip) * 2 + (1 - core)

    barrier = pltpu.get_barrier_semaphore()

    def greet(k, carry):
        pl.semaphore_signal(
            barrier, inc=1, device_id={"member": lax.rem(me + k, n)}, device_id_type=MESH_ID
        )
        return carry

    lax.fori_loop(1, n, greet, 0)
    for peer in (partner, across, diagonal):
        pl.semaphore_signal(barrier, inc=1, device_id={"dp": peer}, device_id_type=MESH_ID)
    pl.semaphore_wait(barrier, n - 1 + 3)

    chunk = send_ref.shape[1]

    def copy(k):
        target = lax.rem(me + k, n)
        return pltpu.make_async_remote_copy(
            src_ref=send_ref.at[target],
            dst_ref=flat.at[pl.ds(pl.multiple_of(me * chunk, 16), chunk)],
            send_sem=send_sem.at[k],
            recv_sem=recv_sem.at[k],
            device_id={"member": target},
            device_id_type=MESH_ID,
        )

    def start(k, carry):
        copy(k).start()
        return carry

    def finish(k, carry):
        copy(k).wait()
        return carry

    lax.fori_loop(1, n, start, 0)
    flat[pl.ds(pl.multiple_of(me * chunk, 16), chunk)] = send_ref[me]
    up_gradient, down_gradient = backward_half(
        normed_ref[...], preact_ref[...], act_ref[...], delta_ref[...], down_ref[...]
    )
    up_term[...] = up_gradient.astype(jnp.bfloat16)
    down_term[...] = down_gradient.astype(jnp.bfloat16)

    def rows(term, index):
        size = term.shape[0] // 4
        return term.at[pl.ds(pl.multiple_of(index * size, size), size)]

    near = []
    slot = 0
    for term, near_buf in ((up_term, up_near), (down_term, down_near)):
        for which, index in ((0, diagonal), (1, partner)):
            near.append(
                pltpu.make_async_remote_copy(
                    src_ref=rows(term, index),
                    dst_ref=near_buf.at[which],
                    send_sem=near_send.at[slot],
                    recv_sem=near_recv.at[slot],
                    device_id={"dp": partner},
                    device_id_type=MESH_ID,
                )
            )
            slot += 1
    for item in near:
        item.start()
    for item in near:
        item.wait()

    far = []
    slot = 0
    for term, near_buf, part, far_buf in (
        (up_term, up_near, up_part, up_far),
        (down_term, down_near, down_part, down_far),
    ):
        part[...] = (
            rows(term, across)[...].astype(jnp.float32) + near_buf[0].astype(jnp.float32)
        ).astype(jnp.bfloat16)
        far.append(
            pltpu.make_async_remote_copy(
                src_ref=part,
                dst_ref=far_buf,
                send_sem=far_send.at[slot],
                recv_sem=far_recv.at[slot],
                device_id={"dp": across},
                device_id_type=MESH_ID,
            )
        )
        slot += 1
    for item in far:
        item.start()
    for item in far:
        item.wait()

    for term, near_buf, far_buf, share in (
        (up_term, up_near, up_far, up_share_ref),
        (down_term, down_near, down_far, down_share_ref),
    ):
        share[...] = (
            rows(term, shard)[...].astype(jnp.float32)
            + near_buf[1].astype(jnp.float32)
            + far_buf[...].astype(jnp.float32)
        )
    lax.fori_loop(1, n, finish, 0)
    lanes = flat.shape[1]
    offset = 0
    for part in (up_first_ref, down_first_ref, up_second_ref, down_second_ref):
        rows, cols = part.shape
        for block in range(cols // lanes):
            part[:, pl.ds(block * lanes, lanes)] = flat[pl.ds(offset, rows), :]
            offset += rows


def scatter_with_gradients(picked, normed, preact, activated, delta, up_full, down_full,
                           kernel_id):
    n = picked.shape[0]
    tokens_n, features = normed.shape
    vmem = pl.BlockSpec(memory_space=pltpu.VMEM)
    moved = picked.size * picked.dtype.itemsize
    flops = 6 * tokens_n * features * up_full.shape[1]
    up_rows = (up_full.shape[0] // 4, up_full.shape[1])
    down_rows = (down_full.shape[0] // 4, down_full.shape[1])
    bf16 = jnp.bfloat16
    return pl.pallas_call(
        functools.partial(scatter_compute_kernel, n),
        out_shape=(
            jax.ShapeDtypeStruct(up_rows, jnp.float32),
            jax.ShapeDtypeStruct(down_rows, jnp.float32),
        ) + tuple(jax.ShapeDtypeStruct(shape, bf16) for shape in (up_rows, down_rows) * 2),
        in_specs=[vmem] * 6,
        out_specs=(vmem,) * 6,
        scratch_shapes=[
            pltpu.VMEM((picked.shape[0] * picked.shape[1], picked.shape[2]), bf16),
            pltpu.VMEM(up_full.shape, bf16),
            pltpu.VMEM(down_full.shape, bf16),
            pltpu.VMEM((2,) + up_rows, bf16),
            pltpu.VMEM((2,) + down_rows, bf16),
            pltpu.VMEM(up_rows, bf16),
            pltpu.VMEM(down_rows, bf16),
            pltpu.VMEM(up_rows, bf16),
            pltpu.VMEM(down_rows, bf16),
            pltpu.SemaphoreType.DMA((n,)),
            pltpu.SemaphoreType.DMA((n,)),
            pltpu.SemaphoreType.DMA((4,)),
            pltpu.SemaphoreType.DMA((4,)),
            pltpu.SemaphoreType.DMA((2,)),
            pltpu.SemaphoreType.DMA((2,)),
        ],
        compiler_params=pltpu.CompilerParams(
            collective_id=kernel_id, has_side_effects=True, vmem_limit_bytes=63 * 1024 * 1024
        ),
        cost_estimate=pl.CostEstimate(flops=flops, transcendentals=0, bytes_accessed=moved * 20),
    )(picked, normed, preact, activated, delta, down_full)


def member_call(body, packed, operands, scratch, kernel_id):
    n, rows, lanes = packed.shape
    moved = packed.size * packed.dtype.itemsize
    smem = [pl.BlockSpec(memory_space=pltpu.SMEM)] * (len(operands) - 1)
    return pl.pallas_call(
        functools.partial(body, n),
        out_shape=jax.ShapeDtypeStruct(packed.shape, packed.dtype),
        in_specs=smem + [pl.BlockSpec(memory_space=pltpu.VMEM)],
        out_specs=pl.BlockSpec(memory_space=pltpu.VMEM),
        scratch_shapes=scratch,
        compiler_params=pltpu.CompilerParams(
            collective_id=kernel_id, has_side_effects=True, vmem_limit_bytes=48 * 1024 * 1024
        ),
        cost_estimate=pl.CostEstimate(flops=0, transcendentals=0, bytes_accessed=moved * 20),
    )(*operands)


def exploit_transfer(packed, source, kernel_id):
    n, rows, lanes = packed.shape
    block = pltpu.VMEM((n, rows, lanes), packed.dtype)
    sems = [pltpu.SemaphoreType.DMA((n,))] * 4
    return member_call(exploit_kernel, packed, (source, packed), [block, block] + sems, kernel_id)


def exploit_gather(parts, shares, source, tokens, labels, classifier, batch_total, members,
                   shards, kernel_id):
    images, patches, features = tokens.shape
    tokens_n = images * patches
    hidden = shares[0].shape[1]
    lanes = 128
    total = sum(part.size for part in parts) // lanes
    shape = (members, total // members, lanes)
    vmem = pl.BlockSpec(memory_space=pltpu.VMEM)
    moved = total * lanes * 2
    fulls = [jax.ShapeDtypeStruct((share.shape[0] * shards, share.shape[1]), share.dtype)
             for share in shares]
    sems = [pltpu.SemaphoreType.DMA((len(shares),))] * 6
    return pl.pallas_call(
        functools.partial(gather_kernel, members, batch_total, patches),
        out_shape=(
            jax.ShapeDtypeStruct(shape, jnp.bfloat16),
            *fulls,
            jax.ShapeDtypeStruct((tokens_n, features), jnp.bfloat16),
            jax.ShapeDtypeStruct((tokens_n, hidden), jnp.float32),
            jax.ShapeDtypeStruct((tokens_n, hidden), jnp.bfloat16),
            jax.ShapeDtypeStruct((tokens_n, features), jnp.bfloat16),
        ),
        in_specs=[pl.BlockSpec(memory_space=pltpu.SMEM)] * 2
        + [vmem] * (len(shares) + 2 + len(parts)),
        out_specs=(vmem,) * 7,
        scratch_shapes=[
            pltpu.VMEM((total, lanes), jnp.bfloat16),
            pltpu.VMEM(shape, jnp.bfloat16),
            pltpu.SemaphoreType.DMA((members,)),
            pltpu.SemaphoreType.DMA((members,)),
        ] + sems,
        compiler_params=pltpu.CompilerParams(
            collective_id=kernel_id, has_side_effects=True, vmem_limit_bytes=63 * 1024 * 1024
        ),
        cost_estimate=pl.CostEstimate(flops=0, transcendentals=0, bytes_accessed=moved * 20),
    )(source, labels, *shares, tokens.reshape(tokens_n, features), classifier, *parts)


def exploit_scatter(packed, kernel_id):
    n = packed.shape[0]
    sems = [pltpu.SemaphoreType.DMA((n,))] * 2
    return member_call(scatter_kernel, packed, (packed,), sems, kernel_id)


def lane_major(part, lanes):
    rows, cols = part.shape
    return part.reshape(rows, cols // lanes, lanes).transpose(1, 0, 2).reshape(-1, lanes)


def from_lane_major(flat, shape, lanes):
    rows, cols = shape
    return flat.reshape(cols // lanes, rows, lanes).transpose(1, 0, 2).reshape(rows, cols)


def exploit_rows(parts, source, members, kernel_id):
    lanes = 128
    rows = [part.size // (members * lanes) for part in parts]
    pad = 0
    pieces = [part.astype(jnp.bfloat16).reshape(members, -1, lanes) for part in parts]
    if pad:
        pieces.append(jnp.zeros((members, pad, lanes), jnp.bfloat16))
    back = exploit_transfer(jnp.concatenate(pieces, axis=1), source, kernel_id)
    out = []
    start = 0
    for part, count in zip(parts, rows):
        out.append(back[:, start:start + count].reshape(part.shape))
        start += count
    return out


def pack_tiles(parts, members):
    lanes = 128
    flat = jnp.concatenate([lane_major(part.astype(jnp.bfloat16), lanes) for part in parts])
    return flat.reshape(members, -1, flat.shape[-1])


def unpack_tiles(back, parts):
    lanes = back.shape[-1]
    back = back.reshape(-1, lanes)
    out = []
    start = 0
    for part in parts:
        count = part.size // lanes
        out.append(from_lane_major(back[start:start + count], part.shape, lanes))
        start += count
    return out


def per_device(
    tokens,
    labels,
    source,
    learn_rate,
    weight_decay,
    classifier,
    up_param,
    up_first,
    up_second,
    down_param,
    down_first,
    down_second,
):
    members = lax.axis_size("member")
    shards = lax.axis_size("dp")
    me = lax.axis_index("member")
    own = source[me] == me

    up_bf, down_bf = exploit_rows((up_param[0], down_param[0]), source, members, 0)
    moments = (up_first[0], down_first[0], up_second[0], down_second[0])
    batch_total = tokens.shape[1] * shards
    picked, up_full, down_full, normed, preact, activated, delta = exploit_gather(
        moments, (up_bf, down_bf), source, tokens[0], labels[0], classifier, batch_total,
        members, shards, 1,
    )
    up_share, down_share, up_mom, down_mom, up_var_bf, down_var_bf = scatter_with_gradients(
        picked, normed, preact, activated, delta, up_full, down_full, 2
    )

    up_now = jnp.where(own, up_param[0], up_bf.astype(jnp.float32))
    down_now = jnp.where(own, down_param[0], down_bf.astype(jnp.float32))
    up_var = jnp.where(own, up_second[0], up_var_bf.astype(jnp.float32))
    down_var = jnp.where(own, down_second[0], down_var_bf.astype(jnp.float32))

    rate_value = learn_rate[0]
    decay_value = weight_decay[0]
    up_new = adamw_step(up_now, up_mom, up_var, up_share, rate_value, decay_value)
    down_new = adamw_step(down_now, down_mom, down_var, down_share, rate_value, decay_value)
    return tuple(value[None] for value in up_new + down_new)


def solution(mesh):
    placed = (
        P("member", "dp", None, None),
        P("member", "dp"),
        P(),
        P("member"),
        P("member"),
        P(),
        P("member", "dp", None),
        P("member", "dp", None),
        P("member", "dp", None),
        P("member", "dp", None),
        P("member", "dp", None),
        P("member", "dp", None),
    )
    return jax.shard_map(
        per_device,
        mesh=mesh,
        in_specs=placed,
        out_specs=(P("member", "dp", None),) * 6,
        check_vma=False,
    )
```

```python
import functools

import jax
import jax.numpy as jnp
from jax import lax
from jax.experimental import pallas as pl
from jax.experimental.pallas import tpu as pltpu
from jax.sharding import PartitionSpec as P

MESH_ID = pl.DeviceIdType.MESH

STEP = 1000


def local_gradients(tokens, labels, up_weight, down_weight, classifier, batch_total):
    images, patches, features = tokens.shape
    hidden_units = up_weight.shape[1]
    token_rows = tokens.reshape(images * patches, features).astype(jnp.float32)
    center = token_rows - jnp.mean(token_rows, axis=1, keepdims=True)
    normed = (center * lax.rsqrt(jnp.mean(center * center, axis=1, keepdims=True) + 1e-06)).astype(
        jnp.bfloat16
    )
    preact = jnp.dot(normed, up_weight, preferred_element_type=jnp.float32) * features ** (-0.5)
    activated = (0.5 * preact * (1.0 + lax.erf(preact * 0.7071067811865476))).astype(jnp.bfloat16)
    residual = token_rows + jnp.dot(
        activated, down_weight, preferred_element_type=jnp.float32
    ) * hidden_units ** (-0.5)
    out_center = residual - jnp.mean(residual, axis=1, keepdims=True)
    inverse = lax.rsqrt(jnp.mean(out_center * out_center, axis=1, keepdims=True) + 1e-06)
    out_normed = out_center * inverse
    pooled = jnp.mean(out_normed.reshape(images, patches, features), axis=1).astype(jnp.bfloat16)
    logits = jnp.dot(pooled, classifier, preferred_element_type=jnp.float32)
    powered = jnp.exp(logits)
    softmax_out = powered / jnp.sum(powered, axis=1, keepdims=True)
    onehot = (labels[:, None] == jnp.arange(classifier.shape[1], dtype=jnp.int32)[None, :]).astype(
        jnp.float32
    )
    logit_delta = ((softmax_out - onehot) / batch_total).astype(jnp.bfloat16)
    pool_delta = (
        lax.dot_general(
            logit_delta, classifier, (((1,), (1,)), ((), ())), preferred_element_type=jnp.float32
        )
        / patches
    )
    token_delta = jnp.broadcast_to(pool_delta[:, None, :], (images, patches, features)).reshape(
        images * patches, features
    )
    residual_delta = inverse * (
        token_delta
        - jnp.mean(token_delta, axis=1, keepdims=True)
        - out_normed * jnp.mean(token_delta * out_normed, axis=1, keepdims=True)
    )
    residual_delta = residual_delta.astype(jnp.bfloat16)
    down_scale = hidden_units ** (-0.5)
    down_gradient = (
        lax.dot_general(
            activated, residual_delta, (((0,), (0,)), ((), ())), preferred_element_type=jnp.float32
        )
        * down_scale
    )
    hidden_delta = (
        lax.dot_general(
            residual_delta,
            down_weight,
            (((1,), (1,)), ((), ())),
            preferred_element_type=jnp.float32,
        )
        * down_scale
    )
    derivative = (
        0.5 * (1.0 + lax.erf(preact * 0.7071067811865476))
        + preact * jnp.exp(-0.5 * preact * preact) * 0.3989422804014327
    )
    preact_delta = (hidden_delta * derivative).astype(jnp.bfloat16)
    up_gradient = lax.dot_general(
        normed, preact_delta, (((0,), (0,)), ((), ())), preferred_element_type=jnp.float32
    ) * features ** (-0.5)
    return (up_gradient, down_gradient)


def adamw_step(param, first, second, gradient, rate_value, decay_value):
    moment = 0.9 * first.astype(jnp.float32) + 0.1 * gradient
    variance = 0.999 * second + 0.001 * gradient * gradient
    update = (
        moment / (1.0 - 0.9**STEP) / (jnp.sqrt(variance / (1.0 - 0.999**STEP)) + 1e-08)
        + decay_value * param
    )
    return (param - rate_value * update, moment.astype(jnp.bfloat16), variance)


def enter(n, me):
    barrier = pltpu.get_barrier_semaphore()

    def greet(k, carry):
        pl.semaphore_signal(
            barrier, inc=1, device_id={"member": lax.rem(me + k, n)}, device_id_type=MESH_ID
        )
        return carry

    lax.fori_loop(1, n, greet, 0)
    pl.semaphore_wait(barrier, n - 1)


def transpose(n, me, src, dst, send_sem, recv_sem):
    def copy(k):
        target = lax.rem(me + k, n)
        return pltpu.make_async_remote_copy(
            src_ref=src.at[target],
            dst_ref=dst.at[me],
            send_sem=send_sem.at[k],
            recv_sem=recv_sem.at[k],
            device_id={"member": target},
            device_id_type=MESH_ID,
        )

    def start(k, carry):
        copy(k).start()
        return carry

    def finish(k, carry):
        copy(k).wait()
        return carry

    lax.fori_loop(1, n, start, 0)
    dst[me] = src[me]
    lax.fori_loop(1, n, finish, 0)


def pick_rows(n, source_ref, held, picked):
    def pick(i, carry):
        picked[i] = held[source_ref[i]]
        return carry

    lax.fori_loop(0, n, pick, 0)


def exploit_kernel(n, source_ref, send_ref, out_ref, held, picked, send1, recv1, send2, recv2):
    me = lax.axis_index("member")
    enter(n, me)
    transpose(n, me, send_ref, held, send1, recv1)
    pick_rows(n, source_ref, held, picked)
    transpose(n, me, picked, out_ref, send2, recv2)


def gather_kernel(n, batch_total, patches, source_ref, labels_ref, up_ref, down_ref, tokens_ref,
                  classifier_ref, *refs):
    parts = refs[:-17]
    (out_ref, up_full, down_full, normed_ref, preact_ref, act_ref, delta_ref,
     flat, held, send1, recv1,
     near_send, near_recv, far_send, far_recv, fwd_send, fwd_recv) = refs[-17:]
    me = lax.axis_index("member")
    shard = lax.axis_index("dp")
    core = shard % 2
    chip = shard // 2
    partner = chip * 2 + (1 - core)
    across = (1 - chip) * 2 + core
    lanes = flat.shape[1]
    chunk = held.shape[1]
    offset = 0
    for part in parts:
        rows, cols = part.shape
        for block in range(cols // lanes):
            flat[pl.ds(offset, rows), :] = part[:, pl.ds(block * lanes, lanes)].astype(flat.dtype)
            offset += rows

    barrier = pltpu.get_barrier_semaphore()

    def greet(k, carry):
        pl.semaphore_signal(
            barrier, inc=1, device_id={"member": lax.rem(me + k, n)}, device_id_type=MESH_ID
        )
        return carry

    lax.fori_loop(1, n, greet, 0)
    for peer in (partner, across):
        pl.semaphore_signal(barrier, inc=1, device_id={"dp": peer}, device_id_type=MESH_ID)
    pl.semaphore_wait(barrier, n - 1 + 2)

    def rows_of(full, index):
        size = full.shape[0] // 4
        return full.at[pl.ds(pl.multiple_of(index * size, size), size)]

    def dp_copy(src, dst, send, recv, slot, peer):
        return pltpu.make_async_remote_copy(
            src_ref=src, dst_ref=dst, send_sem=send.at[slot], recv_sem=recv.at[slot],
            device_id={"dp": peer}, device_id_type=MESH_ID,
        )

    shares = ((up_ref, up_full), (down_ref, down_full))
    far = [dp_copy(share, rows_of(full, shard), far_send, far_recv, slot, across)
           for slot, (share, full) in enumerate(shares)]
    near = [dp_copy(share, rows_of(full, shard), near_send, near_recv, slot, partner)
            for slot, (share, full) in enumerate(shares)]
    for item in far + near:
        item.start()

    def copy(k):
        target = lax.rem(me + k, n)
        return pltpu.make_async_remote_copy(
            src_ref=flat.at[pl.ds(pl.multiple_of(target * chunk, 16), chunk)],
            dst_ref=held.at[me],
            send_sem=send1.at[k],
            recv_sem=recv1.at[k],
            device_id={"member": target},
            device_id_type=MESH_ID,
        )

    def start(k, carry):
        copy(k).start()
        return carry

    def finish(k, carry):
        copy(k).wait()
        return carry

    lax.fori_loop(1, n, start, 0)
    held[me] = flat[pl.ds(pl.multiple_of(me * chunk, 16), chunk)]
    for share, full in shares:
        rows_of(full, shard)[...] = share[...]
    for item in far:
        item.wait()
    forward = [dp_copy(rows_of(full, across), rows_of(full, across), fwd_send, fwd_recv, slot,
                       partner)
               for slot, (share, full) in enumerate(shares)]
    for item in forward:
        item.start()
    for item in near + forward:
        item.wait()
    normed, preact, activated, delta = forward_half(
        tokens_ref[...], labels_ref, up_full[...], down_full[...], classifier_ref[...],
        batch_total, patches,
    )
    normed_ref[...] = normed
    preact_ref[...] = preact
    act_ref[...] = activated
    delta_ref[...] = delta
    lax.fori_loop(1, n, finish, 0)
    pick_rows(n, source_ref, held, out_ref)


def scatter_kernel(n, send_ref, out_ref, send1, recv1):
    me = lax.axis_index("member")
    enter(n, me)
    transpose(n, me, send_ref, out_ref, send1, recv1)


def forward_half(tokens, labels_ref, up_weight, down_weight, classifier, batch_total, patches):
    tokens_n, features = tokens.shape
    hidden_units = up_weight.shape[1]
    classes = classifier.shape[1]
    images = tokens_n // patches
    token_rows = tokens.astype(jnp.float32)
    center = token_rows - jnp.mean(token_rows, axis=1, keepdims=True)
    normed = (center * lax.rsqrt(jnp.mean(center * center, axis=1, keepdims=True) + 1e-06)).astype(
        jnp.bfloat16
    )
    preact = jnp.dot(normed, up_weight, preferred_element_type=jnp.float32) * features ** (-0.5)
    activated = (0.5 * preact * (1.0 + lax.erf(preact * 0.7071067811865476))).astype(jnp.bfloat16)
    residual = token_rows + jnp.dot(
        activated, down_weight, preferred_element_type=jnp.float32
    ) * hidden_units ** (-0.5)
    out_center = residual - jnp.mean(residual, axis=1, keepdims=True)
    inverse = lax.rsqrt(jnp.mean(out_center * out_center, axis=1, keepdims=True) + 1e-06)
    out_normed = out_center * inverse
    image_of_row = lax.broadcasted_iota(jnp.int32, (tokens_n, 1), 0) // patches
    pooled = jnp.concatenate(
        [
            jnp.sum(jnp.where(image_of_row == i, out_normed, 0.0), axis=0, keepdims=True)
            for i in range(images)
        ],
        axis=0,
    ) / patches
    pooled = pooled.astype(jnp.bfloat16)
    logits = jnp.dot(pooled, classifier, preferred_element_type=jnp.float32)
    powered = jnp.exp(logits)
    softmax_out = powered / jnp.sum(powered, axis=1, keepdims=True)
    row = lax.broadcasted_iota(jnp.int32, (images, classes), 0)
    column = lax.broadcasted_iota(jnp.int32, (images, classes), 1)
    label = jnp.zeros((images, classes), jnp.int32)
    for i in range(images):
        label = jnp.where(row == i, labels_ref[i], label)
    onehot = (column == label).astype(jnp.float32)
    logit_delta = ((softmax_out - onehot) / batch_total).astype(jnp.bfloat16)
    pool_delta = (
        lax.dot_general(
            logit_delta, classifier, (((1,), (1,)), ((), ())), preferred_element_type=jnp.float32
        )
        / patches
    )
    token_delta = jnp.zeros((tokens_n, features), jnp.float32)
    for i in range(images):
        token_delta = jnp.where(image_of_row == i, pool_delta[i:i + 1, :], token_delta)
    residual_delta = inverse * (
        token_delta
        - jnp.mean(token_delta, axis=1, keepdims=True)
        - out_normed * jnp.mean(token_delta * out_normed, axis=1, keepdims=True)
    )
    residual_delta = residual_delta.astype(jnp.bfloat16)
    return normed, preact, activated, residual_delta


def backward_half(normed, preact, activated, residual_delta, down_weight):
    features = normed.shape[1]
    hidden_units = preact.shape[1]
    down_scale = hidden_units ** (-0.5)
    down_gradient = (
        lax.dot_general(
            activated, residual_delta, (((0,), (0,)), ((), ())), preferred_element_type=jnp.float32
        )
        * down_scale
    )
    hidden_delta = (
        lax.dot_general(
            residual_delta, down_weight, (((1,), (1,)), ((), ())), preferred_element_type=jnp.float32
        )
        * down_scale
    )
    derivative = (
        0.5 * (1.0 + lax.erf(preact * 0.7071067811865476))
        + preact * jnp.exp(-0.5 * preact * preact) * 0.3989422804014327
    )
    preact_delta = (hidden_delta * derivative).astype(jnp.bfloat16)
    up_gradient = lax.dot_general(
        normed, preact_delta, (((0,), (0,)), ((), ())), preferred_element_type=jnp.float32
    ) * features ** (-0.5)
    return up_gradient, down_gradient


def scatter_compute_kernel(
    n, send_ref, normed_ref, preact_ref, act_ref, delta_ref, down_ref,
    up_share_ref, down_share_ref, up_first_ref, down_first_ref, up_second_ref, down_second_ref,
    flat, up_term, down_term, up_near, down_near, up_part, down_part, up_far, down_far,
    send_sem, recv_sem, near_send, near_recv, far_send, far_recv,
):
    me = lax.axis_index("member")
    shard = lax.axis_index("dp")
    core = shard % 2
    chip = shard // 2
    partner = chip * 2 + (1 - core)
    across = (1 - chip) * 2 + core
    diagonal = (1 - chip) * 2 + (1 - core)

    barrier = pltpu.get_barrier_semaphore()

    def greet(k, carry):
        pl.semaphore_signal(
            barrier, inc=1, device_id={"member": lax.rem(me + k, n)}, device_id_type=MESH_ID
        )
        return carry

    lax.fori_loop(1, n, greet, 0)
    for peer in (partner, across, diagonal):
        pl.semaphore_signal(barrier, inc=1, device_id={"dp": peer}, device_id_type=MESH_ID)
    pl.semaphore_wait(barrier, n - 1 + 3)

    chunk = send_ref.shape[1]

    def copy(j):
        odd = j % 2
        k = odd * (j // 2 + 1) + (1 - odd) * (n - j // 2)
        target = lax.rem(me + k, n)
        return pltpu.make_async_remote_copy(
            src_ref=send_ref.at[target],
            dst_ref=flat.at[pl.ds(pl.multiple_of(me * chunk, 16), chunk)],
            send_sem=send_sem.at[k],
            recv_sem=recv_sem.at[k],
            device_id={"member": target},
            device_id_type=MESH_ID,
        )

    def start(k, carry):
        copy(k).start()
        return carry

    def finish(k, carry):
        copy(k).wait()
        return carry

    lax.fori_loop(1, n, start, 0)
    flat[pl.ds(pl.multiple_of(me * chunk, 16), chunk)] = send_ref[me]
    up_gradient, down_gradient = backward_half(
        normed_ref[...], preact_ref[...], act_ref[...], delta_ref[...], down_ref[...]
    )
    up_term[...] = up_gradient.astype(jnp.bfloat16)
    down_term[...] = down_gradient.astype(jnp.bfloat16)

    def rows(term, index):
        size = term.shape[0] // 4
        return term.at[pl.ds(pl.multiple_of(index * size, size), size)]

    near = []
    slot = 0
    for term, near_buf in ((up_term, up_near), (down_term, down_near)):
        for which, index in ((0, diagonal), (1, partner)):
            near.append(
                pltpu.make_async_remote_copy(
                    src_ref=rows(term, index),
                    dst_ref=near_buf.at[which],
                    send_sem=near_send.at[slot],
                    recv_sem=near_recv.at[slot],
                    device_id={"dp": partner},
                    device_id_type=MESH_ID,
                )
            )
            slot += 1
    for item in near:
        item.start()
    for item in near:
        item.wait()

    far = []
    slot = 0
    for term, near_buf, part, far_buf in (
        (up_term, up_near, up_part, up_far),
        (down_term, down_near, down_part, down_far),
    ):
        part[...] = (
            rows(term, across)[...].astype(jnp.float32) + near_buf[0].astype(jnp.float32)
        ).astype(jnp.bfloat16)
        far.append(
            pltpu.make_async_remote_copy(
                src_ref=part,
                dst_ref=far_buf,
                send_sem=far_send.at[slot],
                recv_sem=far_recv.at[slot],
                device_id={"dp": across},
                device_id_type=MESH_ID,
            )
        )
        slot += 1
    for item in far:
        item.start()
    for item in far:
        item.wait()

    for term, near_buf, far_buf, share in (
        (up_term, up_near, up_far, up_share_ref),
        (down_term, down_near, down_far, down_share_ref),
    ):
        share[...] = (
            rows(term, shard)[...].astype(jnp.float32)
            + near_buf[1].astype(jnp.float32)
            + far_buf[...].astype(jnp.float32)
        )
    lax.fori_loop(1, n, finish, 0)
    lanes = flat.shape[1]
    offset = 0
    for part in (up_first_ref, down_first_ref, up_second_ref, down_second_ref):
        rows, cols = part.shape
        for block in range(cols // lanes):
            part[:, pl.ds(block * lanes, lanes)] = flat[pl.ds(offset, rows), :]
            offset += rows


def scatter_with_gradients(picked, normed, preact, activated, delta, up_full, down_full,
                           kernel_id):
    n = picked.shape[0]
    tokens_n, features = normed.shape
    vmem = pl.BlockSpec(memory_space=pltpu.VMEM)
    moved = picked.size * picked.dtype.itemsize
    flops = 6 * tokens_n * features * up_full.shape[1]
    up_rows = (up_full.shape[0] // 4, up_full.shape[1])
    down_rows = (down_full.shape[0] // 4, down_full.shape[1])
    bf16 = jnp.bfloat16
    return pl.pallas_call(
        functools.partial(scatter_compute_kernel, n),
        out_shape=(
            jax.ShapeDtypeStruct(up_rows, jnp.float32),
            jax.ShapeDtypeStruct(down_rows, jnp.float32),
        ) + tuple(jax.ShapeDtypeStruct(shape, bf16) for shape in (up_rows, down_rows) * 2),
        in_specs=[vmem] * 6,
        out_specs=(vmem,) * 6,
        scratch_shapes=[
            pltpu.VMEM((picked.shape[0] * picked.shape[1], picked.shape[2]), bf16),
            pltpu.VMEM(up_full.shape, bf16),
            pltpu.VMEM(down_full.shape, bf16),
            pltpu.VMEM((2,) + up_rows, bf16),
            pltpu.VMEM((2,) + down_rows, bf16),
            pltpu.VMEM(up_rows, bf16),
            pltpu.VMEM(down_rows, bf16),
            pltpu.VMEM(up_rows, bf16),
            pltpu.VMEM(down_rows, bf16),
            pltpu.SemaphoreType.DMA((n,)),
            pltpu.SemaphoreType.DMA((n,)),
            pltpu.SemaphoreType.DMA((4,)),
            pltpu.SemaphoreType.DMA((4,)),
            pltpu.SemaphoreType.DMA((2,)),
            pltpu.SemaphoreType.DMA((2,)),
        ],
        compiler_params=pltpu.CompilerParams(
            collective_id=kernel_id, has_side_effects=True, vmem_limit_bytes=63 * 1024 * 1024
        ),
        cost_estimate=pl.CostEstimate(flops=flops, transcendentals=0, bytes_accessed=moved * 20),
    )(picked, normed, preact, activated, delta, down_full)


def member_call(body, packed, operands, scratch, kernel_id):
    n, rows, lanes = packed.shape
    moved = packed.size * packed.dtype.itemsize
    smem = [pl.BlockSpec(memory_space=pltpu.SMEM)] * (len(operands) - 1)
    return pl.pallas_call(
        functools.partial(body, n),
        out_shape=jax.ShapeDtypeStruct(packed.shape, packed.dtype),
        in_specs=smem + [pl.BlockSpec(memory_space=pltpu.VMEM)],
        out_specs=pl.BlockSpec(memory_space=pltpu.VMEM),
        scratch_shapes=scratch,
        compiler_params=pltpu.CompilerParams(
            collective_id=kernel_id, has_side_effects=True, vmem_limit_bytes=48 * 1024 * 1024
        ),
        cost_estimate=pl.CostEstimate(flops=0, transcendentals=0, bytes_accessed=moved * 20),
    )(*operands)


def exploit_transfer(packed, source, kernel_id):
    n, rows, lanes = packed.shape
    block = pltpu.VMEM((n, rows, lanes), packed.dtype)
    sems = [pltpu.SemaphoreType.DMA((n,))] * 4
    return member_call(exploit_kernel, packed, (source, packed), [block, block] + sems, kernel_id)


def exploit_gather(parts, shares, source, tokens, labels, classifier, batch_total, members,
                   shards, kernel_id):
    images, patches, features = tokens.shape
    tokens_n = images * patches
    hidden = shares[0].shape[1]
    lanes = 128
    total = sum(part.size for part in parts) // lanes
    shape = (members, total // members, lanes)
    vmem = pl.BlockSpec(memory_space=pltpu.VMEM)
    moved = total * lanes * 2
    fulls = [jax.ShapeDtypeStruct((share.shape[0] * shards, share.shape[1]), share.dtype)
             for share in shares]
    sems = [pltpu.SemaphoreType.DMA((len(shares),))] * 6
    return pl.pallas_call(
        functools.partial(gather_kernel, members, batch_total, patches),
        out_shape=(
            jax.ShapeDtypeStruct(shape, jnp.bfloat16),
            *fulls,
            jax.ShapeDtypeStruct((tokens_n, features), jnp.bfloat16),
            jax.ShapeDtypeStruct((tokens_n, hidden), jnp.float32),
            jax.ShapeDtypeStruct((tokens_n, hidden), jnp.bfloat16),
            jax.ShapeDtypeStruct((tokens_n, features), jnp.bfloat16),
        ),
        in_specs=[pl.BlockSpec(memory_space=pltpu.SMEM)] * 2
        + [vmem] * (len(shares) + 2 + len(parts)),
        out_specs=(vmem,) * 7,
        scratch_shapes=[
            pltpu.VMEM((total, lanes), jnp.bfloat16),
            pltpu.VMEM(shape, jnp.bfloat16),
            pltpu.SemaphoreType.DMA((members,)),
            pltpu.SemaphoreType.DMA((members,)),
        ] + sems,
        compiler_params=pltpu.CompilerParams(
            collective_id=kernel_id, has_side_effects=True, vmem_limit_bytes=63 * 1024 * 1024
        ),
        cost_estimate=pl.CostEstimate(flops=0, transcendentals=0, bytes_accessed=moved * 20),
    )(source, labels, *shares, tokens.reshape(tokens_n, features), classifier, *parts)


def exploit_scatter(packed, kernel_id):
    n = packed.shape[0]
    sems = [pltpu.SemaphoreType.DMA((n,))] * 2
    return member_call(scatter_kernel, packed, (packed,), sems, kernel_id)


def lane_major(part, lanes):
    rows, cols = part.shape
    return part.reshape(rows, cols // lanes, lanes).transpose(1, 0, 2).reshape(-1, lanes)


def from_lane_major(flat, shape, lanes):
    rows, cols = shape
    return flat.reshape(cols // lanes, rows, lanes).transpose(1, 0, 2).reshape(rows, cols)


def exploit_rows(parts, source, members, kernel_id):
    lanes = 128
    rows = [part.size // (members * lanes) for part in parts]
    pad = 0
    pieces = [part.astype(jnp.bfloat16).reshape(members, -1, lanes) for part in parts]
    if pad:
        pieces.append(jnp.zeros((members, pad, lanes), jnp.bfloat16))
    back = exploit_transfer(jnp.concatenate(pieces, axis=1), source, kernel_id)
    out = []
    start = 0
    for part, count in zip(parts, rows):
        out.append(back[:, start:start + count].reshape(part.shape))
        start += count
    return out


def pack_tiles(parts, members):
    lanes = 128
    flat = jnp.concatenate([lane_major(part.astype(jnp.bfloat16), lanes) for part in parts])
    return flat.reshape(members, -1, flat.shape[-1])


def unpack_tiles(back, parts):
    lanes = back.shape[-1]
    back = back.reshape(-1, lanes)
    out = []
    start = 0
    for part in parts:
        count = part.size // lanes
        out.append(from_lane_major(back[start:start + count], part.shape, lanes))
        start += count
    return out


def per_device(
    tokens,
    labels,
    source,
    learn_rate,
    weight_decay,
    classifier,
    up_param,
    up_first,
    up_second,
    down_param,
    down_first,
    down_second,
):
    members = lax.axis_size("member")
    shards = lax.axis_size("dp")
    me = lax.axis_index("member")
    own = source[me] == me

    up_bf, down_bf = exploit_rows((up_param[0], down_param[0]), source, members, 0)
    moments = (up_first[0], down_first[0], up_second[0], down_second[0])
    batch_total = tokens.shape[1] * shards
    picked, up_full, down_full, normed, preact, activated, delta = exploit_gather(
        moments, (up_bf, down_bf), source, tokens[0], labels[0], classifier, batch_total,
        members, shards, 1,
    )
    up_share, down_share, up_mom, down_mom, up_var_bf, down_var_bf = scatter_with_gradients(
        picked, normed, preact, activated, delta, up_full, down_full, 2
    )

    up_now = jnp.where(own, up_param[0], up_bf.astype(jnp.float32))
    down_now = jnp.where(own, down_param[0], down_bf.astype(jnp.float32))
    up_var = jnp.where(own, up_second[0], up_var_bf.astype(jnp.float32))
    down_var = jnp.where(own, down_second[0], down_var_bf.astype(jnp.float32))

    rate_value = learn_rate[0]
    decay_value = weight_decay[0]
    up_new = adamw_step(up_now, up_mom, up_var, up_share, rate_value, decay_value)
    down_new = adamw_step(down_now, down_mom, down_var, down_share, rate_value, decay_value)
    return tuple(value[None] for value in up_new + down_new)


def solution(mesh):
    placed = (
        P("member", "dp", None, None),
        P("member", "dp"),
        P(),
        P("member"),
        P("member"),
        P(),
        P("member", "dp", None),
        P("member", "dp", None),
        P("member", "dp", None),
        P("member", "dp", None),
        P("member", "dp", None),
        P("member", "dp", None),
    )
    return jax.shard_map(
        per_device,
        mesh=mesh,
        in_specs=placed,
        out_specs=(P("member", "dp", None),) * 6,
        check_vma=False,
    )
```
